32 devices in a mesh: path: 2 (over x), trade: 16 (over z, y, core).
Axes of the slice: x: 2, y: 2, z: 4, core: 2. Of those that a mesh axis runs over, the one named last changes fastest.
Arguments:
- factor_paths: bfloat16 [2048, 2, 128], P('trade', None, 'path'), may hold values from -6 to 6
- tenor_basis: bfloat16 [32, 16], replicated, may hold values from -1 to 1
- trade_blocks: int32 [2, 24576], P(None, 'trade'), may hold values from 0 to 63
- trade_set: int32 [24576], P('trade'), may hold values from 0 to 255
- trade_type: int32 [24576], P('trade'), may hold values from 0 to 1
- notional: float32 [24576], P('trade'), may hold values from -3 to 3
- strike: float32 [24576], P('trade'), may hold values from -2 to 2
- vol_level: float32 [24576], P('trade'), may hold values from 0.1 to 0.5
- cash_weights: float32 [16, 24576], P(None, 'trade'), may hold values from 0.02 to 0.12
- set_threshold: float32 [256], P('trade'), may hold values from 0.2 to 2
- date_weight: float32 [256, 2], P('trade'), may hold values from 0.2 to 1
Outputs:
- netting_cva: float32 [256], P('trade')
- factor_cotangent: float32 [2048, 2, 128], P('trade', None, 'path')
The draws below stay inside these ranges and needn't reach their ends.
All inputs are finite; a program needn't handle non-finite values.
Results may differ from the reference program's by a relative error of at most 0.0091.
Values may be sent and summed in bfloat16 or wider, within the bound.
No kernel may reach another device: no remote copies, remote signals or barrier semaphores. Data moves between devices by JAX's collectives and lax.ppermute only.
A program may use at most 64 MiB of HBM per device.

```python
import math
import jax
import jax.numpy as jnp
from jax import lax

F = 2048
BS = 32
M = 16
DATES = 2
NBLK = 64
PATHS = 128
TRADES = 24576
NSETS = 256


def plant(array, rng, smallest, top_value):
    longest = array.shape.index(max(array.shape))
    spots = []
    for shift in (0, 1):
        where = [jax.random.randint(jax.random.fold_in(rng, axis), (), 0, length) for axis, length in enumerate(array.shape)]
        where[longest] = (where[longest] + shift) % array.shape[longest]
        spots.append(tuple(where))
    return array.at[spots[0]].set(smallest).at[spots[1]].set(top_value)


def levels(rng, dims, cuts, low, largest):
    level, own = 1.0, jax.random.fold_in(rng, 6)
    for position, blocks in cuts:
        steps = jnp.exp(jax.random.uniform(jax.random.fold_in(own, position), (blocks,), jnp.float32, low / len(cuts), largest / len(cuts)))
        level = level * jnp.repeat(steps, dims[position] // blocks).reshape([-1 if axis == position else 1 for axis in range(len(dims))])
    return level


def scatter_about(stream_key, dims, scale, bound, split=(), held_as=jnp.bfloat16):
    result = jax.random.normal(stream_key, dims, jnp.float32) * scale
    if len(split) > 0:
        result = levels(stream_key, dims, split, -0.22, 0.18) * result
    return jnp.clip(result, min=-bound, max=bound).astype(held_as)


def setup_inputs(seed: int = 0) -> dict:
    keys = jax.random.split(jax.random.key(seed), 12)
    return {
        "factor_paths": scatter_about(keys[0], (F, DATES, PATHS), 1.0, 6.0, ((0, 16), (2, 2))),
        "tenor_basis": scatter_about(keys[1], (BS, M), BS ** -0.5, 1.0),
        "trade_blocks": plant(jax.random.randint(keys[2], (2, TRADES), 0, NBLK), jax.random.fold_in(keys[2], 1), 0, NBLK - 1).astype(jnp.int32),
        "trade_set": plant(jax.random.randint(keys[3], (TRADES,), 0, NSETS), jax.random.fold_in(keys[3], 1), 0, NSETS - 1).astype(jnp.int32),
        "trade_type": plant(jax.random.randint(keys[4], (TRADES,), 0, 2), jax.random.fold_in(keys[4], 1), 0, 1).astype(jnp.int32),
        "notional": scatter_about(keys[5], (TRADES,), 0.5, 3.0, ((0, 16),), jnp.float32),
        "strike": scatter_about(keys[6], (TRADES,), 0.3, 2.0, ((0, 16),), jnp.float32),
        "vol_level": jnp.clip(jnp.exp(math.log(0.5) - 1.609438 * jax.random.uniform(keys[7], (TRADES,), jnp.float32) ** levels(keys[7], (TRADES,), ((0, 16),), -0.2, 0.2)), 0.1, 0.5),
        "cash_weights": jnp.clip(jnp.exp(math.log(0.12) - 1.7917595 * jax.random.uniform(keys[8], (M, TRADES), jnp.float32) ** levels(keys[8], (M, TRADES), ((1, 16),), -0.2, 0.2)), 0.02, 0.12),
        "set_threshold": jnp.clip(jnp.exp(math.log(2.0) - 2.3025851 * jax.random.uniform(keys[9], (NSETS,), jnp.float32) ** levels(keys[9], (NSETS,), ((0, 16),), -0.2, 0.2)), 0.2, 2.0),
        "date_weight": jnp.clip(jnp.exp(math.log(1.0) - 1.609438 * jax.random.uniform(keys[10], (NSETS, DATES), jnp.float32) ** levels(keys[10], (NSETS, DATES), ((0, 16),), -0.2, 0.2)), 0.2, 1.0),
    }


def price(curves, fwd_block, disc_block, weights, notional, strike, vol_level, trade_kind):
    fwd_curve = jnp.take(curves, fwd_block, axis=0).astype(jnp.float32)
    discount = jnp.exp(-0.5 * jnp.take(curves, disc_block, axis=0).astype(jnp.float32))
    spread = jnp.transpose(weights)[:, :, None]
    forward = jnp.sum(spread * fwd_curve, axis=1)
    annuity = jnp.sum(spread * discount, axis=1)
    moneyness = forward - strike[:, None]
    scaled = moneyness / vol_level[:, None]
    option = trade_kind[:, None] == 1
    payoff = jnp.where(option, vol_level[:, None] * jax.nn.softplus(scaled), moneyness)
    trade_value = notional[:, None] * annuity * payoff
    return trade_value, (discount, spread, annuity, payoff, scaled, option)


def adjoint_terms(saved_state, cotangent, notional):
    discount, spread, annuity, payoff, scaled, option = saved_state
    forward_cot = cotangent * notional[:, None] * annuity * jnp.where(option, jax.nn.sigmoid(scaled), 1.0)
    annuity_cot = cotangent * notional[:, None] * payoff
    from_forward = spread * forward_cot[:, None, :]
    from_discount = -0.5 * spread * discount * annuity_cot[:, None, :]
    return from_forward, from_discount


def reference(factor_paths, tenor_basis, trade_blocks, trade_set, trade_type, notional, strike, vol_level, cash_weights, set_threshold, date_weight):
    row_count = DATES * PATHS
    blocks = factor_paths.reshape(NBLK, BS, row_count).astype(jnp.float32)
    curves = jnp.einsum("jm,bjr->bmr", tenor_basis.astype(jnp.float32), blocks, precision=lax.Precision.HIGHEST).astype(jnp.bfloat16)
    group_size = 128
    group_count = TRADES // group_size
    trade_items = (
        trade_blocks[0].reshape(group_count, group_size),
        trade_blocks[1].reshape(group_count, group_size),
        trade_set.reshape(group_count, group_size),
        trade_type.reshape(group_count, group_size),
        notional.reshape(group_count, group_size),
        strike.reshape(group_count, group_size),
        vol_level.reshape(group_count, group_size),
        jnp.transpose(cash_weights.reshape(M, group_count, group_size), (1, 0, 2)),
    )

    def forward_pass(running, trade_item):
        fwd_block, disc_block, set_ids, trade_kind, notional_part, strike_part, vol_part, weights = trade_item
        trade_value, saved_state = price(curves, fwd_block, disc_block, weights, notional_part, strike_part, vol_part, trade_kind)
        rounded = lax.optimization_barrier(trade_value.astype(jnp.bfloat16)).astype(jnp.float32)
        return running + jax.ops.segment_sum(rounded, set_ids, NSETS), None

    set_value, _ = lax.scan(forward_pass, jnp.zeros((NSETS, row_count), jnp.float32), trade_items)
    excess = set_value - set_threshold[:, None]
    exposure = jax.nn.softplus(excess).reshape(NSETS, DATES, PATHS)
    netting_cva = jnp.sum(date_weight * jnp.mean(exposure, axis=2), axis=1)
    set_cot = (date_weight[:, :, None] * jax.nn.sigmoid(excess).reshape(NSETS, DATES, PATHS)).reshape(NSETS, row_count).astype(jnp.bfloat16)

    def backward_pass(running, trade_item):
        fwd_block, disc_block, set_ids, trade_kind, notional_part, strike_part, vol_part, weights = trade_item
        trade_value, saved_state = price(curves, fwd_block, disc_block, weights, notional_part, strike_part, vol_part, trade_kind)
        cotangent = jnp.take(set_cot, set_ids, axis=0).astype(jnp.float32)
        from_forward, from_discount = adjoint_terms(saved_state, cotangent, notional_part)
        running = running + jax.ops.segment_sum(from_forward, fwd_block, NBLK) + jax.ops.segment_sum(from_discount, disc_block, NBLK)
        return running, None

    curve_cot, _ = lax.scan(backward_pass, jnp.zeros((NBLK, M, row_count), jnp.float32), trade_items)
    factor_cot = jnp.einsum("jm,bmr->bjr", tenor_basis.astype(jnp.float32), curve_cot, precision=lax.Precision.HIGHEST)
    return netting_cva, factor_cot.reshape(F, DATES, PATHS)
```

```python
import functools

import jax
import jax.numpy as jnp
from jax import lax
from jax.experimental import pallas as pl
from jax.experimental.pallas import tpu as pltpu
from jax.sharding import PartitionSpec as P

F32 = jnp.float32
BF16 = jnp.bfloat16
NT = (((1,), (1,)), ((), ()))
TN = (((0,), (0,)), ((), ()))
TILE = 512


def log1p_unit(e):
    return jnp.where(e < 1e-4, (1.0 - 0.5 * e) * e, jnp.log(1.0 + e))


def fill_weighted_onehot(out, ids, weights, blocks):
    tenors = weights.shape[0]
    ids = jnp.broadcast_to(ids, weights.shape)
    zero = jnp.zeros_like(weights)
    for b in range(blocks):
        out[b * tenors : (b + 1) * tenors, :] = jnp.where(ids == b, weights, zero).astype(BF16)


def fill_onehot(out, ids):
    sets, trades = out.shape
    step = 16
    row = lax.broadcasted_iota(jnp.int32, (step, trades), 0)
    ids = jnp.broadcast_to(ids, (step, trades))
    for n in range(0, sets, step):
        out[n : n + step, :] = jnp.where(ids == row + n, 1.0, 0.0).astype(BF16)


def forward_kernel(
    curves, blocks_ref, set_ref, kind_ref, notional_ref, strike_ref, vol_ref, weights_ref,
    sets_out, fwd_scale, ann_scale, w_fwd, w_disc, onehot,
):
    i = pl.program_id(0)
    rows = curves.shape[1]
    tile = weights_ref.shape[1]
    tenors = weights_ref.shape[0]
    blocks = curves.shape[0] // tenors
    weights = weights_ref[...]
    fill_weighted_onehot(w_fwd, blocks_ref[0:1, :], weights, blocks)
    fill_weighted_onehot(w_disc, blocks_ref[1:2, :], weights, blocks)
    fill_onehot(onehot, set_ref[...])
    curve = curves[...]
    discount = jnp.exp(-0.5 * curve.astype(F32)).astype(BF16)
    forward = lax.dot_general(curve, w_fwd[...], TN, preferred_element_type=F32)
    annuity = lax.dot_general(discount, w_disc[...], TN, preferred_element_type=F32)
    vol = vol_ref[...]
    notional = notional_ref[...]
    option = jnp.broadcast_to(kind_ref[...] == 1, (rows, tile))
    moneyness = forward - strike_ref[...]
    scaled = moneyness * (1.0 / vol)
    e = jnp.exp(-jnp.abs(scaled))
    softplus = jnp.maximum(scaled, 0.0) + log1p_unit(e)
    sigmoid = jnp.where(scaled >= 0.0, 1.0, e) / (1.0 + e)
    payoff = jnp.where(option, vol * softplus, moneyness)
    slope = jnp.where(option, sigmoid, 1.0)
    scaled_annuity = notional * annuity
    value = (scaled_annuity * payoff).astype(BF16)
    fwd_scale[...] = scaled_annuity * slope
    ann_scale[...] = notional * payoff
    added = lax.dot_general(onehot[...], value, NT, preferred_element_type=F32)

    @pl.when(i == 0)
    def _():
        sets_out[...] = added

    @pl.when(i > 0)
    def _():
        sets_out[...] += added


def backward_kernel(
    curves, cots, fwd_scale, ann_scale, w_fwd, w_disc, onehot, out, from_fwd, from_disc
):
    i = pl.program_id(0)
    trade_cot = lax.dot_general(cots[...], onehot[...], TN, preferred_element_type=F32)
    fwd_cot = (trade_cot * fwd_scale[...]).astype(BF16)
    ann_cot = (trade_cot * ann_scale[...]).astype(BF16)
    a = lax.dot_general(w_fwd[...], fwd_cot, NT, preferred_element_type=F32)
    b = lax.dot_general(w_disc[...], ann_cot, NT, preferred_element_type=F32)

    @pl.when(i == 0)
    def _():
        from_fwd[...] = a
        from_disc[...] = b

    @pl.when(i > 0)
    def _():
        from_fwd[...] += a
        from_disc[...] += b

    @pl.when(i == pl.num_programs(0) - 1)
    def _():
        discount = jnp.exp(-0.5 * curves[...].astype(F32))
        out[...] = (from_fwd[...] - 0.5 * discount * from_disc[...]).astype(out.dtype)


def whole(shape):
    return pl.BlockSpec(shape, lambda i: (0,) * len(shape))


def column(height, tile):
    return pl.BlockSpec((height, tile), lambda i: (0, i))


def gather_parts(x, axis):
    n = lax.axis_size(axis)
    return lax.all_to_all(jnp.broadcast_to(x[None], (n,) + x.shape), axis, 0, 0)


def scatter_sum(x, axis):
    n = lax.axis_size(axis)
    parts = x.reshape((n, x.shape[0] // n) + x.shape[1:])
    return jnp.sum(lax.all_to_all(parts, axis, 0, 0).astype(F32), axis=0)


def sum_over(x, axis):
    n = lax.axis_size(axis)
    total = x
    for shift in range(1, n):
        total = total + lax.ppermute(x, axis, [(i, (i + shift) % n) for i in range(n)])
    return total


def shards(
    factor_paths, tenor_basis, trade_blocks, trade_set, trade_type, notional, strike,
    vol_level, cash_weights, set_threshold, date_weight,
):
    factor_rows, dates, paths = factor_paths.shape
    block_size, tenors = tenor_basis.shape
    rows = dates * paths
    traders = lax.axis_size("trade")
    blocks = factor_rows * traders // block_size
    local_sets = set_threshold.shape[0]
    sets = local_sets * traders
    trades = trade_set.shape[0]
    tile = TILE if trades % TILE == 0 else trades
    grid = (trades // tile,)

    pieces = factor_paths.reshape(factor_rows // block_size, block_size, rows)
    own_curves = jnp.einsum(
        "jm,bjr->bmr", tenor_basis, pieces, preferred_element_type=F32
    ).astype(BF16)
    curves = gather_parts(own_curves.reshape(-1, rows), "trade").reshape(blocks * tenors, rows)

    params = pltpu.CompilerParams(dimension_semantics=("arbitrary",))
    height = blocks * tenors
    partial, fwd_scale, ann_scale, w_fwd, w_disc, onehot = pl.pallas_call(
        forward_kernel,
        grid=grid,
        in_specs=[whole((height, rows)), column(2, tile)]
        + [column(1, tile)] * 5 + [column(tenors, tile)],
        out_specs=[whole((sets, rows)), column(rows, tile), column(rows, tile),
                   column(height, tile), column(height, tile), column(sets, tile)],
        out_shape=[
            jax.ShapeDtypeStruct((sets, rows), F32),
            jax.ShapeDtypeStruct((rows, trades), F32),
            jax.ShapeDtypeStruct((rows, trades), F32),
            jax.ShapeDtypeStruct((height, trades), BF16),
            jax.ShapeDtypeStruct((height, trades), BF16),
            jax.ShapeDtypeStruct((sets, trades), BF16),
        ],
        compiler_params=params,
        name="price",
    )(
        curves, trade_blocks, trade_set[None], trade_type[None], notional[None],
        strike[None], vol_level[None], cash_weights,
    )

    set_value = scatter_sum(partial, "trade")
    excess = set_value - set_threshold[:, None]
    exposure = jax.nn.softplus(excess).reshape(local_sets, dates, paths)
    path_total = sum_over(jnp.sum(exposure, axis=2), "path")
    netting_cva = jnp.sum(date_weight * path_total, axis=1) / (paths * lax.axis_size("path"))
    set_cot = (jnp.repeat(date_weight, paths, axis=1) * jax.nn.sigmoid(excess)).astype(BF16)
    cots = gather_parts(set_cot, "trade").reshape(sets, rows)

    curve_cot = pl.pallas_call(
        backward_kernel,
        grid=grid,
        in_specs=[whole((height, rows)), whole((sets, rows)), column(rows, tile),
                  column(rows, tile), column(height, tile), column(height, tile),
                  column(sets, tile)],
        out_specs=whole((height, rows)),
        out_shape=jax.ShapeDtypeStruct((height, rows), BF16),
        scratch_shapes=[pltpu.VMEM((height, rows), F32)] * 2,
        compiler_params=params,
        name="adjoint",
    )(curves, cots, fwd_scale, ann_scale, w_fwd, w_disc, onehot)

    own_cot = scatter_sum(curve_cot, "trade").reshape(-1, tenors, rows)
    factor_cot = jnp.einsum(
        "jm,bmr->bjr", tenor_basis.astype(F32), own_cot, precision=lax.Precision.HIGHEST
    )
    return netting_cva, factor_cot.reshape(factor_rows, dates, paths)


def solution(mesh):
    return jax.shard_map(
        shards,
        mesh=mesh,
        in_specs=(
            P("trade", None, "path"), P(), P(None, "trade"), P("trade"), P("trade"),
            P("trade"), P("trade"), P("trade"), P(None, "trade"), P("trade"),
            P("trade", None),
        ),
        out_specs=(P("trade"), P("trade", None, "path")),
        check_vma=False,
    )
```

```python
import functools
import math

import jax
import jax.numpy as jnp
from jax import lax
from jax.experimental import pallas as pl
from jax.experimental.pallas import tpu as pltpu
from jax.sharding import PartitionSpec as P

F32 = jnp.float32
BF16 = jnp.bfloat16
NT = (((1,), (1,)), ((), ()))
TN = (((0,), (0,)), ((), ()))
LANES = 128
TILE = 512
VMEM = pl.BlockSpec(memory_space=pltpu.VMEM)


def log1p_unit(e):
    return jnp.where(e < 1e-4, (1.0 - 0.5 * e) * e, jnp.log(1.0 + e))


def split_bf16(x):
    high = x.astype(BF16)
    return high, (x - high.astype(F32)).astype(BF16)


def iota(shape, dim):
    return lax.broadcasted_iota(jnp.int32, shape, dim)


def block_basis(basis_t, factors, height):
    tenors, size = basis_t.shape
    down = (iota((factors, size), 0) % size == iota((factors, size), 1)).astype(BF16)
    across = (iota((tenors, height), 1) % tenors == iota((tenors, height), 0)).astype(BF16)
    spread = lax.dot_general(down, basis_t, NT, preferred_element_type=F32).astype(BF16)
    tiled = jnp.dot(spread, across, preferred_element_type=F32)
    same = iota((factors, height), 0) // size == iota((factors, height), 1) // tenors
    return jnp.where(same, tiled, 0.0).astype(BF16)


def pair_order(ids, local, devices):
    shift = int(math.log2(local))
    core = lax.rem(lax.axis_index("trade"), 2)
    owner = jnp.right_shift(ids, shift)
    side = jnp.bitwise_xor(jnp.bitwise_and(owner, 1), core)
    place = side * (devices // 2) + jnp.right_shift(owner, 1)
    return place * local + jnp.bitwise_and(ids, local - 1)


def curve_kernel(factors_ref, basis_ref, weight_ref, out):
    copies = out.shape[0]
    rows, factors = factors_ref.shape
    tenors, size = basis_ref.shape
    height = factors // size * tenors
    basis = block_basis(basis_ref[...], factors, height)
    curves = lax.dot_general(
        basis, factors_ref[...], (((0,), (1,)), ((), ())), preferred_element_type=F32
    ).astype(BF16)
    dates, sets = weight_ref.shape
    high, low = split_bf16(weight_ref[...])
    span = rows // dates
    lane = iota((dates, rows), 1)
    owner = (lane // span == iota((dates, rows), 0)).astype(BF16)
    first = (lane % span < span // 2).astype(BF16)
    weights = lax.dot_general(high, owner * first, TN, preferred_element_type=F32)
    weights += lax.dot_general(low, owner * (1.0 - first), TN, preferred_element_type=F32)
    for k in range(copies):
        out[k, :height, :] = curves
        out[k, height:, :] = weights.astype(BF16)


def prep_kernel(devices, blocks_ref, set_ref, weights_ref, w_fwd, w_disc, onehot):
    tenors, trades = weights_ref.shape
    height = w_fwd.shape[0]
    blocks = height // tenors
    sets = onehot.shape[0]
    zero = jnp.zeros((tenors, LANES), F32)
    row = iota((16, LANES), 0)
    set_rows = pair_order(set_ref[...], sets // devices, devices)
    block_rows = pair_order(blocks_ref[...], blocks // devices, devices)
    for t in range(0, trades, LANES):
        lanes = slice(t, t + LANES)
        weights = weights_ref[:, lanes]
        for k, out in enumerate((w_fwd, w_disc)):
            ids = jnp.broadcast_to(block_rows[k : k + 1, lanes], (tenors, LANES))
            for b in range(blocks):
                out[b * tenors : (b + 1) * tenors, lanes] = jnp.where(
                    ids == b, weights, zero
                ).astype(BF16)
        ids = jnp.broadcast_to(set_rows[t // LANES : t // LANES + 1, :], (16, LANES))
        for n in range(0, sets, 16):
            onehot[n : n + 16, lanes] = jnp.where(ids == row + n, 1.0, 0.0).astype(BF16)


def joined_curves(mine, partner, height):
    parts = [ref[k, :height, :] for ref in (mine, partner) for k in range(ref.shape[0])]
    return jnp.concatenate(parts, axis=0)


def param_row(ref, start, tile):
    return jnp.concatenate(
        [ref[j : j + 1, :] for j in range(start // LANES, (start + tile) // LANES)], axis=1
    )


def price_kernel(
    height, mine, partner, w_fwd, w_disc, onehot, kind_ref, notional_ref, strike_ref, vol_ref,
    threshold_ref, keep, send, fwd_scale, ann_scale,
):
    rows = mine.shape[2]
    trades = w_fwd.shape[1]
    half = keep.shape[0]
    tile = TILE if trades % TILE == 0 else trades
    curve = joined_curves(mine, partner, height)
    discount = jnp.exp(-0.5 * curve.astype(F32)).astype(BF16)
    total = jnp.zeros((2 * half, rows), F32)
    for t in range(0, trades, tile):
        lanes = slice(t, t + tile)
        forward = lax.dot_general(curve, w_fwd[:, lanes], TN, preferred_element_type=F32)
        annuity = lax.dot_general(discount, w_disc[:, lanes], TN, preferred_element_type=F32)
        vol = param_row(vol_ref, t, tile)
        notional = param_row(notional_ref, t, tile)
        option = jnp.broadcast_to(param_row(kind_ref, t, tile) == 1, (rows, tile))
        moneyness = forward - param_row(strike_ref, t, tile)
        scaled = moneyness * (1.0 / vol)
        e = jnp.exp(-jnp.abs(scaled))
        softplus = jnp.maximum(scaled, 0.0) + log1p_unit(e)
        sigmoid = jnp.where(scaled >= 0.0, 1.0, e) / (1.0 + e)
        payoff = jnp.where(option, vol * softplus, moneyness)
        slope = jnp.where(option, sigmoid, 1.0)
        scaled_annuity = notional * annuity
        value = (scaled_annuity * payoff).astype(BF16)
        fwd_scale[:, lanes] = scaled_annuity * slope
        ann_scale[:, lanes] = notional * payoff
        total += lax.dot_general(onehot[:, lanes], value, NT, preferred_element_type=F32)
    keep[...] = total[:half]
    send[...] = total[half:].astype(BF16)
    sets = threshold_ref.shape[1]
    chip = lax.axis_index("trade") // 2
    own = pl.ds(pl.multiple_of(chip * sets, sets), sets)
    square = iota((sets, sets), 0) == iota((sets, sets), 1)
    column = jnp.sum(jnp.where(square, threshold_ref[...], 0.0), axis=1, keepdims=True)
    keep[own, :] = keep[own, :] - column


def sets_kernel(height, mine, *refs):
    parts, (cots, own_out, excess_ref) = refs[:-3], refs[-3:]
    chips, padded, rows = mine.shape
    sets = padded - height
    excess = parts[0][...].astype(F32)
    for part in parts[1:]:
        excess += part[...].astype(F32)
    excess_ref[...] = excess
    split = jnp.concatenate([mine[k, height:, :] for k in range(chips)], axis=0).astype(F32)
    quarter = rows // 4
    lane = iota(split.shape, 1)
    other = jnp.where(
        lane % (2 * quarter) < quarter,
        pltpu.roll(split, rows - quarter, 1),
        pltpu.roll(split, quarter, 1),
    )
    e = jnp.exp(-jnp.abs(excess))
    sigmoid = jnp.where(excess >= 0.0, 1.0, e) / (1.0 + e)
    cots[...] = ((split + other) * sigmoid).astype(BF16)
    chip = lax.axis_index("trade") // 2
    own_out[...] = excess_ref[pl.ds(pl.multiple_of(chip * sets, sets), sets), :]


def adjoint_kernel(
    height, mine, partner, cots_mine, cots_partner, fwd_scale, ann_scale, w_fwd, w_disc, onehot,
    keep, send,
):
    half = keep.shape[0]
    rows, trades = fwd_scale.shape
    tile = TILE if trades % TILE == 0 else trades
    cots = jnp.concatenate([cots_mine[...], cots_partner[...]], axis=0)
    from_fwd = jnp.zeros((2 * half, rows), F32)
    from_disc = jnp.zeros((2 * half, rows), F32)
    for t in range(0, trades, tile):
        lanes = slice(t, t + tile)
        trade_cot = lax.dot_general(cots, onehot[:, lanes], TN, preferred_element_type=F32)
        fwd_cot = (trade_cot * fwd_scale[:, lanes]).astype(BF16)
        ann_cot = (trade_cot * ann_scale[:, lanes]).astype(BF16)
        from_fwd += lax.dot_general(w_fwd[:, lanes], fwd_cot, NT, preferred_element_type=F32)
        from_disc += lax.dot_general(w_disc[:, lanes], ann_cot, NT, preferred_element_type=F32)
    discount = jnp.exp(-0.5 * joined_curves(mine, partner, height).astype(F32))
    total = from_fwd - 0.5 * discount * from_disc
    keep[...] = total[:half]
    send[...] = total[half:].astype(BF16)


def factor_kernel(parts, basis_ref, out):
    total = parts[0].astype(F32)
    for k in range(1, parts.shape[0]):
        total += parts[k].astype(F32)
    basis = block_basis(basis_ref[...], out.shape[1], total.shape[0])
    dims = (((0,), (1,)), ((), ()))
    high, low = split_bf16(total)
    out[...] = lax.dot_general(high, basis, dims, preferred_element_type=F32) + lax.dot_general(
        low, basis, dims, preferred_element_type=F32
    )


def call(kernel, name, out_shape, scratch=(), flops=1_000_000, moved=1_000_000):
    def run(*args):
        return pl.pallas_call(
            kernel,
            in_specs=[VMEM] * len(args),
            out_specs=jax.tree.map(lambda _: VMEM, out_shape),
            out_shape=out_shape,
            scratch_shapes=scratch,
            cost_estimate=pl.CostEstimate(flops=flops, bytes_accessed=moved, transcendentals=0),
            compiler_params=pltpu.CompilerParams(vmem_limit_bytes=24 * 2**20),
            name=name,
        )(*args)

    return run


def swap(x, mask):
    n = lax.axis_size("trade")
    return lax.ppermute(x, "trade", [(i, i ^ mask) for i in range(n)])


def chip_exchange(x):
    n = lax.axis_size("trade")
    groups = [[2 * k + core for k in range(n // 2)] for core in range(2)]
    return lax.all_to_all(x, "trade", 0, 0, axis_index_groups=groups)


def sum_over(x, axis):
    n = lax.axis_size(axis)
    total = x
    for shift in range(1, n):
        total = total + lax.ppermute(x, axis, [(i, (i + shift) % n) for i in range(n)])
    return total


def shards(
    factor_paths, tenor_basis, trade_blocks, trade_set, trade_type, notional, strike,
    vol_level, cash_weights, set_threshold, date_weight,
):
    factor_rows, dates, paths = factor_paths.shape
    block_size, tenors = tenor_basis.shape
    rows = dates * paths
    devices = lax.axis_size("trade")
    chips = devices // 2
    local_blocks = factor_rows // block_size
    height = local_blocks * tenors
    local_sets = set_threshold.shape[0]
    half_sets = local_sets * chips
    half_rows = height * chips
    trades = trade_set.shape[0]
    shape = jax.ShapeDtypeStruct

    factors = jnp.transpose(factor_paths, (1, 2, 0)).reshape(rows, factor_rows)
    basis_t = jnp.transpose(tenor_basis)
    payload = call(curve_kernel, "curves", shape((chips, height + local_sets, rows), BF16))(
        factors, basis_t, jnp.transpose(date_weight)
    )
    mine = chip_exchange(payload)
    partner = swap(mine, 1)

    w_fwd, w_disc, onehot = call(
        functools.partial(prep_kernel, devices), "prep",
        [shape((2 * half_rows, trades), BF16)] * 2 + [shape((2 * half_sets, trades), BF16)],
        flops=400_000_000, moved=8_000_000,
    )(trade_blocks, trade_set.reshape(-1, LANES), cash_weights)
    keep, send, fwd_scale, ann_scale = call(
        functools.partial(price_kernel, height), "price",
        [shape((half_sets, rows), F32), shape((half_sets, rows), BF16),
         shape((rows, trades), F32), shape((rows, trades), F32)],
    )(
        mine, partner, w_fwd, w_disc, onehot, trade_type.reshape(-1, LANES),
        notional.reshape(-1, LANES), strike.reshape(-1, LANES), vol_level.reshape(-1, LANES),
        set_threshold[None],
    )

    total = (keep + swap(send, 1).astype(F32)).astype(BF16)
    bits = [1 << k for k in range(1, int(math.log2(devices)))]
    steps = [bits[:1]] if len(bits) % 2 else []
    steps += [bits[k : k + 2] for k in range(len(bits) % 2, len(bits), 2)]
    for step in steps:
        masks = step if len(step) == 1 else [step[0], step[1], step[0] + step[1]]
        parts = [total] + [swap(total, mask) for mask in masks]
        if step is not steps[-1]:
            total = functools.reduce(jnp.add, [p.astype(F32) for p in parts]).astype(BF16)
    cots_mine, excess = call(
        functools.partial(sets_kernel, height), "sets",
        [shape((half_sets, rows), BF16), shape((local_sets, rows), F32)],
        [pltpu.VMEM((half_sets, rows), F32)],
    )(mine, *parts)
    cots_partner = swap(cots_mine, 1)

    keep, send = call(
        functools.partial(adjoint_kernel, height), "adjoint",
        [shape((half_rows, rows), F32), shape((half_rows, rows), BF16)],
    )(mine, partner, cots_mine, cots_partner, fwd_scale, ann_scale, w_fwd, w_disc, onehot)
    pair = (keep + swap(send, 1).astype(F32)).astype(BF16)
    arrived = chip_exchange(pair.reshape(chips, height, rows))
    factor_cot = call(factor_kernel, "factors", shape((rows, factor_rows), F32))(arrived, basis_t)
    factor_cot = jnp.transpose(factor_cot.reshape(dates, paths, factor_rows), (2, 0, 1))

    exposure = jax.nn.softplus(excess).reshape(local_sets, dates, paths)
    weighted = jnp.sum(date_weight * jnp.sum(exposure, axis=2), axis=1)
    netting_cva = sum_over(weighted, "path") / (paths * lax.axis_size("path"))
    return netting_cva, factor_cot


def solution(mesh):
    return jax.shard_map(
        shards,
        mesh=mesh,
        in_specs=(
            P("trade", None, "path"), P(), P(None, "trade"), P("trade"), P("trade"),
            P("trade"), P("trade"), P("trade"), P(None, "trade"), P("trade"),
            P("trade", None),
        ),
        out_specs=(P("trade"), P("trade", None, "path")),
        check_vma=False,
    )
```

```python
import functools
import math

import jax
import jax.numpy as jnp
from jax import lax
from jax.experimental import pallas as pl
from jax.experimental.pallas import tpu as pltpu
from jax.sharding import PartitionSpec as P

F32 = jnp.float32
BF16 = jnp.bfloat16
NT = (((1,), (1,)), ((), ()))
TN = (((0,), (0,)), ((), ()))
LANES = 128
TILE = 512
VMEM = pl.BlockSpec(memory_space=pltpu.VMEM)
HBM = pl.BlockSpec(memory_space=pltpu.HBM)
VMEM_LIMIT = 8 * 2**20


def log1p_unit(e):
    return jnp.where(e < 1e-4, (1.0 - 0.5 * e) * e, jnp.log(1.0 + e))


def split_bf16(x):
    high = x.astype(BF16)
    return high, (x - high.astype(F32)).astype(BF16)


def iota(shape, dim):
    return lax.broadcasted_iota(jnp.int32, shape, dim)


def block_basis(basis_t, factors, height):
    tenors, size = basis_t.shape
    down = (iota((factors, size), 0) % size == iota((factors, size), 1)).astype(BF16)
    across = (iota((tenors, height), 1) % tenors == iota((tenors, height), 0)).astype(BF16)
    spread = lax.dot_general(down, basis_t, NT, preferred_element_type=F32).astype(BF16)
    tiled = jnp.dot(spread, across, preferred_element_type=F32)
    same = iota((factors, height), 0) // size == iota((factors, height), 1) // tenors
    return jnp.where(same, tiled, 0.0).astype(BF16)


def bits_of(n):
    return int(math.log2(n))


def pair_order(ids, local, devices):
    core = lax.rem(lax.axis_index("trade"), 2)
    owner = jnp.right_shift(ids, bits_of(local))
    side = jnp.bitwise_xor(jnp.bitwise_and(owner, 1), core)
    place = side * (devices // 2) + jnp.right_shift(owner, 1)
    return place * local + jnp.bitwise_and(ids, local - 1)


def cube_place(owner, devices):
    distance = jnp.bitwise_xor(owner, lax.axis_index("trade"))
    bits = bits_of(devices)
    place = jnp.zeros_like(distance)
    for k in range(bits):
        bit = jnp.bitwise_and(jnp.right_shift(distance, k), 1)
        place = jnp.bitwise_or(place, jnp.left_shift(bit, bits - 1 - k))
    return place


def cube_order(ids, local, devices):
    place = cube_place(jnp.right_shift(ids, bits_of(local)), devices)
    return place * local + jnp.bitwise_and(ids, local - 1)


def fetch(pairs, sems):
    copies = [pltpu.make_async_copy(src, dst, sems.at[k]) for k, (src, dst) in enumerate(pairs)]
    for copy in copies:
        copy.start()
    for copy in copies:
        copy.wait()


def curve_kernel(
    factors_hbm, basis_hbm, weight_hbm, out, basis_out, weight_ref, factors_ref, basis_ref, sems
):
    fetch(
        [(factors_hbm, factors_ref), (basis_hbm, basis_ref), (weight_hbm, weight_ref)], sems
    )
    rows, factors = factors_ref.shape
    tenors, size = basis_ref.shape
    height = factors // size * tenors
    basis = block_basis(basis_ref[...], factors, height)
    basis_out[...] = basis
    out[:height, :] = lax.dot_general(
        basis, factors_ref[...], (((0,), (1,)), ((), ())), preferred_element_type=F32
    ).astype(BF16)
    dates = weight_ref.shape[0]
    high, low = split_bf16(weight_ref[...])
    span = rows // dates
    lane = iota((dates, rows), 1)
    owner = (lane // span == iota((dates, rows), 0)).astype(BF16)
    first = (lane % span < span // 2).astype(BF16)
    weights = lax.dot_general(high, owner * first, TN, preferred_element_type=F32)
    weights += lax.dot_general(low, owner * (1.0 - first), TN, preferred_element_type=F32)
    out[height:, :] = weights.astype(BF16)


def prep_kernel(devices, *refs):
    sources, rest = refs[:8], refs[8:]
    w_fwd, w_disc, onehot = rest[:3]
    params, (blocks_ref, set_ref, weights_ref, sems) = rest[3:8], rest[8:]
    fetch(list(zip(sources, (blocks_ref, set_ref, weights_ref) + tuple(params))), sems)
    tenors, trades = weights_ref.shape
    height = w_fwd.shape[0]
    blocks = height // tenors
    sets = onehot.shape[0]
    zero = jnp.zeros((tenors, LANES), F32)
    row = iota((16, LANES), 0)
    set_rows = pair_order(set_ref[...], sets // devices, devices)
    block_rows = cube_order(blocks_ref[...], blocks // devices, devices)
    for t in range(0, trades, LANES):
        lanes = slice(t, t + LANES)
        weights = weights_ref[:, lanes]
        for k, out in enumerate((w_fwd, w_disc)):
            ids = jnp.broadcast_to(block_rows[k : k + 1, lanes], (tenors, LANES))
            for b in range(blocks):
                out[b * tenors : (b + 1) * tenors, lanes] = jnp.where(
                    ids == b, weights, zero
                ).astype(BF16)
        ids = jnp.broadcast_to(set_rows[t // LANES : t // LANES + 1, :], (16, LANES))
        for n in range(0, sets, 16):
            onehot[n : n + 16, lanes] = jnp.where(ids == row + n, 1.0, 0.0).astype(BF16)


def joined_curves(ref, height, padded):
    parts = [ref[k : k + height, :] for k in range(0, ref.shape[0], padded)]
    return jnp.concatenate(parts, axis=0)


def param_row(ref, start, tile):
    return jnp.concatenate(
        [ref[j : j + 1, :] for j in range(start // LANES, (start + tile) // LANES)], axis=1
    )


def price_kernel(
    height, padded, gathered, w_fwd, w_disc, onehot, kind_ref, notional_ref, strike_ref, vol_ref,
    threshold_ref, keep, send, fwd_scale, ann_scale,
):
    rows = gathered.shape[1]
    trades = w_fwd.shape[1]
    half = keep.shape[0]
    tile = TILE if trades % TILE == 0 else trades
    curve = joined_curves(gathered, height, padded)
    discount = jnp.exp(-0.5 * curve.astype(F32)).astype(BF16)
    total = jnp.zeros((2 * half, rows), F32)
    for t in range(0, trades, tile):
        lanes = slice(t, t + tile)
        forward = lax.dot_general(curve, w_fwd[:, lanes], TN, preferred_element_type=F32)
        annuity = lax.dot_general(discount, w_disc[:, lanes], TN, preferred_element_type=F32)
        vol = param_row(vol_ref, t, tile)
        notional = param_row(notional_ref, t, tile)
        option = jnp.broadcast_to(param_row(kind_ref, t, tile) == 1, (rows, tile))
        moneyness = forward - param_row(strike_ref, t, tile)
        scaled = moneyness * (1.0 / vol)
        e = jnp.exp(-jnp.abs(scaled))
        softplus = jnp.maximum(scaled, 0.0) + log1p_unit(e)
        sigmoid = jnp.where(scaled >= 0.0, 1.0, e) / (1.0 + e)
        payoff = jnp.where(option, vol * softplus, moneyness)
        slope = jnp.where(option, sigmoid, 1.0)
        scaled_annuity = notional * annuity
        value = (scaled_annuity * payoff).astype(BF16)
        fwd_scale[:, lanes] = scaled_annuity * slope
        ann_scale[:, lanes] = notional * payoff
        total += lax.dot_general(onehot[:, lanes], value, NT, preferred_element_type=F32)
    keep[...] = total[:half]
    send[...] = total[half:].astype(BF16)
    sets = threshold_ref.shape[1]
    chip = lax.axis_index("trade") // 2
    own = pl.ds(pl.multiple_of(chip * sets, sets), sets)
    square = iota((sets, sets), 0) == iota((sets, sets), 1)
    column = jnp.sum(jnp.where(square, threshold_ref[...], 0.0), axis=1, keepdims=True)
    keep[own, :] = keep[own, :] - column


def sets_kernel(height, gathered, weight_ref, *refs):
    parts, (cots, cva, excess_ref) = refs[:-3], refs[-3:]
    dates, sets = weight_ref.shape
    padded = height + sets
    rows = gathered.shape[1]
    devices = gathered.shape[0] // padded
    me = lax.axis_index("trade")
    excess = parts[0][...].astype(F32)
    for part in parts[1:]:
        excess += part[...].astype(F32)
    excess_ref[...] = excess
    chunks = []
    for k in range(devices // 2):
        place = cube_place(2 * k + lax.rem(me, 2), devices)
        start = pl.multiple_of(place * padded + height, math.gcd(padded, height))
        chunks.append(gathered[pl.ds(start, sets), :])
    split = jnp.concatenate(chunks, axis=0).astype(F32)
    span = rows // dates
    lane = iota(split.shape, 1)
    other = jnp.where(
        lane % span < span // 2,
        pltpu.roll(split, rows - span // 2, 1),
        pltpu.roll(split, span // 2, 1),
    )
    e = jnp.exp(-jnp.abs(excess))
    sigmoid = jnp.where(excess >= 0.0, 1.0, e) / (1.0 + e)
    cots[...] = ((split + other) * sigmoid).astype(BF16)
    chip = me // 2
    own = excess_ref[pl.ds(pl.multiple_of(chip * sets, sets), sets), :]
    exposure = jnp.maximum(own, 0.0) + log1p_unit(jnp.exp(-jnp.abs(own)))
    square = iota((sets, sets), 0) == iota((sets, sets), 1)
    date = iota((sets, rows), 1) // span
    total = jnp.zeros((sets, 1), F32)
    for d in range(dates):
        weight = jnp.where(square, weight_ref[d : d + 1, :], 0.0)
        weight = jnp.sum(weight, axis=1, keepdims=True)
        total += weight * jnp.sum(jnp.where(date == d, exposure, 0.0), axis=1, keepdims=True)
    cva[...] = jnp.sum(jnp.where(square, total, 0.0), axis=0, keepdims=True)


def half_cot(height, padded, side, gathered, fwd_cots, ann_cots, w_fwd, w_disc):
    trades = w_fwd.shape[1]
    half = gathered.shape[0] // padded * height // 2
    tile = TILE if trades % TILE == 0 else trades
    band = slice(side * half, (side + 1) * half)
    from_fwd = from_disc = 0.0
    for t in range(0, trades, tile):
        lanes = slice(t, t + tile)
        from_fwd += lax.dot_general(
            w_fwd[band, lanes], fwd_cots[:, lanes], NT, preferred_element_type=F32
        )
        from_disc += lax.dot_general(
            w_disc[band, lanes], ann_cots[:, lanes], NT, preferred_element_type=F32
        )
    curve = joined_curves(gathered, height, padded)[band]
    return from_fwd - 0.5 * jnp.exp(-0.5 * curve.astype(F32)) * from_disc


def adjoint_kernel(
    height, padded, gathered, cots_mine, cots_partner, fwd_scale, ann_scale, w_fwd, w_disc,
    onehot, send, fwd_cots, ann_cots,
):
    trades = fwd_scale.shape[1]
    tile = TILE if trades % TILE == 0 else trades
    cots = jnp.concatenate([cots_mine[...], cots_partner[...]], axis=0)
    for t in range(0, trades, tile):
        lanes = slice(t, t + tile)
        trade_cot = lax.dot_general(cots, onehot[:, lanes], TN, preferred_element_type=F32)
        fwd_cots[:, lanes] = (trade_cot * fwd_scale[:, lanes]).astype(BF16)
        ann_cots[:, lanes] = (trade_cot * ann_scale[:, lanes]).astype(BF16)
    total = half_cot(height, padded, 1, gathered, fwd_cots, ann_cots, w_fwd, w_disc)
    send[...] = total.astype(BF16)


def keep_kernel(height, padded, gathered, fwd_cots, ann_cots, w_fwd, w_disc, keep):
    keep[...] = half_cot(height, padded, 0, gathered, fwd_cots, ann_cots, w_fwd, w_disc)


def fold_kernel(kept, arrived, keep, send):
    half = keep.shape[0]
    keep[...] = kept[:half, :] + arrived[:half, :].astype(F32)
    send[...] = (kept[half:, :] + arrived[half:, :].astype(F32)).astype(BF16)


def factor_kernel(kept, arrived, basis, out):
    total = kept[...] + arrived[...].astype(F32)
    dims = (((0,), (1,)), ((), ()))
    high, low = split_bf16(total)
    out[...] = lax.dot_general(high, basis[...], dims, preferred_element_type=F32)
    out[...] += lax.dot_general(low, basis[...], dims, preferred_element_type=F32)


def call(kernel, name, out_shape, scratch=(), flops=1_000_000, moved=1_000_000, space=VMEM):
    def run(*args):
        return pl.pallas_call(
            kernel,
            in_specs=[space] * len(args),
            out_specs=jax.tree.map(lambda _: VMEM, out_shape),
            out_shape=out_shape,
            scratch_shapes=scratch,
            cost_estimate=pl.CostEstimate(flops=flops, bytes_accessed=moved, transcendentals=0),
            compiler_params=pltpu.CompilerParams(vmem_limit_bytes=VMEM_LIMIT),
            name=name,
        )(*args)

    return run


def swap(x, mask):
    n = lax.axis_size("trade")
    return lax.ppermute(x, "trade", [(i, i ^ mask) for i in range(n)])


def sum_over(x, axis):
    n = lax.axis_size(axis)
    total = x
    for shift in range(1, n):
        total = total + lax.ppermute(x, axis, [(i, (i + shift) % n) for i in range(n)])
    return total


def shards(
    factor_paths, tenor_basis, trade_blocks, trade_set, trade_type, notional, strike,
    vol_level, cash_weights, set_threshold, date_weight,
):
    factor_rows, dates, paths = factor_paths.shape
    block_size, tenors = tenor_basis.shape
    rows = dates * paths
    devices = lax.axis_size("trade")
    local_blocks = factor_rows // block_size
    height = local_blocks * tenors
    local_sets = set_threshold.shape[0]
    padded = height + local_sets
    half_sets = local_sets * devices // 2
    all_rows = height * devices
    trades = trade_set.shape[0]
    shape = jax.ShapeDtypeStruct
    lane_rows = (trades // LANES, LANES)
    dma = pltpu.SemaphoreType.DMA

    factors = jnp.transpose(factor_paths, (1, 2, 0)).reshape(rows, factor_rows)
    gathered, basis, weights = call(
        curve_kernel, "curves",
        [shape((padded, rows), BF16), shape((factor_rows, height), BF16),
         shape((dates, local_sets), F32)],
        [pltpu.VMEM((rows, factor_rows), BF16), pltpu.VMEM((tenors, block_size), BF16), dma((3,))],
        space=HBM,
    )(factors, jnp.transpose(tenor_basis), jnp.transpose(date_weight))
    for k in reversed(range(bits_of(devices))):
        gathered = jnp.concatenate([gathered, swap(gathered, 1 << k)], axis=0)

    w_fwd, w_disc, onehot, *params = call(
        functools.partial(prep_kernel, devices), "prep",
        [shape((all_rows, trades), BF16)] * 2 + [shape((2 * half_sets, trades), BF16)]
        + [shape(lane_rows, jnp.int32)] + [shape(lane_rows, F32)] * 3 + [shape((1, local_sets), F32)],
        [pltpu.VMEM((2, trades), jnp.int32), pltpu.VMEM(lane_rows, jnp.int32),
         pltpu.VMEM((tenors, trades), F32), dma((8,))],
        flops=400_000_000, moved=8_000_000, space=HBM,
    )(
        trade_blocks, trade_set.reshape(lane_rows), cash_weights, trade_type.reshape(lane_rows),
        notional.reshape(lane_rows), strike.reshape(lane_rows), vol_level.reshape(lane_rows),
        set_threshold[None],
    )
    keep, send, fwd_scale, ann_scale = call(
        functools.partial(price_kernel, height, padded), "price",
        [shape((half_sets, rows), F32), shape((half_sets, rows), BF16),
         shape((rows, trades), F32), shape((rows, trades), F32)],
    )(gathered, w_fwd, w_disc, onehot, *params)

    total = (keep + swap(send, 1).astype(F32)).astype(BF16)
    bits = [1 << k for k in range(1, bits_of(devices))]
    steps = [bits[:1]] if len(bits) % 2 else []
    steps += [bits[k : k + 2] for k in range(len(bits) % 2, len(bits), 2)]
    for step in steps:
        masks = step if len(step) == 1 else [step[0], step[1], step[0] + step[1]]
        parts = [total] + [swap(total, mask) for mask in masks]
        if step is not steps[-1]:
            total = functools.reduce(jnp.add, [p.astype(F32) for p in parts]).astype(BF16)
    cots_mine, cva = call(
        functools.partial(sets_kernel, height), "sets",
        [shape((half_sets, rows), BF16), shape((1, local_sets), F32)],
        [pltpu.VMEM((half_sets, rows), F32)],
    )(gathered, weights, *parts)
    cots_partner = swap(cots_mine, 1)

    send, fwd_cots, ann_cots = call(
        functools.partial(adjoint_kernel, height, padded), "adjoint",
        [shape((all_rows // 2, rows), BF16)] + [shape((rows, trades), BF16)] * 2,
    )(gathered, cots_mine, cots_partner, fwd_scale, ann_scale, w_fwd, w_disc, onehot)
    keep = call(
        functools.partial(keep_kernel, height, padded), "keep", shape((all_rows // 2, rows), F32),
        flops=200_000_000, moved=4_000_000,
    )(gathered, fwd_cots, ann_cots, w_fwd, w_disc)
    arrived = swap(send, 1)
    for k in range(1, bits_of(devices)):
        size = all_rows >> (k + 1)
        keep, send = call(
            fold_kernel, f"fold{k}", [shape((size, rows), F32), shape((size, rows), BF16)]
        )(keep, arrived)
        arrived = swap(send, 1 << k)
    factor_cot = call(factor_kernel, "factors", shape((rows, factor_rows), F32))(
        keep, arrived, basis
    )
    factor_cot = jnp.transpose(factor_cot.reshape(dates, paths, factor_rows), (2, 0, 1))
    netting_cva = sum_over(cva[0], "path") / (paths * lax.axis_size("path"))
    return netting_cva, factor_cot


def solution(mesh):
    return jax.shard_map(
        shards,
        mesh=mesh,
        in_specs=(
            P("trade", None, "path"), P(), P(None, "trade"), P("trade"), P("trade"),
            P("trade"), P("trade"), P("trade"), P(None, "trade"), P("trade"),
            P("trade", None),
        ),
        out_specs=(P("trade"), P("trade", None, "path")),
        check_vma=False,
    )
```

```python
import functools
import math

import jax
import jax.numpy as jnp
from jax import lax
from jax.experimental import pallas as pl
from jax.experimental.pallas import tpu as pltpu
from jax.sharding import PartitionSpec as P

F32 = jnp.float32
BF16 = jnp.bfloat16
NT = (((1,), (1,)), ((), ()))
TN = (((0,), (0,)), ((), ()))
LANES = 128
TILE = 512
VMEM = pl.BlockSpec(memory_space=pltpu.VMEM)
HBM = pl.BlockSpec(memory_space=pltpu.HBM)
VMEM_LIMIT = 8 * 2**20


def log1p_unit(e):
    return jnp.where(e < 1e-4, (1.0 - 0.5 * e) * e, jnp.log(1.0 + e))


def split_bf16(x):
    high = x.astype(BF16)
    return high, (x - high.astype(F32)).astype(BF16)


def iota(shape, dim):
    return lax.broadcasted_iota(jnp.int32, shape, dim)


def block_basis(basis_t, factors, height):
    tenors, size = basis_t.shape
    down = (iota((factors, size), 0) % size == iota((factors, size), 1)).astype(BF16)
    across = (iota((tenors, height), 1) % tenors == iota((tenors, height), 0)).astype(BF16)
    spread = lax.dot_general(down, basis_t, NT, preferred_element_type=F32).astype(BF16)
    tiled = jnp.dot(spread, across, preferred_element_type=F32)
    same = iota((factors, height), 0) // size == iota((factors, height), 1) // tenors
    return jnp.where(same, tiled, 0.0).astype(BF16)


def bits_of(n):
    return int(math.log2(n))


def pair_order(ids, local, devices):
    core = lax.rem(lax.axis_index("trade"), 2)
    owner = jnp.right_shift(ids, bits_of(local))
    side = jnp.bitwise_xor(jnp.bitwise_and(owner, 1), core)
    place = side * (devices // 2) + jnp.right_shift(owner, 1)
    return place * local + jnp.bitwise_and(ids, local - 1)


def cube_place(owner, devices):
    distance = jnp.bitwise_xor(owner, lax.axis_index("trade"))
    bits = bits_of(devices)
    place = jnp.zeros_like(distance)
    for k in range(bits):
        bit = jnp.bitwise_and(jnp.right_shift(distance, k), 1)
        place = jnp.bitwise_or(place, jnp.left_shift(bit, bits - 1 - k))
    return place


def cube_order(ids, local, devices):
    place = cube_place(jnp.right_shift(ids, bits_of(local)), devices)
    return place * local + jnp.bitwise_and(ids, local - 1)


def fetch(pairs, sems):
    copies = [pltpu.make_async_copy(src, dst, sems.at[k]) for k, (src, dst) in enumerate(pairs)]
    for copy in copies:
        copy.start()
    for copy in copies:
        copy.wait()


def curve_kernel(
    factors_hbm, basis_hbm, weight_hbm, out, basis_out, weight_ref, factors_ref, basis_ref, sems
):
    fetch(
        [(factors_hbm, factors_ref), (basis_hbm, basis_ref), (weight_hbm, weight_ref)], sems
    )
    rows, factors = factors_ref.shape
    tenors, size = basis_ref.shape
    height = factors // size * tenors
    basis = block_basis(basis_ref[...], factors, height)
    basis_out[...] = basis
    out[:height, :] = lax.dot_general(
        basis, factors_ref[...], (((0,), (1,)), ((), ())), preferred_element_type=F32
    ).astype(BF16)
    dates = weight_ref.shape[0]
    high, low = split_bf16(weight_ref[...])
    span = rows // dates
    lane = iota((dates, rows), 1)
    owner = (lane // span == iota((dates, rows), 0)).astype(BF16)
    first = (lane % span < span // 2).astype(BF16)
    weights = lax.dot_general(high, owner * first, TN, preferred_element_type=F32)
    weights += lax.dot_general(low, owner * (1.0 - first), TN, preferred_element_type=F32)
    out[height:, :] = weights.astype(BF16)


def prep_kernel(devices, *refs):
    sources, rest = refs[:8], refs[8:]
    w_fwd, w_disc, onehot = rest[:3]
    params, (blocks_ref, set_ref, weights_ref, sems) = rest[3:8], rest[8:]
    fetch(list(zip(sources, (blocks_ref, set_ref, weights_ref) + tuple(params))), sems)
    tenors, trades = weights_ref.shape
    height = w_fwd.shape[0]
    blocks = height // tenors
    sets = onehot.shape[0]
    zero = jnp.zeros((tenors, LANES), F32)
    row = iota((16, LANES), 0)
    set_rows = pair_order(set_ref[...], sets // devices, devices)
    block_rows = cube_order(blocks_ref[...], blocks // devices, devices)
    for t in range(0, trades, LANES):
        lanes = slice(t, t + LANES)
        weights = weights_ref[:, lanes]
        for k, out in enumerate((w_fwd, w_disc)):
            ids = jnp.broadcast_to(block_rows[k : k + 1, lanes], (tenors, LANES))
            for b in range(blocks):
                out[b * tenors : (b + 1) * tenors, lanes] = jnp.where(
                    ids == b, weights, zero
                ).astype(BF16)
        ids = jnp.broadcast_to(set_rows[t // LANES : t // LANES + 1, :], (16, LANES))
        for n in range(0, sets, 16):
            onehot[n : n + 16, lanes] = jnp.where(ids == row + n, 1.0, 0.0).astype(BF16)


def joined_curves(ref, height, padded):
    parts = [ref[k : k + height, :] for k in range(0, ref.shape[0], padded)]
    return jnp.concatenate(parts, axis=0)


def param_row(ref, start, tile):
    return jnp.concatenate(
        [ref[j : j + 1, :] for j in range(start // LANES, (start + tile) // LANES)], axis=1
    )


def price_kernel(
    height, padded, gathered, w_fwd, w_disc, onehot, kind_ref, notional_ref, strike_ref, vol_ref,
    threshold_ref, keep, send, fwd_scale, ann_scale,
):
    rows = gathered.shape[1]
    trades = w_fwd.shape[1]
    half = keep.shape[0]
    tile = TILE if trades % TILE == 0 else trades
    curve = joined_curves(gathered, height, padded)
    discount = jnp.exp(-0.5 * curve.astype(F32)).astype(BF16)
    total = jnp.zeros((2 * half, rows), F32)
    for t in range(0, trades, tile):
        lanes = slice(t, t + tile)
        forward = lax.dot_general(curve, w_fwd[:, lanes], TN, preferred_element_type=F32)
        annuity = lax.dot_general(discount, w_disc[:, lanes], TN, preferred_element_type=F32)
        vol = param_row(vol_ref, t, tile)
        notional = param_row(notional_ref, t, tile)
        option = jnp.broadcast_to(param_row(kind_ref, t, tile) == 1, (rows, tile))
        moneyness = forward - param_row(strike_ref, t, tile)
        scaled = moneyness * (1.0 / vol)
        e = jnp.exp(-jnp.abs(scaled))
        softplus = jnp.maximum(scaled, 0.0) + log1p_unit(e)
        sigmoid = jnp.where(scaled >= 0.0, 1.0, e) / (1.0 + e)
        payoff = jnp.where(option, vol * softplus, moneyness)
        slope = jnp.where(option, sigmoid, 1.0)
        scaled_annuity = notional * annuity
        value = (scaled_annuity * payoff).astype(BF16)
        fwd_scale[:, lanes] = scaled_annuity * slope
        ann_scale[:, lanes] = notional * payoff
        total += lax.dot_general(onehot[:, lanes], value, NT, preferred_element_type=F32)
    keep[...] = total[:half]
    send[...] = total[half:].astype(BF16)
    sets = threshold_ref.shape[1]
    chip = lax.axis_index("trade") // 2
    own = pl.ds(pl.multiple_of(chip * sets, sets), sets)
    square = iota((sets, sets), 0) == iota((sets, sets), 1)
    column = jnp.sum(jnp.where(square, threshold_ref[...], 0.0), axis=1, keepdims=True)
    keep[own, :] = keep[own, :] - column


def sets_kernel(height, gathered, weight_ref, *refs):
    parts, (cots, cva, excess_ref) = refs[:-3], refs[-3:]
    dates, sets = weight_ref.shape
    padded = height + sets
    rows = gathered.shape[1]
    devices = gathered.shape[0] // padded
    me = lax.axis_index("trade")
    excess = parts[0][...].astype(F32)
    for part in parts[1:]:
        excess += part[...].astype(F32)
    excess_ref[...] = excess
    chunks = []
    for k in range(devices // 2):
        place = cube_place(2 * k + lax.rem(me, 2), devices)
        start = pl.multiple_of(place * padded + height, math.gcd(padded, height))
        chunks.append(gathered[pl.ds(start, sets), :])
    split = jnp.concatenate(chunks, axis=0).astype(F32)
    span = rows // dates
    lane = iota(split.shape, 1)
    other = jnp.where(
        lane % span < span // 2,
        pltpu.roll(split, rows - span // 2, 1),
        pltpu.roll(split, span // 2, 1),
    )
    e = jnp.exp(-jnp.abs(excess))
    sigmoid = jnp.where(excess >= 0.0, 1.0, e) / (1.0 + e)
    cots[...] = ((split + other) * sigmoid).astype(BF16)
    chip = me // 2
    own = excess_ref[pl.ds(pl.multiple_of(chip * sets, sets), sets), :]
    exposure = jnp.maximum(own, 0.0) + log1p_unit(jnp.exp(-jnp.abs(own)))
    square = iota((sets, sets), 0) == iota((sets, sets), 1)
    date = iota((sets, rows), 1) // span
    total = jnp.zeros((sets, 1), F32)
    for d in range(dates):
        weight = jnp.where(square, weight_ref[d : d + 1, :], 0.0)
        weight = jnp.sum(weight, axis=1, keepdims=True)
        total += weight * jnp.sum(jnp.where(date == d, exposure, 0.0), axis=1, keepdims=True)
    cva[...] = jnp.sum(jnp.where(square, total, 0.0), axis=0, keepdims=True)


def half_cot(height, padded, side, gathered, fwd_cots, ann_cots, w_fwd, w_disc):
    trades = w_fwd.shape[1]
    half = gathered.shape[0] // padded * height // 2
    tile = TILE if trades % TILE == 0 else trades
    band = slice(side * half, (side + 1) * half)
    from_fwd = from_disc = 0.0
    for t in range(0, trades, tile):
        lanes = slice(t, t + tile)
        from_fwd += lax.dot_general(
            w_fwd[band, lanes], fwd_cots[:, lanes], NT, preferred_element_type=F32
        )
        from_disc += lax.dot_general(
            w_disc[band, lanes], ann_cots[:, lanes], NT, preferred_element_type=F32
        )
    curve = joined_curves(gathered, height, padded)[band]
    return from_fwd - 0.5 * jnp.exp(-0.5 * curve.astype(F32)) * from_disc


def adjoint_kernel(
    height, padded, gathered, cots_mine, cots_partner, fwd_scale, ann_scale, w_fwd, w_disc,
    onehot, send, fwd_cots, ann_cots,
):
    trades = fwd_scale.shape[1]
    tile = TILE if trades % TILE == 0 else trades
    cots = jnp.concatenate([cots_mine[...], cots_partner[...]], axis=0)
    for t in range(0, trades, tile):
        lanes = slice(t, t + tile)
        trade_cot = lax.dot_general(cots, onehot[:, lanes], TN, preferred_element_type=F32)
        fwd_cots[:, lanes] = (trade_cot * fwd_scale[:, lanes]).astype(BF16)
        ann_cots[:, lanes] = (trade_cot * ann_scale[:, lanes]).astype(BF16)
    total = half_cot(height, padded, 1, gathered, fwd_cots, ann_cots, w_fwd, w_disc)
    send[...] = total.astype(BF16)


def keep_kernel(height, padded, gathered, fwd_cots, ann_cots, w_fwd, w_disc, keep):
    keep[...] = half_cot(height, padded, 0, gathered, fwd_cots, ann_cots, w_fwd, w_disc)


def fold_kernel(kept, arrived, keep, send):
    half = keep.shape[0]
    keep[...] = kept[:half, :] + arrived[:half, :].astype(F32)
    send[...] = (kept[half:, :] + arrived[half:, :].astype(F32)).astype(BF16)


def factor_kernel(kept, arrived, basis, out):
    total = kept[...] + arrived[...].astype(F32)
    dims = (((0,), (1,)), ((), ()))
    high, low = split_bf16(total)
    out[...] = lax.dot_general(high, basis[...], dims, preferred_element_type=F32)
    out[...] += lax.dot_general(low, basis[...], dims, preferred_element_type=F32)


def call(
    kernel, name, out_shape, scratch=(), flops=1_000_000, moved=1_000_000, space=VMEM,
    limit=VMEM_LIMIT,
):
    def run(*args):
        if space is HBM:
            args = [pltpu.with_memory_space_constraint(x, pltpu.HBM) for x in args]
        return pl.pallas_call(
            kernel,
            in_specs=[space] * len(args),
            out_specs=jax.tree.map(lambda _: VMEM, out_shape),
            out_shape=out_shape,
            scratch_shapes=scratch,
            cost_estimate=pl.CostEstimate(flops=flops, bytes_accessed=moved, transcendentals=0),
            compiler_params=pltpu.CompilerParams(vmem_limit_bytes=limit),
            name=name,
        )(*args)

    return run


def swap(x, mask):
    n = lax.axis_size("trade")
    return lax.ppermute(x, "trade", [(i, i ^ mask) for i in range(n)])


def sum_over(x, axis):
    n = lax.axis_size(axis)
    total = x
    for shift in range(1, n):
        total = total + lax.ppermute(x, axis, [(i, (i + shift) % n) for i in range(n)])
    return total


def shards(
    factor_paths, tenor_basis, trade_blocks, trade_set, trade_type, notional, strike,
    vol_level, cash_weights, set_threshold, date_weight,
):
    factor_rows, dates, paths = factor_paths.shape
    block_size, tenors = tenor_basis.shape
    rows = dates * paths
    devices = lax.axis_size("trade")
    local_blocks = factor_rows // block_size
    height = local_blocks * tenors
    local_sets = set_threshold.shape[0]
    padded = height + local_sets
    half_sets = local_sets * devices // 2
    all_rows = height * devices
    trades = trade_set.shape[0]
    shape = jax.ShapeDtypeStruct
    lane_rows = (trades // LANES, LANES)
    dma = pltpu.SemaphoreType.DMA

    factors = jnp.transpose(factor_paths, (1, 2, 0)).reshape(rows, factor_rows)
    gathered, basis, weights = call(
        curve_kernel, "curves",
        [shape((padded, rows), BF16), shape((factor_rows, height), BF16),
         shape((dates, local_sets), F32)],
        [pltpu.VMEM((rows, factor_rows), BF16), pltpu.VMEM((tenors, block_size), BF16), dma((3,))],
        space=HBM,
    )(factors, jnp.transpose(tenor_basis), jnp.transpose(date_weight))
    for k in reversed(range(bits_of(devices))):
        gathered = jnp.concatenate([gathered, swap(gathered, 1 << k)], axis=0)

    w_fwd, w_disc, onehot, *params = call(
        functools.partial(prep_kernel, devices), "prep",
        [shape((all_rows, trades), BF16)] * 2 + [shape((2 * half_sets, trades), BF16)]
        + [shape(lane_rows, jnp.int32)] + [shape(lane_rows, F32)] * 3 + [shape((1, local_sets), F32)],
        [pltpu.VMEM((2, trades), jnp.int32), pltpu.VMEM(lane_rows, jnp.int32),
         pltpu.VMEM((tenors, trades), F32), dma((8,))],
        flops=400_000_000, moved=8_000_000, space=HBM,
    )(
        trade_blocks, trade_set.reshape(lane_rows), cash_weights, trade_type.reshape(lane_rows),
        notional.reshape(lane_rows), strike.reshape(lane_rows), vol_level.reshape(lane_rows),
        set_threshold[None],
    )
    keep, send, fwd_scale, ann_scale = call(
        functools.partial(price_kernel, height, padded), "price",
        [shape((half_sets, rows), F32), shape((half_sets, rows), BF16),
         shape((rows, trades), F32), shape((rows, trades), F32)],
    )(gathered, w_fwd, w_disc, onehot, *params)

    total = (keep + swap(send, 1).astype(F32)).astype(BF16)
    bits = [1 << k for k in range(1, bits_of(devices))]
    steps = [bits[:1]] if len(bits) % 2 else []
    steps += [bits[k : k + 2] for k in range(len(bits) % 2, len(bits), 2)]
    for step in steps:
        masks = step if len(step) == 1 else [step[0], step[1], step[0] + step[1]]
        parts = [total] + [swap(total, mask) for mask in masks]
        if step is not steps[-1]:
            total = functools.reduce(jnp.add, [p.astype(F32) for p in parts]).astype(BF16)
    cots_mine, cva = call(
        functools.partial(sets_kernel, height), "sets",
        [shape((half_sets, rows), BF16), shape((1, local_sets), F32)],
        [pltpu.VMEM((half_sets, rows), F32)],
    )(gathered, weights, *parts)
    cots_partner = swap(cots_mine, 1)

    send, fwd_cots, ann_cots = call(
        functools.partial(adjoint_kernel, height, padded), "adjoint",
        [shape((all_rows // 2, rows), BF16)] + [shape((rows, trades), BF16)] * 2,
    )(gathered, cots_mine, cots_partner, fwd_scale, ann_scale, w_fwd, w_disc, onehot)
    keep = call(
        functools.partial(keep_kernel, height, padded), "keep", shape((all_rows // 2, rows), F32),
        flops=200_000_000, moved=4_000_000,
    )(gathered, fwd_cots, ann_cots, w_fwd, w_disc)
    arrived = swap(send, 1)
    for k in range(1, bits_of(devices)):
        size = all_rows >> (k + 1)
        keep, send = call(
            fold_kernel, f"fold{k}", [shape((size, rows), F32), shape((size, rows), BF16)]
        )(keep, arrived)
        arrived = swap(send, 1 << k)
    factor_cot = call(factor_kernel, "factors", shape((rows, factor_rows), F32))(
        keep, arrived, basis
    )
    factor_cot = jnp.transpose(factor_cot.reshape(dates, paths, factor_rows), (2, 0, 1))
    netting_cva = sum_over(cva[0], "path") / (paths * lax.axis_size("path"))
    return netting_cva, factor_cot


def solution(mesh):
    return jax.shard_map(
        shards,
        mesh=mesh,
        in_specs=(
            P("trade", None, "path"), P(), P(None, "trade"), P("trade"), P("trade"),
            P("trade"), P("trade"), P("trade"), P(None, "trade"), P("trade"),
            P("trade", None),
        ),
        out_specs=(P("trade"), P("trade", None, "path")),
        check_vma=False,
    )
```

```python
import functools
import math

import jax
import jax.numpy as jnp
from jax import lax
from jax.experimental import pallas as pl
from jax.experimental.pallas import tpu as pltpu
from jax.sharding import PartitionSpec as P

F32 = jnp.float32
BF16 = jnp.bfloat16
NT = (((1,), (1,)), ((), ()))
TN = (((0,), (0,)), ((), ()))
LANES = 128
TILE = 512
VMEM = pl.BlockSpec(memory_space=pltpu.VMEM)
HBM = pl.BlockSpec(memory_space=pltpu.HBM)
VMEM_LIMIT = 8 * 2**20


def log1p_unit(e):
    return jnp.where(e < 1e-4, (1.0 - 0.5 * e) * e, jnp.log(1.0 + e))


def split_bf16(x):
    high = x.astype(BF16)
    return high, (x - high.astype(F32)).astype(BF16)


def iota(shape, dim):
    return lax.broadcasted_iota(jnp.int32, shape, dim)


def block_basis(basis_t, factors, height):
    tenors, size = basis_t.shape
    down = (iota((factors, size), 0) % size == iota((factors, size), 1)).astype(BF16)
    across = (iota((tenors, height), 1) % tenors == iota((tenors, height), 0)).astype(BF16)
    spread = lax.dot_general(down, basis_t, NT, preferred_element_type=F32).astype(BF16)
    tiled = jnp.dot(spread, across, preferred_element_type=F32)
    same = iota((factors, height), 0) // size == iota((factors, height), 1) // tenors
    return jnp.where(same, tiled, 0.0).astype(BF16)


def bits_of(n):
    return int(math.log2(n))


def pair_order(ids, local, devices):
    core = lax.rem(lax.axis_index("trade"), 2)
    owner = jnp.right_shift(ids, bits_of(local))
    side = jnp.bitwise_xor(jnp.bitwise_and(owner, 1), core)
    place = side * (devices // 2) + jnp.right_shift(owner, 1)
    return place * local + jnp.bitwise_and(ids, local - 1)


def steps_of(devices):
    bits = [1 << k for k in range(1, bits_of(devices))]
    return bits[2:][::-1], bits[:2]


def cube_place(owner, devices):
    distance = jnp.bitwise_xor(owner, lax.axis_index("trade"))
    single, group = steps_of(devices)
    place = jnp.zeros_like(distance)
    for k, mask in enumerate(single + group + [1]):
        bit = jnp.bitwise_and(jnp.right_shift(distance, bits_of(mask)), 1)
        place = jnp.bitwise_or(place, jnp.left_shift(bit, k))
    return place


def cube_order(ids, local, devices):
    place = cube_place(jnp.right_shift(ids, bits_of(local)), devices)
    return place * local + jnp.bitwise_and(ids, local - 1)


def fetch(pairs, sems):
    copies = [pltpu.make_async_copy(src, dst, sems.at[k]) for k, (src, dst) in enumerate(pairs)]
    for copy in copies:
        copy.start()
    for copy in copies:
        copy.wait()


def curves_of(basis, factors):
    dims = (((0,), (1,)), ((), ()))
    return lax.dot_general(basis, factors, dims, preferred_element_type=F32).astype(BF16)


def curve_kernel(
    factors_hbm, basis_hbm, weight_hbm, out, basis_out, weight_ref, extra, factors_ref,
    basis_ref, sems,
):
    fetch(
        [(factors_hbm, factors_ref), (basis_hbm, basis_ref), (weight_hbm, weight_ref)], sems
    )
    factors = factors_ref.shape[1]
    tenors, size = basis_ref.shape
    basis = block_basis(basis_ref[...], factors, factors // size * tenors)
    basis_out[...] = basis
    out[...] = curves_of(basis, factors_ref[...])
    dates, sets = weight_ref.shape
    rows, lanes = extra.shape
    first = lax.axis_index("trade") // 2 * sets
    spot = (iota((sets, lanes), 1) == iota((sets, lanes), 0) + lax.rem(first, lanes)).astype(BF16)
    total = jnp.zeros((rows, lanes), F32)
    for k, part in enumerate(split_bf16(weight_ref[...])):
        top = (first // lanes * 2 + k) * dates
        lift = (iota((rows, dates), 0) == iota((rows, dates), 1) + top).astype(BF16)
        lifted = jnp.dot(lift, part, preferred_element_type=F32).astype(BF16)
        total += jnp.dot(lifted, spot, preferred_element_type=F32)
    extra[...] = total.astype(BF16)


def next_curve_kernel(own, arrived, basis, out):
    height = own.shape[0]
    out[:height, :] = own[...]
    out[height:, :] = curves_of(basis[...], arrived[...])


def join_kernel(*refs):
    *parts, _, out = refs
    height = parts[0].shape[0]
    for k, part in enumerate(parts):
        out[k * height : (k + 1) * height, :] = part[...]


def prep_kernel(devices, *refs):
    sources, rest = refs[:8], refs[9:]
    w_fwd, w_disc, onehot = rest[:3]
    params, (blocks_ref, set_ref, weights_ref, sems) = rest[3:8], rest[8:]
    fetch(list(zip(sources, (blocks_ref, set_ref, weights_ref) + tuple(params))), sems)
    tenors, trades = weights_ref.shape
    height = w_fwd.shape[0]
    blocks = height // tenors
    sets = onehot.shape[0]
    zero = jnp.zeros((tenors, LANES), F32)
    row = iota((16, LANES), 0)
    set_rows = pair_order(set_ref[...], sets // devices, devices)
    block_rows = cube_order(blocks_ref[...], blocks // devices, devices)
    for t in range(0, trades, LANES):
        lanes = slice(t, t + LANES)
        weights = weights_ref[:, lanes]
        for k, out in enumerate((w_fwd, w_disc)):
            ids = jnp.broadcast_to(block_rows[k : k + 1, lanes], (tenors, LANES))
            for b in range(blocks):
                out[b * tenors : (b + 1) * tenors, lanes] = jnp.where(
                    ids == b, weights, zero
                ).astype(BF16)
        ids = jnp.broadcast_to(set_rows[t // LANES : t // LANES + 1, :], (16, LANES))
        for n in range(0, sets, 16):
            onehot[n : n + 16, lanes] = jnp.where(ids == row + n, 1.0, 0.0).astype(BF16)


def param_row(ref, start, tile):
    return jnp.concatenate(
        [ref[j : j + 1, :] for j in range(start // LANES, (start + tile) // LANES)], axis=1
    )


def half_price_kernel(curves, w_fwd, w_disc, forward, annuity):
    half, trades = curves.shape[0], w_fwd.shape[1]
    tile = TILE if trades % TILE == 0 else trades
    curve = curves[...]
    discount = jnp.exp(-0.5 * curve.astype(F32)).astype(BF16)
    for t in range(0, trades, tile):
        lanes = slice(t, t + tile)
        forward[:, lanes] = lax.dot_general(
            curve, w_fwd[:half, lanes], TN, preferred_element_type=F32
        )
        annuity[:, lanes] = lax.dot_general(
            discount, w_disc[:half, lanes], TN, preferred_element_type=F32
        )


def price_kernel(
    curves, forward_ref, annuity_ref, w_fwd, w_disc, onehot, kind_ref, notional_ref, strike_ref,
    vol_ref, threshold_ref, keep, send, fwd_scale, ann_scale,
):
    near, rows = curves.shape
    trades = w_fwd.shape[1]
    half = keep.shape[0]
    tile = TILE if trades % TILE == 0 else trades
    curve = curves[...]
    discount = jnp.exp(-0.5 * curve.astype(F32)).astype(BF16)
    total = jnp.zeros((2 * half, rows), F32)
    for t in range(0, trades, tile):
        lanes = slice(t, t + tile)
        forward = forward_ref[:, lanes] + lax.dot_general(
            curve, w_fwd[near:, lanes], TN, preferred_element_type=F32
        )
        annuity = annuity_ref[:, lanes] + lax.dot_general(
            discount, w_disc[near:, lanes], TN, preferred_element_type=F32
        )
        vol = param_row(vol_ref, t, tile)
        notional = param_row(notional_ref, t, tile)
        option = jnp.broadcast_to(param_row(kind_ref, t, tile) == 1, (rows, tile))
        moneyness = forward - param_row(strike_ref, t, tile)
        scaled = moneyness * (1.0 / vol)
        e = jnp.exp(-jnp.abs(scaled))
        softplus = jnp.maximum(scaled, 0.0) + log1p_unit(e)
        sigmoid = jnp.where(scaled >= 0.0, 1.0, e) / (1.0 + e)
        payoff = jnp.where(option, vol * softplus, moneyness)
        slope = jnp.where(option, sigmoid, 1.0)
        scaled_annuity = notional * annuity
        value = (scaled_annuity * payoff).astype(BF16)
        fwd_scale[:, lanes] = scaled_annuity * slope
        ann_scale[:, lanes] = notional * payoff
        total += lax.dot_general(onehot[:, lanes], value, NT, preferred_element_type=F32)
    keep[...] = total[:half]
    send[...] = total[half:].astype(BF16)
    sets = threshold_ref.shape[1]
    chip = lax.axis_index("trade") // 2
    own = pl.ds(pl.multiple_of(chip * sets, sets), sets)
    square = iota((sets, sets), 0) == iota((sets, sets), 1)
    column = jnp.sum(jnp.where(square, threshold_ref[...], 0.0), axis=1, keepdims=True)
    keep[own, :] = keep[own, :] - column


def pair_kernel(keep, arrived, extra, out):
    half = keep.shape[0]
    out[:half, :] = (keep[...] + arrived[...].astype(F32)).astype(BF16)
    out[half:, :] = extra[...]


def sets_kernel(weight_ref, *refs):
    parts, (cots, cva, excess_ref) = refs[:-3], refs[-3:]
    dates, sets = weight_ref.shape
    half, rows = excess_ref.shape
    me = lax.axis_index("trade")
    total = parts[0][...].astype(F32)
    for part in parts[1:]:
        total += part[...].astype(F32)
    excess = total[:half]
    excess_ref[...] = excess
    span = rows // dates
    pieces = total[half:].astype(BF16)
    line = iota((pieces.shape[0], rows), 0)
    weights = []
    for k in range(max(1, half // rows)):
        spread = (line % dates == iota(line.shape, 1) // span) & (line // (2 * dates) == k)
        weights.append(
            lax.dot_general(pieces, spread.astype(BF16), TN, preferred_element_type=F32)
        )
    weights = jnp.concatenate(weights, axis=0)[:half]
    e = jnp.exp(-jnp.abs(excess))
    sigmoid = jnp.where(excess >= 0.0, 1.0, e) / (1.0 + e)
    cots[...] = (weights * sigmoid).astype(BF16)
    chip = me // 2
    own = excess_ref[pl.ds(pl.multiple_of(chip * sets, sets), sets), :]
    exposure = jnp.maximum(own, 0.0) + log1p_unit(jnp.exp(-jnp.abs(own)))
    square = iota((sets, sets), 0) == iota((sets, sets), 1)
    date = iota((sets, rows), 1) // span
    column = jnp.zeros((sets, 1), F32)
    for d in range(dates):
        weight = jnp.where(square, weight_ref[d : d + 1, :], 0.0)
        weight = jnp.sum(weight, axis=1, keepdims=True)
        column += weight * jnp.sum(jnp.where(date == d, exposure, 0.0), axis=1, keepdims=True)
    cva[...] = jnp.sum(jnp.where(square, column, 0.0), axis=0, keepdims=True)


def half_cot(side, curves, fwd_cots, ann_cots, w_fwd, w_disc):
    half, trades = curves.shape[0], w_fwd.shape[1]
    tile = TILE if trades % TILE == 0 else trades
    band = slice(side * half, (side + 1) * half)
    from_fwd = from_disc = 0.0
    for t in range(0, trades, tile):
        lanes = slice(t, t + tile)
        from_fwd += lax.dot_general(
            w_fwd[band, lanes], fwd_cots[:, lanes], NT, preferred_element_type=F32
        )
        from_disc += lax.dot_general(
            w_disc[band, lanes], ann_cots[:, lanes], NT, preferred_element_type=F32
        )
    return from_fwd - 0.5 * jnp.exp(-0.5 * curves[...].astype(F32)) * from_disc


def adjoint_kernel(
    partner, cots_mine, cots_partner, fwd_scale, ann_scale, w_fwd, w_disc, onehot, send,
    fwd_cots, ann_cots,
):
    trades = fwd_scale.shape[1]
    tile = TILE if trades % TILE == 0 else trades
    cots = jnp.concatenate([cots_mine[...], cots_partner[...]], axis=0)
    for t in range(0, trades, tile):
        lanes = slice(t, t + tile)
        trade_cot = lax.dot_general(cots, onehot[:, lanes], TN, preferred_element_type=F32)
        fwd_cots[:, lanes] = (trade_cot * fwd_scale[:, lanes]).astype(BF16)
        ann_cots[:, lanes] = (trade_cot * ann_scale[:, lanes]).astype(BF16)
    send[...] = half_cot(1, partner, fwd_cots, ann_cots, w_fwd, w_disc).astype(BF16)


def keep_kernel(mine, fwd_cots, ann_cots, w_fwd, w_disc, keep):
    keep[...] = half_cot(0, mine, fwd_cots, ann_cots, w_fwd, w_disc)


def fold_kernel(count, kept, *refs):
    arrived, (keep, *sends) = refs[:count], refs[count:]
    total = kept[...]
    for part in arrived:
        total += part[...].astype(F32)
    size = keep.shape[0]
    keep[...] = total[:size]
    for k, send in enumerate(sends):
        send[...] = total[(k + 1) * size : (k + 2) * size].astype(BF16)


def factor_kernel(kept, arrived, basis, out):
    total = kept[...] + arrived[...].astype(F32)
    dims = (((0,), (1,)), ((), ()))
    high, low = split_bf16(total)
    out[...] = lax.dot_general(high, basis[...], dims, preferred_element_type=F32)
    out[...] += lax.dot_general(low, basis[...], dims, preferred_element_type=F32)


def call(
    kernel, name, out_shape, scratch=(), flops=1_000_000, moved=1_000_000, space=VMEM, last=None
):
    def run(*args):
        spaces = [space] * len(args)
        if last is not None:
            spaces[-1] = last
        args = [
            pltpu.with_memory_space_constraint(x, pltpu.HBM) if where is HBM else x
            for x, where in zip(args, spaces)
        ]
        return pl.pallas_call(
            kernel,
            in_specs=spaces,
            out_specs=jax.tree.map(lambda _: VMEM, out_shape),
            out_shape=out_shape,
            scratch_shapes=scratch,
            cost_estimate=pl.CostEstimate(flops=flops, bytes_accessed=moved, transcendentals=0),
            compiler_params=pltpu.CompilerParams(vmem_limit_bytes=VMEM_LIMIT),
            name=name,
        )(*args)

    return run


def swap(x, mask):
    n = lax.axis_size("trade")
    return lax.ppermute(x, "trade", [(i, i ^ mask) for i in range(n)])


def swaps(x, step):
    masks = [sum(b for k, b in enumerate(step) if j >> k & 1) for j in range(1, 2 ** len(step))]
    parts = {}
    for j in sorted(range(len(masks)), key=lambda j: -bin(masks[j]).count("1")):
        parts[j] = swap(x[j] if isinstance(x, (list, tuple)) else x, masks[j])
    return [parts[j] for j in range(len(masks))]


def sum_over(x, axis):
    n = lax.axis_size(axis)
    total = x
    for shift in range(1, n):
        total = total + lax.ppermute(x, axis, [(i, (i + shift) % n) for i in range(n)])
    return total


def shards(
    factor_paths, tenor_basis, trade_blocks, trade_set, trade_type, notional, strike,
    vol_level, cash_weights, set_threshold, date_weight,
):
    factor_rows, dates, paths = factor_paths.shape
    block_size, tenors = tenor_basis.shape
    rows = dates * paths
    devices = lax.axis_size("trade")
    local_blocks = factor_rows // block_size
    height = local_blocks * tenors
    local_sets = set_threshold.shape[0]
    half_sets = local_sets * devices // 2
    all_rows = height * devices
    trades = trade_set.shape[0]
    shape = jax.ShapeDtypeStruct
    extra_rows = -(-max(1, half_sets // rows) * 2 * dates // 16) * 16
    lane_rows = (trades // LANES, LANES)
    dma = pltpu.SemaphoreType.DMA

    factors = jnp.transpose(factor_paths, (1, 2, 0)).reshape(rows, factor_rows)
    single, group = steps_of(devices)
    arrived = swap(factors, single[0])
    curves, basis, weights, extra = call(
        curve_kernel, "curves",
        [shape((height, rows), BF16), shape((factor_rows, height), BF16),
         shape((dates, local_sets), F32), shape((extra_rows, rows), BF16)],
        [pltpu.VMEM((rows, factor_rows), BF16), pltpu.VMEM((tenors, block_size), BF16), dma((3,))],
        space=HBM,
    )(factors, jnp.transpose(tenor_basis), jnp.transpose(date_weight))
    curves = call(next_curve_kernel, "curves2", shape((2 * height, rows), BF16))(
        curves, arrived, basis
    )
    for mask in single[1:]:
        curves = jnp.concatenate([curves, swap(curves, mask)], axis=0)
    near = [curves] + swaps(curves, group)
    w_fwd, w_disc, onehot, *params = call(
        functools.partial(prep_kernel, devices), "prep",
        [shape((all_rows, trades), BF16)] * 2 + [shape((2 * half_sets, trades), BF16)]
        + [shape(lane_rows, jnp.int32)] + [shape(lane_rows, F32)] * 3 + [shape((1, local_sets), F32)],
        [pltpu.VMEM((2, trades), jnp.int32), pltpu.VMEM(lane_rows, jnp.int32),
         pltpu.VMEM((tenors, trades), F32), dma((8,))],
        flops=400_000_000, moved=8_000_000, space=HBM,
        last=VMEM,
    )(
        trade_blocks, trade_set.reshape(lane_rows), cash_weights, trade_type.reshape(lane_rows),
        notional.reshape(lane_rows), strike.reshape(lane_rows), vol_level.reshape(lane_rows),
        set_threshold[None], curves,
    )
    mine = call(join_kernel, "join", shape((all_rows // 2, rows), BF16))(*near, params[-1])
    partner = swap(mine, 1)
    forward, annuity = call(
        half_price_kernel, "price1", [shape((rows, trades), F32)] * 2,
        flops=400_000_000, moved=4_000_000,
    )(mine, w_fwd, w_disc)
    keep, send, fwd_scale, ann_scale = call(
        price_kernel, "price2",
        [shape((half_sets, rows), F32), shape((half_sets, rows), BF16),
         shape((rows, trades), F32), shape((rows, trades), F32)],
    )(partner, forward, annuity, w_fwd, w_disc, onehot, *params)

    total = call(pair_kernel, "pair", shape((half_sets + extra_rows, rows), BF16))(
        keep, swap(send, 1), extra
    )
    bits = [1 << k for k in range(1, bits_of(devices))]
    steps = [bits[:1]] if len(bits) % 2 else []
    steps += [bits[k : k + 2] for k in range(len(bits) % 2, len(bits), 2)]
    for step in steps:
        parts = [total] + swaps(total, step)
        if step is not steps[-1]:
            total = functools.reduce(jnp.add, [p.astype(F32) for p in parts]).astype(BF16)
    cots_mine, cva = call(
        sets_kernel, "sets",
        [shape((half_sets, rows), BF16), shape((1, local_sets), F32)],
        [pltpu.VMEM((half_sets, rows), F32)],
    )(weights, *parts)
    cots_partner = swap(cots_mine, 1)

    send, fwd_cots, ann_cots = call(
        adjoint_kernel, "adjoint",
        [shape((all_rows // 2, rows), BF16)] + [shape((rows, trades), BF16)] * 2,
    )(partner, cots_mine, cots_partner, fwd_scale, ann_scale, w_fwd, w_disc, onehot)
    keep = call(
        keep_kernel, "keep", shape((all_rows // 2, rows), F32),
        flops=200_000_000, moved=4_000_000,
    )(mine, fwd_cots, ann_cots, w_fwd, w_disc)
    arrived = [swap(send, 1)]
    size = all_rows // 2
    for step in [group] + [[mask] for mask in single[::-1]]:
        size >>= len(step)
        shapes = [shape((size, rows), F32)]
        shapes += [shape((size, rows), BF16)] * (2 ** len(step) - 1)
        keep, *sends = call(
            functools.partial(fold_kernel, len(arrived)), f"fold{step[0]}", shapes
        )(keep, *arrived)
        arrived = swaps(sends, step)
    factor_cot = call(factor_kernel, "factors", shape((rows, factor_rows), F32))(
        keep, *arrived, basis
    )
    factor_cot = jnp.transpose(factor_cot.reshape(dates, paths, factor_rows), (2, 0, 1))
    netting_cva = sum_over(cva[0], "path") / (paths * lax.axis_size("path"))
    return netting_cva, factor_cot


def solution(mesh):
    return jax.shard_map(
        shards,
        mesh=mesh,
        in_specs=(
            P("trade", None, "path"), P(), P(None, "trade"), P("trade"), P("trade"),
            P("trade"), P("trade"), P("trade"), P(None, "trade"), P("trade"),
            P("trade", None),
        ),
        out_specs=(P("trade"), P("trade", None, "path")),
        check_vma=False,
    )
```

```python
import functools
import math

import jax
import jax.numpy as jnp
from jax import lax
from jax.experimental import pallas as pl
from jax.experimental.pallas import tpu as pltpu
from jax.sharding import PartitionSpec as P

F32 = jnp.float32
BF16 = jnp.bfloat16
NT = (((1,), (1,)), ((), ()))
TN = (((0,), (0,)), ((), ()))
LANES = 128
TILE = 768
VMEM = pl.BlockSpec(memory_space=pltpu.VMEM)
HBM = pl.BlockSpec(memory_space=pltpu.HBM)
VMEM_LIMIT = 8 * 2**20


def log1p_unit(e):
    return jnp.where(e < 1e-4, (1.0 - 0.5 * e) * e, jnp.log(1.0 + e))


def split_bf16(x):
    high = x.astype(BF16)
    return high, (x - high.astype(F32)).astype(BF16)


def iota(shape, dim):
    return lax.broadcasted_iota(jnp.int32, shape, dim)


def block_basis(basis_t, factors, height):
    tenors, size = basis_t.shape
    down = (iota((factors, size), 0) % size == iota((factors, size), 1)).astype(BF16)
    across = (iota((tenors, height), 1) % tenors == iota((tenors, height), 0)).astype(BF16)
    spread = lax.dot_general(down, basis_t, NT, preferred_element_type=F32).astype(BF16)
    tiled = jnp.dot(spread, across, preferred_element_type=F32)
    same = iota((factors, height), 0) // size == iota((factors, height), 1) // tenors
    return jnp.where(same, tiled, 0.0).astype(BF16)


def bits_of(n):
    return int(math.log2(n))


def pair_order(ids, local, devices):
    core = lax.rem(lax.axis_index("trade"), 2)
    owner = jnp.right_shift(ids, bits_of(local))
    side = jnp.bitwise_xor(jnp.bitwise_and(owner, 1), core)
    place = side * (devices // 2) + jnp.right_shift(owner, 1)
    return place * local + jnp.bitwise_and(ids, local - 1)


def steps_of(devices):
    bits = [1 << k for k in range(1, bits_of(devices))]
    return bits[2:][::-1], bits[:2]


def cube_place(owner, devices):
    distance = jnp.bitwise_xor(owner, lax.axis_index("trade"))
    single, group = steps_of(devices)
    place = jnp.zeros_like(distance)
    for k, mask in enumerate(single + group + [1]):
        bit = jnp.bitwise_and(jnp.right_shift(distance, bits_of(mask)), 1)
        place = jnp.bitwise_or(place, jnp.left_shift(bit, k))
    return place


def cube_order(ids, local, devices):
    place = cube_place(jnp.right_shift(ids, bits_of(local)), devices)
    return place * local + jnp.bitwise_and(ids, local - 1)


def fetch(pairs, sems):
    copies = [pltpu.make_async_copy(src, dst, sems.at[k]) for k, (src, dst) in enumerate(pairs)]
    for copy in copies:
        copy.start()
    for copy in copies:
        copy.wait()


def curves_of(basis, factors):
    dims = (((0,), (1,)), ((), ()))
    return lax.dot_general(basis, factors, dims, preferred_element_type=F32).astype(BF16)


def curve_kernel(
    factors_hbm, basis_hbm, weight_hbm, out, basis_out, weight_ref, extra, factors_ref,
    basis_ref, sems,
):
    fetch(
        [(factors_hbm, factors_ref), (basis_hbm, basis_ref), (weight_hbm, weight_ref)], sems
    )
    factors = factors_ref.shape[1]
    tenors, size = basis_ref.shape
    basis = block_basis(basis_ref[...], factors, factors // size * tenors)
    basis_out[...] = basis
    out[...] = curves_of(basis, factors_ref[...])
    dates, sets = weight_ref.shape
    rows, lanes = extra.shape
    first = lax.axis_index("trade") // 2 * sets
    spot = (iota((sets, lanes), 1) == iota((sets, lanes), 0) + lax.rem(first, lanes)).astype(BF16)
    total = jnp.zeros((rows, lanes), F32)
    for k, part in enumerate(split_bf16(weight_ref[...])):
        top = (first // lanes * 2 + k) * dates
        lift = (iota((rows, dates), 0) == iota((rows, dates), 1) + top).astype(BF16)
        lifted = jnp.dot(lift, part, preferred_element_type=F32).astype(BF16)
        total += jnp.dot(lifted, spot, preferred_element_type=F32)
    extra[...] = total.astype(BF16)


def next_curve_kernel(own, arrived, basis, out):
    height = own.shape[0]
    out[:height, :] = own[...]
    out[height:, :] = curves_of(basis[...], arrived[...])


def join_kernel(*refs):
    *parts, _, out = refs
    height = parts[0].shape[0]
    for k, part in enumerate(parts):
        out[k * height : (k + 1) * height, :] = part[...]


def prep_kernel(devices, *refs):
    sources, rest = refs[:8], refs[9:]
    w_fwd, w_disc, onehot = rest[:3]
    params, (blocks_ref, set_ref, weights_ref, sems) = rest[3:8], rest[8:]
    fetch(list(zip(sources, (blocks_ref, set_ref, weights_ref) + tuple(params))), sems)
    tenors, trades = weights_ref.shape
    height = w_fwd.shape[0]
    blocks = height // tenors
    sets = onehot.shape[0]
    zero = jnp.zeros((tenors, LANES), F32)
    row = iota((16, LANES), 0)
    set_rows = pair_order(set_ref[...], sets // devices, devices)
    block_rows = cube_order(blocks_ref[...], blocks // devices, devices)
    for t in range(0, trades, LANES):
        lanes = slice(t, t + LANES)
        weights = weights_ref[:, lanes]
        for k, out in enumerate((w_fwd, w_disc)):
            ids = jnp.broadcast_to(block_rows[k : k + 1, lanes], (tenors, LANES))
            for b in range(blocks):
                out[b * tenors : (b + 1) * tenors, lanes] = jnp.where(
                    ids == b, weights, zero
                ).astype(BF16)
        ids = jnp.broadcast_to(set_rows[t // LANES : t // LANES + 1, :], (16, LANES))
        for n in range(0, sets, 16):
            onehot[n : n + 16, lanes] = jnp.where(ids == row + n, 1.0, 0.0).astype(BF16)


def param_row(ref, start, tile):
    return jnp.concatenate(
        [ref[j : j + 1, :] for j in range(start // LANES, (start + tile) // LANES)], axis=1
    )


def half_price_kernel(curves, w_fwd, w_disc, forward, annuity):
    half, trades = curves.shape[0], w_fwd.shape[1]
    tile = TILE if trades % TILE == 0 else trades
    curve = curves[...]
    discount = jnp.exp(-0.5 * curve.astype(F32)).astype(BF16)
    for t in range(0, trades, tile):
        lanes = slice(t, t + tile)
        forward[:, lanes] = lax.dot_general(
            curve, w_fwd[:half, lanes], TN, preferred_element_type=F32
        )
        annuity[:, lanes] = lax.dot_general(
            discount, w_disc[:half, lanes], TN, preferred_element_type=F32
        )


def option_terms(forward, strike, vol):
    moneyness = forward - strike
    return moneyness, jnp.exp(jnp.abs(moneyness) * (-1.0 / vol))


def swaption_payoff(moneyness, e, vol):
    return jnp.maximum(moneyness, 0.0) + vol * log1p_unit(e)


def price_kernel(
    curves, forward_ref, annuity_ref, w_fwd, w_disc, onehot, kind_ref, notional_ref, strike_ref,
    vol_ref, threshold_ref, keep, send, forward_out, annuity_out,
):
    near, rows = curves.shape
    trades = w_fwd.shape[1]
    half = keep.shape[0]
    tile = TILE if trades % TILE == 0 else trades
    curve = curves[...]
    discount = jnp.exp(-0.5 * curve.astype(F32)).astype(BF16)
    total = jnp.zeros((2 * half, rows), F32)
    for t in range(0, trades, tile):
        lanes = slice(t, t + tile)
        forward = forward_ref[:, lanes] + lax.dot_general(
            curve, w_fwd[near:, lanes], TN, preferred_element_type=F32
        )
        annuity = annuity_ref[:, lanes] + lax.dot_general(
            discount, w_disc[near:, lanes], TN, preferred_element_type=F32
        )
        forward_out[:, lanes] = forward
        annuity_out[:, lanes] = annuity
        vol = param_row(vol_ref, t, tile)
        option = jnp.broadcast_to(param_row(kind_ref, t, tile) == 1, (rows, tile))
        moneyness, e = option_terms(forward, param_row(strike_ref, t, tile), vol)
        payoff = jnp.where(option, swaption_payoff(moneyness, e, vol), moneyness)
        value = (param_row(notional_ref, t, tile) * annuity * payoff).astype(BF16)
        total += lax.dot_general(onehot[:, lanes], value, NT, preferred_element_type=F32)
    keep[...] = total[:half]
    send[...] = total[half:].astype(BF16)
    sets = threshold_ref.shape[1]
    chip = lax.axis_index("trade") // 2
    own = pl.ds(pl.multiple_of(chip * sets, sets), sets)
    square = iota((sets, sets), 0) == iota((sets, sets), 1)
    column = jnp.sum(jnp.where(square, threshold_ref[...], 0.0), axis=1, keepdims=True)
    keep[own, :] = keep[own, :] - column


def scale_kernel(
    forward_ref, annuity_ref, kind_ref, notional_ref, strike_ref, vol_ref, fwd_scale, ann_scale
):
    rows, trades = forward_ref.shape
    tile = TILE if trades % TILE == 0 else trades
    for t in range(0, trades, tile):
        lanes = slice(t, t + tile)
        vol = param_row(vol_ref, t, tile)
        notional = param_row(notional_ref, t, tile)
        option = jnp.broadcast_to(param_row(kind_ref, t, tile) == 1, (rows, tile))
        moneyness, e = option_terms(forward_ref[:, lanes], param_row(strike_ref, t, tile), vol)
        payoff = jnp.where(option, swaption_payoff(moneyness, e, vol), moneyness)
        sigmoid = jnp.where(moneyness >= 0.0, 1.0, e) / (1.0 + e)
        fwd_scale[:, lanes] = notional * annuity_ref[:, lanes] * jnp.where(option, sigmoid, 1.0)
        ann_scale[:, lanes] = notional * payoff


def pair_kernel(keep, arrived, extra, out):
    half = keep.shape[0]
    out[:half, :] = (keep[...] + arrived[...].astype(F32)).astype(BF16)
    out[half:, :] = extra[...]


def sets_kernel(weight_ref, *refs):
    parts, (cots, cva, excess_ref) = refs[:-3], refs[-3:]
    dates, sets = weight_ref.shape
    half, rows = excess_ref.shape
    me = lax.axis_index("trade")
    total = parts[0][...].astype(F32)
    for part in parts[1:]:
        total += part[...].astype(F32)
    excess = total[:half]
    excess_ref[...] = excess
    span = rows // dates
    pieces = total[half:].astype(BF16)
    line = iota((pieces.shape[0], rows), 0)
    weights = []
    for k in range(max(1, half // rows)):
        spread = (line % dates == iota(line.shape, 1) // span) & (line // (2 * dates) == k)
        weights.append(
            lax.dot_general(pieces, spread.astype(BF16), TN, preferred_element_type=F32)
        )
    weights = jnp.concatenate(weights, axis=0)[:half]
    e = jnp.exp(-jnp.abs(excess))
    sigmoid = jnp.where(excess >= 0.0, 1.0, e) / (1.0 + e)
    cots[...] = (weights * sigmoid).astype(BF16)
    chip = me // 2
    own = excess_ref[pl.ds(pl.multiple_of(chip * sets, sets), sets), :]
    exposure = jnp.maximum(own, 0.0) + log1p_unit(jnp.exp(-jnp.abs(own)))
    square = iota((sets, sets), 0) == iota((sets, sets), 1)
    date = iota((sets, rows), 1) // span
    column = jnp.zeros((sets, 1), F32)
    for d in range(dates):
        weight = jnp.where(square, weight_ref[d : d + 1, :], 0.0)
        weight = jnp.sum(weight, axis=1, keepdims=True)
        column += weight * jnp.sum(jnp.where(date == d, exposure, 0.0), axis=1, keepdims=True)
    cva[...] = jnp.sum(jnp.where(square, column, 0.0), axis=0, keepdims=True)


def half_cot(side, curves, fwd_cots, ann_cots, w_fwd, w_disc):
    half, trades = curves.shape[0], w_fwd.shape[1]
    tile = TILE if trades % TILE == 0 else trades
    band = slice(side * half, (side + 1) * half)
    from_fwd = from_disc = 0.0
    for t in range(0, trades, tile):
        lanes = slice(t, t + tile)
        from_fwd += lax.dot_general(
            w_fwd[band, lanes], fwd_cots[:, lanes], NT, preferred_element_type=F32
        )
        from_disc += lax.dot_general(
            w_disc[band, lanes], ann_cots[:, lanes], NT, preferred_element_type=F32
        )
    return from_fwd - 0.5 * jnp.exp(-0.5 * curves[...].astype(F32)) * from_disc


def adjoint_kernel(
    partner, cots_mine, cots_partner, fwd_scale, ann_scale, w_fwd, w_disc, onehot, send,
    fwd_cots, ann_cots,
):
    trades = fwd_scale.shape[1]
    tile = TILE if trades % TILE == 0 else trades
    cots = jnp.concatenate([cots_mine[...], cots_partner[...]], axis=0)
    for t in range(0, trades, tile):
        lanes = slice(t, t + tile)
        trade_cot = lax.dot_general(cots, onehot[:, lanes], TN, preferred_element_type=F32)
        fwd_cots[:, lanes] = (trade_cot * fwd_scale[:, lanes]).astype(BF16)
        ann_cots[:, lanes] = (trade_cot * ann_scale[:, lanes]).astype(BF16)
    send[...] = half_cot(1, partner, fwd_cots, ann_cots, w_fwd, w_disc).astype(BF16)


def keep_kernel(mine, fwd_cots, ann_cots, w_fwd, w_disc, keep):
    keep[...] = half_cot(0, mine, fwd_cots, ann_cots, w_fwd, w_disc)


def fold_kernel(count, kept, *refs):
    arrived, (keep, *sends) = refs[:count], refs[count:]
    total = kept[...]
    for part in arrived:
        total += part[...].astype(F32)
    size = keep.shape[0]
    keep[...] = total[:size]
    for k, send in enumerate(sends):
        send[...] = total[(k + 1) * size : (k + 2) * size].astype(BF16)


def factor_kernel(kept, arrived, basis, out):
    total = kept[...] + arrived[...].astype(F32)
    dims = (((0,), (1,)), ((), ()))
    high, low = split_bf16(total)
    out[...] = lax.dot_general(high, basis[...], dims, preferred_element_type=F32)
    out[...] += lax.dot_general(low, basis[...], dims, preferred_element_type=F32)


def call(
    kernel, name, out_shape, scratch=(), flops=1_000_000, moved=1_000_000, space=VMEM, last=None
):
    def run(*args):
        spaces = [space] * len(args)
        if last is not None:
            spaces[-1] = last
        args = [
            pltpu.with_memory_space_constraint(x, pltpu.HBM) if where is HBM else x
            for x, where in zip(args, spaces)
        ]
        return pl.pallas_call(
            kernel,
            in_specs=spaces,
            out_specs=jax.tree.map(lambda _: VMEM, out_shape),
            out_shape=out_shape,
            scratch_shapes=scratch,
            cost_estimate=pl.CostEstimate(flops=flops, bytes_accessed=moved, transcendentals=0),
            compiler_params=pltpu.CompilerParams(vmem_limit_bytes=VMEM_LIMIT),
            name=name,
        )(*args)

    return run


def swap(x, mask):
    n = lax.axis_size("trade")
    return lax.ppermute(x, "trade", [(i, i ^ mask) for i in range(n)])


def swaps(x, step):
    masks = [sum(b for k, b in enumerate(step) if j >> k & 1) for j in range(1, 2 ** len(step))]
    parts = {}
    for j in sorted(range(len(masks)), key=lambda j: -bin(masks[j]).count("1")):
        parts[j] = swap(x[j] if isinstance(x, (list, tuple)) else x, masks[j])
    return [parts[j] for j in range(len(masks))]


def sum_over(x, axis):
    n = lax.axis_size(axis)
    total = x
    for shift in range(1, n):
        total = total + lax.ppermute(x, axis, [(i, (i + shift) % n) for i in range(n)])
    return total


def shards(
    factor_paths, tenor_basis, trade_blocks, trade_set, trade_type, notional, strike,
    vol_level, cash_weights, set_threshold, date_weight,
):
    factor_rows, dates, paths = factor_paths.shape
    block_size, tenors = tenor_basis.shape
    rows = dates * paths
    devices = lax.axis_size("trade")
    local_blocks = factor_rows // block_size
    height = local_blocks * tenors
    local_sets = set_threshold.shape[0]
    half_sets = local_sets * devices // 2
    all_rows = height * devices
    trades = trade_set.shape[0]
    shape = jax.ShapeDtypeStruct
    extra_rows = -(-max(1, half_sets // rows) * 2 * dates // 8) * 8
    lane_rows = (trades // LANES, LANES)
    dma = pltpu.SemaphoreType.DMA

    factors = jnp.transpose(factor_paths, (1, 2, 0)).reshape(rows, factor_rows)
    single, group = steps_of(devices)
    arrived = swap(factors, single[0])
    curves, basis, weights, extra = call(
        curve_kernel, "curves",
        [shape((height, rows), BF16), shape((factor_rows, height), BF16),
         shape((dates, local_sets), F32), shape((extra_rows, rows), BF16)],
        [pltpu.VMEM((rows, factor_rows), BF16), pltpu.VMEM((tenors, block_size), BF16), dma((3,))],
        space=HBM,
    )(factors, jnp.transpose(tenor_basis), jnp.transpose(date_weight))
    curves = call(next_curve_kernel, "curves2", shape((2 * height, rows), BF16))(
        curves, arrived, basis
    )
    for mask in single[1:]:
        curves = jnp.concatenate([curves, swap(curves, mask)], axis=0)
    near = [curves] + swaps(curves, group)
    w_fwd, w_disc, onehot, *params = call(
        functools.partial(prep_kernel, devices), "prep",
        [shape((all_rows, trades), BF16)] * 2 + [shape((2 * half_sets, trades), BF16)]
        + [shape(lane_rows, jnp.int32)] + [shape(lane_rows, F32)] * 3 + [shape((1, local_sets), F32)],
        [pltpu.VMEM((2, trades), jnp.int32), pltpu.VMEM(lane_rows, jnp.int32),
         pltpu.VMEM((tenors, trades), F32), dma((8,))],
        flops=400_000_000, moved=8_000_000, space=HBM,
        last=VMEM,
    )(
        trade_blocks, trade_set.reshape(lane_rows), cash_weights, trade_type.reshape(lane_rows),
        notional.reshape(lane_rows), strike.reshape(lane_rows), vol_level.reshape(lane_rows),
        set_threshold[None], curves,
    )
    mine = call(join_kernel, "join", shape((all_rows // 2, rows), BF16))(*near, params[-1])
    partner = swap(mine, 1)
    forward, annuity = call(
        half_price_kernel, "price1", [shape((rows, trades), F32)] * 2,
        flops=400_000_000, moved=4_000_000,
    )(mine, w_fwd, w_disc)
    keep, send, forward, annuity = call(
        price_kernel, "price2",
        [shape((half_sets, rows), F32), shape((half_sets, rows), BF16),
         shape((rows, trades), F32), shape((rows, trades), F32)],
    )(partner, forward, annuity, w_fwd, w_disc, onehot, *params)
    fwd_scale, ann_scale = call(
        scale_kernel, "scales", [shape((rows, trades), F32)] * 2,
        flops=400_000_000, moved=4_000_000,
    )(forward, annuity, *params[:-1])

    total = call(pair_kernel, "pair", shape((half_sets + extra_rows, rows), BF16))(
        keep, swap(send, 1), extra
    )
    bits = [1 << k for k in range(1, bits_of(devices))]
    steps = [bits[:1]] if len(bits) % 2 else []
    steps += [bits[k : k + 2] for k in range(len(bits) % 2, len(bits), 2)]
    for step in steps:
        parts = [total] + swaps(total, step)
        if step is not steps[-1]:
            total = functools.reduce(jnp.add, [p.astype(F32) for p in parts]).astype(BF16)
    cots_mine, cva = call(
        sets_kernel, "sets",
        [shape((half_sets, rows), BF16), shape((1, local_sets), F32)],
        [pltpu.VMEM((half_sets, rows), F32)],
    )(weights, *parts)
    cots_partner = swap(cots_mine, 1)

    send, fwd_cots, ann_cots = call(
        adjoint_kernel, "adjoint",
        [shape((all_rows // 2, rows), BF16)] + [shape((rows, trades), BF16)] * 2,
    )(partner, cots_mine, cots_partner, fwd_scale, ann_scale, w_fwd, w_disc, onehot)
    keep = call(
        keep_kernel, "keep", shape((all_rows // 2, rows), F32),
        flops=200_000_000, moved=4_000_000,
    )(mine, fwd_cots, ann_cots, w_fwd, w_disc)
    arrived = [swap(send, 1)]
    size = all_rows // 2
    for step in [group] + [[mask] for mask in single[::-1]]:
        size >>= len(step)
        shapes = [shape((size, rows), F32)]
        shapes += [shape((size, rows), BF16)] * (2 ** len(step) - 1)
        keep, *sends = call(
            functools.partial(fold_kernel, len(arrived)), f"fold{step[0]}", shapes
        )(keep, *arrived)
        arrived = swaps(sends, step)
    factor_cot = call(factor_kernel, "factors", shape((rows, factor_rows), F32))(
        keep, *arrived, basis
    )
    factor_cot = jnp.transpose(factor_cot.reshape(dates, paths, factor_rows), (2, 0, 1))
    netting_cva = sum_over(cva[0], "path") / (paths * lax.axis_size("path"))
    return netting_cva, factor_cot


def solution(mesh):
    return jax.shard_map(
        shards,
        mesh=mesh,
        in_specs=(
            P("trade", None, "path"), P(), P(None, "trade"), P("trade"), P("trade"),
            P("trade"), P("trade"), P("trade"), P(None, "trade"), P("trade"),
            P("trade", None),
        ),
        out_specs=(P("trade"), P("trade", None, "path")),
        check_vma=False,
    )
```

```python
import functools
import math

import jax
import jax.numpy as jnp
from jax import lax
from jax.experimental import pallas as pl
from jax.experimental.pallas import tpu as pltpu
from jax.sharding import PartitionSpec as P

F32 = jnp.float32
BF16 = jnp.bfloat16
NT = (((1,), (1,)), ((), ()))
TN = (((0,), (0,)), ((), ()))
LANES = 128
TILE = 768
VMEM = pl.BlockSpec(memory_space=pltpu.VMEM)
HBM = pl.BlockSpec(memory_space=pltpu.HBM)
VMEM_LIMIT = 8 * 2**20


def log1p_unit(e):
    return jnp.where(e < 1e-4, (1.0 - 0.5 * e) * e, jnp.log(1.0 + e))


def split_bf16(x):
    high = x.astype(BF16)
    return high, (x - high.astype(F32)).astype(BF16)


def iota(shape, dim):
    return lax.broadcasted_iota(jnp.int32, shape, dim)


def block_basis(basis_t, factors, height):
    tenors, size = basis_t.shape
    down = (iota((factors, size), 0) % size == iota((factors, size), 1)).astype(BF16)
    across = (iota((tenors, height), 1) % tenors == iota((tenors, height), 0)).astype(BF16)
    spread = lax.dot_general(down, basis_t, NT, preferred_element_type=F32).astype(BF16)
    tiled = jnp.dot(spread, across, preferred_element_type=F32)
    same = iota((factors, height), 0) // size == iota((factors, height), 1) // tenors
    return jnp.where(same, tiled, 0.0).astype(BF16)


def bits_of(n):
    return int(math.log2(n))


def pair_order(ids, local, devices):
    core = lax.rem(lax.axis_index("trade"), 2)
    owner = jnp.right_shift(ids, bits_of(local))
    side = jnp.bitwise_xor(jnp.bitwise_and(owner, 1), core)
    place = side * (devices // 2) + jnp.right_shift(owner, 1)
    return place * local + jnp.bitwise_and(ids, local - 1)


def steps_of(devices):
    bits = [1 << k for k in range(1, bits_of(devices))]
    return bits[2:][::-1], bits[:2]


def cube_place(owner, devices):
    distance = jnp.bitwise_xor(owner, lax.axis_index("trade"))
    single, group = steps_of(devices)
    place = jnp.zeros_like(distance)
    for k, mask in enumerate(single + group + [1]):
        bit = jnp.bitwise_and(jnp.right_shift(distance, bits_of(mask)), 1)
        place = jnp.bitwise_or(place, jnp.left_shift(bit, k))
    return place


def cube_order(ids, local, devices):
    place = cube_place(jnp.right_shift(ids, bits_of(local)), devices)
    return place * local + jnp.bitwise_and(ids, local - 1)


def fetch(pairs, sems):
    copies = [pltpu.make_async_copy(src, dst, sems.at[k]) for k, (src, dst) in enumerate(pairs)]
    for copy in copies:
        copy.start()
    for copy in copies:
        copy.wait()


def curves_of(basis, factors):
    dims = (((0,), (1,)), ((), ()))
    return lax.dot_general(basis, factors, dims, preferred_element_type=F32).astype(BF16)


def curve_kernel(
    factors_hbm, basis_hbm, weight_hbm, out, basis_out, weight_ref, extra, factors_ref,
    basis_ref, sems,
):
    fetch(
        [(factors_hbm, factors_ref), (basis_hbm, basis_ref), (weight_hbm, weight_ref)], sems
    )
    factors = factors_ref.shape[1]
    tenors, size = basis_ref.shape
    basis = block_basis(basis_ref[...], factors, factors // size * tenors)
    basis_out[...] = basis
    out[...] = curves_of(basis, factors_ref[...])
    dates, sets = weight_ref.shape
    rows, lanes = extra.shape
    first = lax.axis_index("trade") // 2 * sets
    spot = (iota((sets, lanes), 1) == iota((sets, lanes), 0) + lax.rem(first, lanes)).astype(BF16)
    total = jnp.zeros((rows, lanes), F32)
    for k, part in enumerate(split_bf16(weight_ref[...])):
        top = (first // lanes * 2 + k) * dates
        lift = (iota((rows, dates), 0) == iota((rows, dates), 1) + top).astype(BF16)
        lifted = jnp.dot(lift, part, preferred_element_type=F32).astype(BF16)
        total += jnp.dot(lifted, spot, preferred_element_type=F32)
    extra[...] = total.astype(BF16)


def next_curve_kernel(own, arrived, basis, out):
    height = own.shape[0]
    out[:height, :] = own[...]
    out[height:, :] = curves_of(basis[...], arrived[...])


def join_kernel(*refs):
    *parts, _, out = refs
    height = parts[0].shape[0]
    for k, part in enumerate(parts):
        out[k * height : (k + 1) * height, :] = part[...]


def prep_kernel(devices, *refs):
    sources, rest = refs[:8], refs[9:]
    w_fwd, w_disc, onehot = rest[:3]
    params, (blocks_ref, set_ref, weights_ref, sems) = rest[3:8], rest[8:]
    fetch(list(zip(sources, (blocks_ref, set_ref, weights_ref) + tuple(params))), sems)
    tenors, trades = weights_ref.shape
    height = w_fwd.shape[0]
    blocks = height // tenors
    sets = onehot.shape[0]
    zero = jnp.zeros((tenors, LANES), F32)
    row = iota((16, LANES), 0)
    set_rows = pair_order(set_ref[...], sets // devices, devices)
    block_rows = cube_order(blocks_ref[...], blocks // devices, devices)
    for t in range(0, trades, LANES):
        lanes = slice(t, t + LANES)
        weights = weights_ref[:, lanes]
        for k, out in enumerate((w_fwd, w_disc)):
            ids = jnp.broadcast_to(block_rows[k : k + 1, lanes], (tenors, LANES))
            for b in range(blocks):
                out[b * tenors : (b + 1) * tenors, lanes] = jnp.where(
                    ids == b, weights, zero
                ).astype(BF16)
        ids = jnp.broadcast_to(set_rows[t // LANES : t // LANES + 1, :], (16, LANES))
        for n in range(0, sets, 16):
            onehot[n : n + 16, lanes] = jnp.where(ids == row + n, 1.0, 0.0).astype(BF16)


def param_row(ref, start, tile):
    return jnp.concatenate(
        [ref[j : j + 1, :] for j in range(start // LANES, (start + tile) // LANES)], axis=1
    )


def half_price_kernel(curves, w_fwd, w_disc, forward, annuity):
    half, trades = curves.shape[0], w_fwd.shape[1]
    tile = TILE if trades % TILE == 0 else trades
    curve = curves[...]
    discount = jnp.exp(-0.5 * curve.astype(F32)).astype(BF16)
    for t in range(0, trades, tile):
        lanes = slice(t, t + tile)
        forward[:, lanes] = lax.dot_general(
            curve, w_fwd[:half, lanes], TN, preferred_element_type=F32
        )
        annuity[:, lanes] = lax.dot_general(
            discount, w_disc[:half, lanes], TN, preferred_element_type=F32
        )


def option_terms(forward, strike, vol):
    moneyness = forward - strike
    return moneyness, jnp.exp(jnp.abs(moneyness) * (-1.0 / vol))


def swaption_payoff(moneyness, e, vol):
    return jnp.maximum(moneyness, 0.0) + vol * log1p_unit(e)


def price_kernel(
    curves, forward_ref, annuity_ref, w_fwd, w_disc, onehot, kind_ref, notional_ref, strike_ref,
    vol_ref, threshold_ref, keep, send, forward_out, annuity_out,
):
    near, rows = curves.shape
    trades = w_fwd.shape[1]
    half = keep.shape[0]
    tile = TILE if trades % TILE == 0 else trades
    curve = curves[...]
    discount = jnp.exp(-0.5 * curve.astype(F32)).astype(BF16)
    total = jnp.zeros((2 * half, rows), F32)
    for t in range(0, trades, tile):
        lanes = slice(t, t + tile)
        forward = forward_ref[:, lanes] + lax.dot_general(
            curve, w_fwd[near:, lanes], TN, preferred_element_type=F32
        )
        annuity = annuity_ref[:, lanes] + lax.dot_general(
            discount, w_disc[near:, lanes], TN, preferred_element_type=F32
        )
        forward_out[:, lanes] = forward
        annuity_out[:, lanes] = annuity
        vol = param_row(vol_ref, t, tile)
        option = jnp.broadcast_to(param_row(kind_ref, t, tile) == 1, (rows, tile))
        moneyness, e = option_terms(forward, param_row(strike_ref, t, tile), vol)
        payoff = jnp.where(option, swaption_payoff(moneyness, e, vol), moneyness)
        value = (param_row(notional_ref, t, tile) * annuity * payoff).astype(BF16)
        total += lax.dot_general(onehot[:, lanes], value, NT, preferred_element_type=F32)
    keep[...] = total[:half]
    send[...] = total[half:].astype(BF16)
    sets = threshold_ref.shape[1]
    chip = lax.axis_index("trade") // 2
    own = pl.ds(pl.multiple_of(chip * sets, sets), sets)
    square = iota((sets, sets), 0) == iota((sets, sets), 1)
    column = jnp.sum(jnp.where(square, threshold_ref[...], 0.0), axis=1, keepdims=True)
    keep[own, :] = keep[own, :] - column


def scale_kernel(
    forward_ref, annuity_ref, kind_ref, notional_ref, strike_ref, vol_ref, fwd_scale, ann_scale
):
    rows, trades = forward_ref.shape
    tile = TILE if trades % TILE == 0 else trades
    for t in range(0, trades, tile):
        lanes = slice(t, t + tile)
        vol = param_row(vol_ref, t, tile)
        notional = param_row(notional_ref, t, tile)
        option = jnp.broadcast_to(param_row(kind_ref, t, tile) == 1, (rows, tile))
        moneyness, e = option_terms(forward_ref[:, lanes], param_row(strike_ref, t, tile), vol)
        payoff = jnp.where(option, swaption_payoff(moneyness, e, vol), moneyness)
        sigmoid = jnp.where(moneyness >= 0.0, 1.0, e) / (1.0 + e)
        fwd_scale[:, lanes] = notional * annuity_ref[:, lanes] * jnp.where(option, sigmoid, 1.0)
        ann_scale[:, lanes] = notional * payoff


def pair_kernel(keep, arrived, extra, out):
    half = keep.shape[0]
    out[:half, :] = (keep[...] + arrived[...].astype(F32)).astype(BF16)
    out[half:, :] = extra[...]


def sets_kernel(weight_ref, *refs):
    parts, (cots, cva, excess_ref) = refs[:-3], refs[-3:]
    dates, sets = weight_ref.shape
    half, rows = excess_ref.shape
    me = lax.axis_index("trade")
    total = parts[0][...].astype(F32)
    for part in parts[1:]:
        total += part[...].astype(F32)
    excess = total[:half]
    excess_ref[...] = excess
    span = rows // dates
    pieces = total[half:].astype(BF16)
    line = iota((pieces.shape[0], rows), 0)
    weights = []
    for k in range(max(1, half // rows)):
        spread = (line % dates == iota(line.shape, 1) // span) & (line // (2 * dates) == k)
        weights.append(
            lax.dot_general(pieces, spread.astype(BF16), TN, preferred_element_type=F32)
        )
    weights = jnp.concatenate(weights, axis=0)[:half]
    e = jnp.exp(-jnp.abs(excess))
    sigmoid = jnp.where(excess >= 0.0, 1.0, e) / (1.0 + e)
    cots[...] = (weights * sigmoid).astype(BF16)
    chip = me // 2
    own = excess_ref[pl.ds(pl.multiple_of(chip * sets, sets), sets), :]
    exposure = jnp.maximum(own, 0.0) + log1p_unit(jnp.exp(-jnp.abs(own)))
    square = iota((sets, sets), 0) == iota((sets, sets), 1)
    date = iota((sets, rows), 1) // span
    column = jnp.zeros((sets, 1), F32)
    for d in range(dates):
        weight = jnp.where(square, weight_ref[d : d + 1, :], 0.0)
        weight = jnp.sum(weight, axis=1, keepdims=True)
        column += weight * jnp.sum(jnp.where(date == d, exposure, 0.0), axis=1, keepdims=True)
    cva[...] = jnp.sum(jnp.where(square, column, 0.0), axis=0, keepdims=True)


def half_cot(side, curves, fwd_cots, ann_cots, w_fwd, w_disc):
    half, trades = curves.shape[0], w_fwd.shape[1]
    tile = TILE if trades % TILE == 0 else trades
    band = slice(side * half, (side + 1) * half)
    from_fwd = from_disc = 0.0
    for t in range(0, trades, tile):
        lanes = slice(t, t + tile)
        from_fwd += lax.dot_general(
            w_fwd[band, lanes], fwd_cots[:, lanes], NT, preferred_element_type=F32
        )
        from_disc += lax.dot_general(
            w_disc[band, lanes], ann_cots[:, lanes], NT, preferred_element_type=F32
        )
    return from_fwd - 0.5 * jnp.exp(-0.5 * curves[...].astype(F32)) * from_disc


def adjoint_kernel(
    partner, cots_mine, cots_partner, fwd_scale, ann_scale, w_fwd, w_disc, onehot, send,
    fwd_cots, ann_cots,
):
    trades = fwd_scale.shape[1]
    tile = TILE if trades % TILE == 0 else trades
    cots = jnp.concatenate([cots_mine[...], cots_partner[...]], axis=0)
    for t in range(0, trades, tile):
        lanes = slice(t, t + tile)
        trade_cot = lax.dot_general(cots, onehot[:, lanes], TN, preferred_element_type=F32)
        fwd_cots[:, lanes] = (trade_cot * fwd_scale[:, lanes]).astype(BF16)
        ann_cots[:, lanes] = (trade_cot * ann_scale[:, lanes]).astype(BF16)
    send[...] = half_cot(1, partner, fwd_cots, ann_cots, w_fwd, w_disc).astype(BF16)


def keep_kernel(mine, fwd_cots, ann_cots, w_fwd, w_disc, keep):
    keep[...] = half_cot(0, mine, fwd_cots, ann_cots, w_fwd, w_disc)


def fold_kernel(count, kept, *refs):
    arrived, (keep, *sends) = refs[:count], refs[count:]
    total = kept[...]
    for part in arrived:
        total += part[...].astype(F32)
    size = keep.shape[0]
    keep[...] = total[:size]
    for k, send in enumerate(sends):
        send[...] = total[(k + 1) * size : (k + 2) * size].astype(BF16)


def factor_kernel(kept, arrived, basis, out):
    total = kept[...] + arrived[...].astype(F32)
    dims = (((0,), (1,)), ((), ()))
    high, low = split_bf16(total)
    out[...] = lax.dot_general(high, basis[...], dims, preferred_element_type=F32)
    out[...] += lax.dot_general(low, basis[...], dims, preferred_element_type=F32)


def call(
    kernel, name, out_shape, scratch=(), flops=1_000_000, moved=1_000_000, space=VMEM, last=None
):
    def run(*args):
        spaces = [space] * len(args)
        if last is not None:
            spaces[-1] = last
        args = [
            pltpu.with_memory_space_constraint(x, pltpu.HBM) if where is HBM else x
            for x, where in zip(args, spaces)
        ]
        return pl.pallas_call(
            kernel,
            in_specs=spaces,
            out_specs=jax.tree.map(lambda _: VMEM, out_shape),
            out_shape=out_shape,
            scratch_shapes=scratch,
            cost_estimate=pl.CostEstimate(flops=flops, bytes_accessed=moved, transcendentals=0),
            compiler_params=pltpu.CompilerParams(vmem_limit_bytes=VMEM_LIMIT),
            name=name,
        )(*args)

    return run


def swap(x, mask):
    n = lax.axis_size("trade")
    return lax.ppermute(x, "trade", [(i, i ^ mask) for i in range(n)])


def swaps(x, step):
    masks = [sum(b for k, b in enumerate(step) if j >> k & 1) for j in range(1, 2 ** len(step))]
    parts = {}
    for j in sorted(range(len(masks)), key=lambda j: -bin(masks[j]).count("1")):
        parts[j] = swap(x[j] if isinstance(x, (list, tuple)) else x, masks[j])
    return [parts[j] for j in range(len(masks))]


def ordered(parts, order):
    return [parts[k] for k in order] if len(parts) == len(order) else parts


def sum_over(x, axis):
    n = lax.axis_size(axis)
    total = x
    for shift in range(1, n):
        total = total + lax.ppermute(x, axis, [(i, (i + shift) % n) for i in range(n)])
    return total


def shards(
    factor_paths, tenor_basis, trade_blocks, trade_set, trade_type, notional, strike,
    vol_level, cash_weights, set_threshold, date_weight,
):
    factor_rows, dates, paths = factor_paths.shape
    block_size, tenors = tenor_basis.shape
    rows = dates * paths
    devices = lax.axis_size("trade")
    local_blocks = factor_rows // block_size
    height = local_blocks * tenors
    local_sets = set_threshold.shape[0]
    half_sets = local_sets * devices // 2
    all_rows = height * devices
    trades = trade_set.shape[0]
    shape = jax.ShapeDtypeStruct
    extra_rows = -(-max(1, half_sets // rows) * 2 * dates // 8) * 8
    lane_rows = (trades // LANES, LANES)
    dma = pltpu.SemaphoreType.DMA

    factors = jnp.transpose(factor_paths, (1, 2, 0)).reshape(rows, factor_rows)
    single, group = steps_of(devices)
    arrived = swap(factors, single[0])
    curves, basis, weights, extra = call(
        curve_kernel, "curves",
        [shape((height, rows), BF16), shape((factor_rows, height), BF16),
         shape((dates, local_sets), F32), shape((extra_rows, rows), BF16)],
        [pltpu.VMEM((rows, factor_rows), BF16), pltpu.VMEM((tenors, block_size), BF16), dma((3,))],
        space=HBM,
    )(factors, jnp.transpose(tenor_basis), jnp.transpose(date_weight))
    curves = call(next_curve_kernel, "curves2", shape((2 * height, rows), BF16))(
        curves, arrived, basis
    )
    for mask in single[1:]:
        curves = jnp.concatenate([curves, swap(curves, mask)], axis=0)
    near = [curves] + swaps(curves, group)
    w_fwd, w_disc, onehot, *params = call(
        functools.partial(prep_kernel, devices), "prep",
        [shape((all_rows, trades), BF16)] * 2 + [shape((2 * half_sets, trades), BF16)]
        + [shape(lane_rows, jnp.int32)] + [shape(lane_rows, F32)] * 3 + [shape((1, local_sets), F32)],
        [pltpu.VMEM((2, trades), jnp.int32), pltpu.VMEM(lane_rows, jnp.int32),
         pltpu.VMEM((tenors, trades), F32), dma((8,))],
        flops=400_000_000, moved=8_000_000, space=HBM,
        last=VMEM,
    )(
        trade_blocks, trade_set.reshape(lane_rows), cash_weights, trade_type.reshape(lane_rows),
        notional.reshape(lane_rows), strike.reshape(lane_rows), vol_level.reshape(lane_rows),
        set_threshold[None], curves,
    )
    mine = call(join_kernel, "join", shape((all_rows // 2, rows), BF16))(*near, params[-1])
    partner = swap(mine, 1)
    forward, annuity = call(
        half_price_kernel, "price1", [shape((rows, trades), F32)] * 2,
        flops=400_000_000, moved=4_000_000,
    )(mine, w_fwd, w_disc)
    keep, send, forward, annuity = call(
        price_kernel, "price2",
        [shape((half_sets, rows), F32), shape((half_sets, rows), BF16),
         shape((rows, trades), F32), shape((rows, trades), F32)],
    )(partner, forward, annuity, w_fwd, w_disc, onehot, *params)
    fwd_scale, ann_scale = call(
        scale_kernel, "scales", [shape((rows, trades), F32)] * 2,
        flops=400_000_000, moved=4_000_000,
    )(forward, annuity, *params[:-1])

    total = call(pair_kernel, "pair", shape((half_sets + extra_rows, rows), BF16))(
        keep, swap(send, 1), extra
    )
    bits = [1 << k for k in range(1, bits_of(devices))]
    steps = [bits[:1]] if len(bits) % 2 else []
    steps += [bits[k : k + 2] for k in range(len(bits) % 2, len(bits), 2)]
    for step in steps:
        parts = [total] + swaps(total, step)
        if step is not steps[-1]:
            total = functools.reduce(jnp.add, [p.astype(F32) for p in parts]).astype(BF16)
    cots_mine, cva = call(
        sets_kernel, "sets",
        [shape((half_sets, rows), BF16), shape((1, local_sets), F32)],
        [pltpu.VMEM((half_sets, rows), F32)],
    )(weights, *ordered(parts, (0, 1, 3, 2)))
    cots_partner = swap(cots_mine, 1)

    send, fwd_cots, ann_cots = call(
        adjoint_kernel, "adjoint",
        [shape((all_rows // 2, rows), BF16)] + [shape((rows, trades), BF16)] * 2,
    )(partner, cots_mine, cots_partner, fwd_scale, ann_scale, w_fwd, w_disc, onehot)
    keep = call(
        keep_kernel, "keep", shape((all_rows // 2, rows), F32),
        flops=200_000_000, moved=4_000_000,
    )(mine, fwd_cots, ann_cots, w_fwd, w_disc)
    arrived = [swap(send, 1)]
    size = all_rows // 2
    for step in [group] + [[mask] for mask in single[::-1]]:
        size >>= len(step)
        shapes = [shape((size, rows), F32)]
        shapes += [shape((size, rows), BF16)] * (2 ** len(step) - 1)
        keep, *sends = call(
            functools.partial(fold_kernel, len(arrived)), f"fold{step[0]}", shapes
        )(keep, *ordered(arrived, (2, 0, 1)))
        arrived = swaps(sends, step)
    factor_cot = call(factor_kernel, "factors", shape((rows, factor_rows), F32))(
        keep, *arrived, basis
    )
    factor_cot = jnp.transpose(factor_cot.reshape(dates, paths, factor_rows), (2, 0, 1))
    netting_cva = sum_over(cva[0], "path") / (paths * lax.axis_size("path"))
    return netting_cva, factor_cot


def solution(mesh):
    return jax.shard_map(
        shards,
        mesh=mesh,
        in_specs=(
            P("trade", None, "path"), P(), P(None, "trade"), P("trade"), P("trade"),
            P("trade"), P("trade"), P("trade"), P(None, "trade"), P("trade"),
            P("trade", None),
        ),
        out_specs=(P("trade"), P("trade", None, "path")),
        check_vma=False,
    )
```

```python
import functools
import math

import jax
import jax.numpy as jnp
from jax import lax
from jax.experimental import pallas as pl
from jax.experimental.pallas import tpu as pltpu
from jax.sharding import PartitionSpec as P

F32 = jnp.float32
BF16 = jnp.bfloat16
NT = (((1,), (1,)), ((), ()))
TN = (((0,), (0,)), ((), ()))
LANES = 128
TILE = 768
VMEM = pl.BlockSpec(memory_space=pltpu.VMEM)
HBM = pl.BlockSpec(memory_space=pltpu.HBM)
VMEM_LIMIT = 8 * 2**20


def log1p_unit(e):
    return jnp.where(e < 1e-4, (1.0 - 0.5 * e) * e, jnp.log(1.0 + e))


def split_bf16(x):
    high = x.astype(BF16)
    return high, (x - high.astype(F32)).astype(BF16)


def iota(shape, dim):
    return lax.broadcasted_iota(jnp.int32, shape, dim)


def block_basis(basis_t, factors, height):
    tenors, size = basis_t.shape
    down = (iota((factors, size), 0) % size == iota((factors, size), 1)).astype(BF16)
    across = (iota((tenors, height), 1) % tenors == iota((tenors, height), 0)).astype(BF16)
    spread = lax.dot_general(down, basis_t, NT, preferred_element_type=F32).astype(BF16)
    tiled = jnp.dot(spread, across, preferred_element_type=F32)
    same = iota((factors, height), 0) // size == iota((factors, height), 1) // tenors
    return jnp.where(same, tiled, 0.0).astype(BF16)


def bits_of(n):
    return int(math.log2(n))


def pair_order(ids, local, devices):
    core = lax.rem(lax.axis_index("trade"), 2)
    owner = jnp.right_shift(ids, bits_of(local))
    side = jnp.bitwise_xor(jnp.bitwise_and(owner, 1), core)
    place = side * (devices // 2) + jnp.right_shift(owner, 1)
    return place * local + jnp.bitwise_and(ids, local - 1)


def steps_of(devices):
    bits = [1 << k for k in range(1, bits_of(devices))]
    return bits[2:][::-1], bits[:2]


def cube_place(owner, devices):
    distance = jnp.bitwise_xor(owner, lax.axis_index("trade"))
    single, group = steps_of(devices)
    place = jnp.zeros_like(distance)
    for k, mask in enumerate(single + group + [1]):
        bit = jnp.bitwise_and(jnp.right_shift(distance, bits_of(mask)), 1)
        place = jnp.bitwise_or(place, jnp.left_shift(bit, k))
    return place


def cube_order(ids, local, devices):
    place = cube_place(jnp.right_shift(ids, bits_of(local)), devices)
    return place * local + jnp.bitwise_and(ids, local - 1)


def fetch(pairs, sems):
    copies = [pltpu.make_async_copy(src, dst, sems.at[k]) for k, (src, dst) in enumerate(pairs)]
    for copy in copies:
        copy.start()
    for copy in copies:
        copy.wait()


def curves_of(basis, factors):
    dims = (((0,), (1,)), ((), ()))
    return lax.dot_general(basis, factors, dims, preferred_element_type=F32).astype(BF16)


def curve_kernel(
    factors_hbm, basis_hbm, weight_hbm, out, basis_out, weight_ref, extra, factors_ref,
    basis_ref, sems,
):
    fetch(
        [(factors_hbm, factors_ref), (basis_hbm, basis_ref), (weight_hbm, weight_ref)], sems
    )
    factors = factors_ref.shape[1]
    tenors, size = basis_ref.shape
    basis = block_basis(basis_ref[...], factors, factors // size * tenors)
    basis_out[...] = basis
    out[...] = curves_of(basis, factors_ref[...])
    dates, sets = weight_ref.shape
    rows, lanes = extra.shape
    first = lax.axis_index("trade") // 2 * sets
    spot = (iota((sets, lanes), 1) == iota((sets, lanes), 0) + lax.rem(first, lanes)).astype(BF16)
    total = jnp.zeros((rows, lanes), F32)
    for k, part in enumerate(split_bf16(weight_ref[...])):
        top = (first // lanes * 2 + k) * dates
        lift = (iota((rows, dates), 0) == iota((rows, dates), 1) + top).astype(BF16)
        lifted = jnp.dot(lift, part, preferred_element_type=F32).astype(BF16)
        total += jnp.dot(lifted, spot, preferred_element_type=F32)
    extra[...] = total.astype(BF16)


def next_curve_kernel(own, arrived, basis, out):
    height = own.shape[0]
    out[:height, :] = own[...]
    out[height:, :] = curves_of(basis[...], arrived[...])


def join_kernel(*refs):
    *parts, _, out = refs
    height = parts[0].shape[0]
    for k, part in enumerate(parts):
        out[k * height : (k + 1) * height, :] = part[...]


def prep_kernel(devices, *refs):
    sources, rest = refs[:8], refs[9:]
    w_fwd, w_disc, onehot = rest[:3]
    params, (blocks_ref, set_ref, weights_ref, sems) = rest[3:8], rest[8:]
    fetch(list(zip(sources, (blocks_ref, set_ref, weights_ref) + tuple(params))), sems)
    tenors, trades = weights_ref.shape
    height = w_fwd.shape[0]
    blocks = height // tenors
    sets = onehot.shape[0]
    zero = jnp.zeros((tenors, LANES), F32)
    row = iota((16, LANES), 0)
    set_rows = pair_order(set_ref[...], sets // devices, devices)
    block_rows = cube_order(blocks_ref[...], blocks // devices, devices)
    for t in range(0, trades, LANES):
        lanes = slice(t, t + LANES)
        weights = weights_ref[:, lanes]
        for k, out in enumerate((w_fwd, w_disc)):
            ids = jnp.broadcast_to(block_rows[k : k + 1, lanes], (tenors, LANES))
            for b in range(blocks):
                out[b * tenors : (b + 1) * tenors, lanes] = jnp.where(
                    ids == b, weights, zero
                ).astype(BF16)
        ids = jnp.broadcast_to(set_rows[t // LANES : t // LANES + 1, :], (16, LANES))
        for n in range(0, sets, 16):
            onehot[n : n + 16, lanes] = jnp.where(ids == row + n, 1.0, 0.0).astype(BF16)


def param_row(ref, start, tile):
    return jnp.concatenate(
        [ref[j : j + 1, :] for j in range(start // LANES, (start + tile) // LANES)], axis=1
    )


def half_price_kernel(curves, w_fwd, w_disc, forward, annuity):
    half, trades = curves.shape[0], w_fwd.shape[1]
    tile = TILE if trades % TILE == 0 else trades
    curve = curves[...]
    discount = jnp.exp(-0.5 * curve.astype(F32)).astype(BF16)
    for t in range(0, trades, tile):
        lanes = slice(t, t + tile)
        forward[:, lanes] = lax.dot_general(
            curve, w_fwd[:half, lanes], TN, preferred_element_type=F32
        )
        annuity[:, lanes] = lax.dot_general(
            discount, w_disc[:half, lanes], TN, preferred_element_type=F32
        )


def option_terms(forward, strike, vol):
    moneyness = forward - strike
    return moneyness, jnp.exp(jnp.abs(moneyness) * (-1.0 / vol))


def swaption_payoff(moneyness, e, vol):
    return jnp.maximum(moneyness, 0.0) + vol * log1p_unit(e)


def price_kernel(
    curves, forward_ref, annuity_ref, w_fwd, w_disc, onehot, kind_ref, notional_ref, strike_ref,
    vol_ref, send, values, forward_out, annuity_out,
):
    near, rows = curves.shape
    trades = w_fwd.shape[1]
    half = send.shape[0]
    tile = TILE if trades % TILE == 0 else trades
    curve = curves[...]
    discount = jnp.exp(-0.5 * curve.astype(F32)).astype(BF16)
    total = jnp.zeros((half, rows), F32)
    for t in range(0, trades, tile):
        lanes = slice(t, t + tile)
        forward = forward_ref[:, lanes] + lax.dot_general(
            curve, w_fwd[near:, lanes], TN, preferred_element_type=F32
        )
        annuity = annuity_ref[:, lanes] + lax.dot_general(
            discount, w_disc[near:, lanes], TN, preferred_element_type=F32
        )
        forward_out[:, lanes] = forward
        annuity_out[:, lanes] = annuity
        vol = param_row(vol_ref, t, tile)
        option = jnp.broadcast_to(param_row(kind_ref, t, tile) == 1, (rows, tile))
        moneyness, e = option_terms(forward, param_row(strike_ref, t, tile), vol)
        payoff = jnp.where(option, swaption_payoff(moneyness, e, vol), moneyness)
        value = (param_row(notional_ref, t, tile) * annuity * payoff).astype(BF16)
        values[:, lanes] = value
        total += lax.dot_general(onehot[half:, lanes], value, NT, preferred_element_type=F32)
    send[...] = total.astype(BF16)


def own_sets_kernel(values, onehot, threshold_ref, keep):
    half = keep.shape[0]
    keep[...] = lax.dot_general(onehot[:half, :], values[...], NT, preferred_element_type=F32)
    sets = threshold_ref.shape[1]
    chip = lax.axis_index("trade") // 2
    own = pl.ds(pl.multiple_of(chip * sets, sets), sets)
    square = iota((sets, sets), 0) == iota((sets, sets), 1)
    column = jnp.sum(jnp.where(square, threshold_ref[...], 0.0), axis=1, keepdims=True)
    keep[own, :] = keep[own, :] - column


def scale_kernel(
    forward_ref, annuity_ref, kind_ref, notional_ref, strike_ref, vol_ref, fwd_scale, ann_scale
):
    rows, trades = forward_ref.shape
    tile = TILE if trades % TILE == 0 else trades
    for t in range(0, trades, tile):
        lanes = slice(t, t + tile)
        vol = param_row(vol_ref, t, tile)
        notional = param_row(notional_ref, t, tile)
        option = jnp.broadcast_to(param_row(kind_ref, t, tile) == 1, (rows, tile))
        moneyness, e = option_terms(forward_ref[:, lanes], param_row(strike_ref, t, tile), vol)
        payoff = jnp.where(option, swaption_payoff(moneyness, e, vol), moneyness)
        sigmoid = jnp.where(moneyness >= 0.0, 1.0, e) / (1.0 + e)
        fwd_scale[:, lanes] = notional * annuity_ref[:, lanes] * jnp.where(option, sigmoid, 1.0)
        ann_scale[:, lanes] = notional * payoff


def pair_kernel(keep, arrived, extra, out):
    half = keep.shape[0]
    out[:half, :] = (keep[...] + arrived[...].astype(F32)).astype(BF16)
    out[half:, :] = extra[...]


def sets_kernel(weight_ref, *refs):
    parts, (cots, cva, excess_ref) = refs[:-3], refs[-3:]
    dates, sets = weight_ref.shape
    half, rows = excess_ref.shape
    me = lax.axis_index("trade")
    total = parts[0][...].astype(F32)
    for part in parts[1:]:
        total += part[...].astype(F32)
    excess = total[:half]
    excess_ref[...] = excess
    span = rows // dates
    pieces = total[half:].astype(BF16)
    line = iota((pieces.shape[0], rows), 0)
    weights = []
    for k in range(max(1, half // rows)):
        spread = (line % dates == iota(line.shape, 1) // span) & (line // (2 * dates) == k)
        weights.append(
            lax.dot_general(pieces, spread.astype(BF16), TN, preferred_element_type=F32)
        )
    weights = jnp.concatenate(weights, axis=0)[:half]
    e = jnp.exp(-jnp.abs(excess))
    sigmoid = jnp.where(excess >= 0.0, 1.0, e) / (1.0 + e)
    cots[...] = (weights * sigmoid).astype(BF16)
    chip = me // 2
    own = excess_ref[pl.ds(pl.multiple_of(chip * sets, sets), sets), :]
    exposure = jnp.maximum(own, 0.0) + log1p_unit(jnp.exp(-jnp.abs(own)))
    square = iota((sets, sets), 0) == iota((sets, sets), 1)
    date = iota((sets, rows), 1) // span
    column = jnp.zeros((sets, 1), F32)
    for d in range(dates):
        weight = jnp.where(square, weight_ref[d : d + 1, :], 0.0)
        weight = jnp.sum(weight, axis=1, keepdims=True)
        column += weight * jnp.sum(jnp.where(date == d, exposure, 0.0), axis=1, keepdims=True)
    cva[...] = jnp.sum(jnp.where(square, column, 0.0), axis=0, keepdims=True)


def half_cot(side, curves, fwd_cots, ann_cots, w_fwd, w_disc):
    half, trades = curves.shape[0], w_fwd.shape[1]
    tile = TILE if trades % TILE == 0 else trades
    band = slice(side * half, (side + 1) * half)
    from_fwd = from_disc = 0.0
    for t in range(0, trades, tile):
        lanes = slice(t, t + tile)
        from_fwd += lax.dot_general(
            w_fwd[band, lanes], fwd_cots[:, lanes], NT, preferred_element_type=F32
        )
        from_disc += lax.dot_general(
            w_disc[band, lanes], ann_cots[:, lanes], NT, preferred_element_type=F32
        )
    return from_fwd - 0.5 * jnp.exp(-0.5 * curves[...].astype(F32)) * from_disc


def adjoint_kernel(
    partner, cots_mine, cots_partner, fwd_scale, ann_scale, w_fwd, w_disc, onehot, send,
    fwd_cots, ann_cots,
):
    trades = fwd_scale.shape[1]
    tile = TILE if trades % TILE == 0 else trades
    cots = jnp.concatenate([cots_mine[...], cots_partner[...]], axis=0)
    for t in range(0, trades, tile):
        lanes = slice(t, t + tile)
        trade_cot = lax.dot_general(cots, onehot[:, lanes], TN, preferred_element_type=F32)
        fwd_cots[:, lanes] = (trade_cot * fwd_scale[:, lanes]).astype(BF16)
        ann_cots[:, lanes] = (trade_cot * ann_scale[:, lanes]).astype(BF16)
    send[...] = half_cot(1, partner, fwd_cots, ann_cots, w_fwd, w_disc).astype(BF16)


def keep_kernel(mine, fwd_cots, ann_cots, w_fwd, w_disc, keep):
    keep[...] = half_cot(0, mine, fwd_cots, ann_cots, w_fwd, w_disc)


def fold_kernel(count, kept, *refs):
    arrived, (keep, *sends) = refs[:count], refs[count:]
    total = kept[...]
    for part in arrived:
        total += part[...].astype(F32)
    size = keep.shape[0]
    keep[...] = total[:size]
    for k, send in enumerate(sends):
        send[...] = total[(k + 1) * size : (k + 2) * size].astype(BF16)


def factor_kernel(kept, arrived, basis, out):
    total = kept[...] + arrived[...].astype(F32)
    dims = (((0,), (1,)), ((), ()))
    high, low = split_bf16(total)
    out[...] = lax.dot_general(high, basis[...], dims, preferred_element_type=F32)
    out[...] += lax.dot_general(low, basis[...], dims, preferred_element_type=F32)


def call(
    kernel, name, out_shape, scratch=(), flops=1_000_000, moved=1_000_000, space=VMEM, last=None
):
    def run(*args):
        spaces = [space] * len(args)
        if last is not None:
            spaces[-1] = last
        args = [
            pltpu.with_memory_space_constraint(x, pltpu.HBM) if where is HBM else x
            for x, where in zip(args, spaces)
        ]
        return pl.pallas_call(
            kernel,
            in_specs=spaces,
            out_specs=jax.tree.map(lambda _: VMEM, out_shape),
            out_shape=out_shape,
            scratch_shapes=scratch,
            cost_estimate=pl.CostEstimate(flops=flops, bytes_accessed=moved, transcendentals=0),
            compiler_params=pltpu.CompilerParams(vmem_limit_bytes=VMEM_LIMIT),
            name=name,
        )(*args)

    return run


def swap(x, mask):
    n = lax.axis_size("trade")
    return lax.ppermute(x, "trade", [(i, i ^ mask) for i in range(n)])


def swaps(x, step):
    masks = [sum(b for k, b in enumerate(step) if j >> k & 1) for j in range(1, 2 ** len(step))]
    parts = {}
    for j in sorted(range(len(masks)), key=lambda j: -bin(masks[j]).count("1")):
        parts[j] = swap(x[j] if isinstance(x, (list, tuple)) else x, masks[j])
    return [parts[j] for j in range(len(masks))]


def ordered(parts, order):
    return [parts[k] for k in order] if len(parts) == len(order) else parts


def sum_over(x, axis):
    n = lax.axis_size(axis)
    total = x
    for shift in range(1, n):
        total = total + lax.ppermute(x, axis, [(i, (i + shift) % n) for i in range(n)])
    return total


def shards(
    factor_paths, tenor_basis, trade_blocks, trade_set, trade_type, notional, strike,
    vol_level, cash_weights, set_threshold, date_weight,
):
    factor_rows, dates, paths = factor_paths.shape
    block_size, tenors = tenor_basis.shape
    rows = dates * paths
    devices = lax.axis_size("trade")
    local_blocks = factor_rows // block_size
    height = local_blocks * tenors
    local_sets = set_threshold.shape[0]
    half_sets = local_sets * devices // 2
    all_rows = height * devices
    trades = trade_set.shape[0]
    shape = jax.ShapeDtypeStruct
    extra_rows = -(-max(1, half_sets // rows) * 2 * dates // 8) * 8
    lane_rows = (trades // LANES, LANES)
    dma = pltpu.SemaphoreType.DMA

    factors = jnp.transpose(factor_paths, (1, 2, 0)).reshape(rows, factor_rows)
    single, group = steps_of(devices)
    arrived = swap(factors, single[0])
    curves, basis, weights, extra = call(
        curve_kernel, "curves",
        [shape((height, rows), BF16), shape((factor_rows, height), BF16),
         shape((dates, local_sets), F32), shape((extra_rows, rows), BF16)],
        [pltpu.VMEM((rows, factor_rows), BF16), pltpu.VMEM((tenors, block_size), BF16), dma((3,))],
        space=HBM,
    )(factors, jnp.transpose(tenor_basis), jnp.transpose(date_weight))
    curves = call(next_curve_kernel, "curves2", shape((2 * height, rows), BF16))(
        curves, arrived, basis
    )
    for mask in single[1:]:
        curves = jnp.concatenate([curves, swap(curves, mask)], axis=0)
    near = [curves] + swaps(curves, group)
    w_fwd, w_disc, onehot, *params = call(
        functools.partial(prep_kernel, devices), "prep",
        [shape((all_rows, trades), BF16)] * 2 + [shape((2 * half_sets, trades), BF16)]
        + [shape(lane_rows, jnp.int32)] + [shape(lane_rows, F32)] * 3 + [shape((1, local_sets), F32)],
        [pltpu.VMEM((2, trades), jnp.int32), pltpu.VMEM(lane_rows, jnp.int32),
         pltpu.VMEM((tenors, trades), F32), dma((8,))],
        flops=400_000_000, moved=8_000_000, space=HBM,
        last=VMEM,
    )(
        trade_blocks, trade_set.reshape(lane_rows), cash_weights, trade_type.reshape(lane_rows),
        notional.reshape(lane_rows), strike.reshape(lane_rows), vol_level.reshape(lane_rows),
        set_threshold[None], curves,
    )
    mine = call(join_kernel, "join", shape((all_rows // 2, rows), BF16))(*near, params[-1])
    partner = swap(mine, 1)
    forward, annuity = call(
        half_price_kernel, "price1", [shape((rows, trades), F32)] * 2,
        flops=400_000_000, moved=4_000_000,
    )(mine, w_fwd, w_disc)
    send, values, forward, annuity = call(
        price_kernel, "price2",
        [shape((half_sets, rows), BF16), shape((rows, trades), BF16),
         shape((rows, trades), F32), shape((rows, trades), F32)],
    )(partner, forward, annuity, w_fwd, w_disc, onehot, *params[:-1])
    keep = call(own_sets_kernel, "ownsets", shape((half_sets, rows), F32))(
        values, onehot, params[-1]
    )
    fwd_scale, ann_scale = call(
        scale_kernel, "scales", [shape((rows, trades), F32)] * 2,
        flops=400_000_000, moved=4_000_000,
    )(forward, annuity, *params[:-1])

    total = call(pair_kernel, "pair", shape((half_sets + extra_rows, rows), BF16))(
        keep, swap(send, 1), extra
    )
    bits = [1 << k for k in range(1, bits_of(devices))]
    steps = [bits[:1]] if len(bits) % 2 else []
    steps += [bits[k : k + 2] for k in range(len(bits) % 2, len(bits), 2)]
    for step in steps:
        parts = [total] + swaps(total, step)
        if step is not steps[-1]:
            total = functools.reduce(jnp.add, [p.astype(F32) for p in parts]).astype(BF16)
    cots_mine, cva = call(
        sets_kernel, "sets",
        [shape((half_sets, rows), BF16), shape((1, local_sets), F32)],
        [pltpu.VMEM((half_sets, rows), F32)],
    )(weights, *ordered(parts, (0, 1, 3, 2)))
    cots_partner = swap(cots_mine, 1)

    send, fwd_cots, ann_cots = call(
        adjoint_kernel, "adjoint",
        [shape((all_rows // 2, rows), BF16)] + [shape((rows, trades), BF16)] * 2,
    )(partner, cots_mine, cots_partner, fwd_scale, ann_scale, w_fwd, w_disc, onehot)
    keep = call(
        keep_kernel, "keep", shape((all_rows // 2, rows), F32),
        flops=200_000_000, moved=4_000_000,
    )(mine, fwd_cots, ann_cots, w_fwd, w_disc)
    arrived = [swap(send, 1)]
    size = all_rows // 2
    for step in [group] + [[mask] for mask in single[::-1]]:
        size >>= len(step)
        shapes = [shape((size, rows), F32)]
        shapes += [shape((size, rows), BF16)] * (2 ** len(step) - 1)
        keep, *sends = call(
            functools.partial(fold_kernel, len(arrived)), f"fold{step[0]}", shapes
        )(keep, *ordered(arrived, (2, 0, 1)))
        arrived = swaps(sends, step)
    factor_cot = call(factor_kernel, "factors", shape((rows, factor_rows), F32))(
        keep, *arrived, basis
    )
    factor_cot = jnp.transpose(factor_cot.reshape(dates, paths, factor_rows), (2, 0, 1))
    netting_cva = sum_over(cva[0], "path") / (paths * lax.axis_size("path"))
    return netting_cva, factor_cot


def solution(mesh):
    return jax.shard_map(
        shards,
        mesh=mesh,
        in_specs=(
            P("trade", None, "path"), P(), P(None, "trade"), P("trade"), P("trade"),
            P("trade"), P("trade"), P("trade"), P(None, "trade"), P("trade"),
            P("trade", None),
        ),
        out_specs=(P("trade"), P("trade", None, "path")),
        check_vma=False,
    )
```

```python
import functools
import math

import jax
import jax.numpy as jnp
from jax import lax
from jax.experimental import pallas as pl
from jax.experimental.pallas import tpu as pltpu
from jax.sharding import PartitionSpec as P

F32 = jnp.float32
BF16 = jnp.bfloat16
NT = (((1,), (1,)), ((), ()))
TN = (((0,), (0,)), ((), ()))
LANES = 128
TILE = 768
VMEM = pl.BlockSpec(memory_space=pltpu.VMEM)
HBM = pl.BlockSpec(memory_space=pltpu.HBM)
VMEM_LIMIT = 8 * 2**20


def log1p_unit(e):
    return jnp.where(e < 1e-4, (1.0 - 0.5 * e) * e, jnp.log(1.0 + e))


def split_bf16(x):
    high = x.astype(BF16)
    return high, (x - high.astype(F32)).astype(BF16)


def iota(shape, dim):
    return lax.broadcasted_iota(jnp.int32, shape, dim)


def block_basis(basis_t, factors, height):
    tenors, size = basis_t.shape
    down = (iota((factors, size), 0) % size == iota((factors, size), 1)).astype(BF16)
    across = (iota((tenors, height), 1) % tenors == iota((tenors, height), 0)).astype(BF16)
    spread = lax.dot_general(down, basis_t, NT, preferred_element_type=F32).astype(BF16)
    tiled = jnp.dot(spread, across, preferred_element_type=F32)
    same = iota((factors, height), 0) // size == iota((factors, height), 1) // tenors
    return jnp.where(same, tiled, 0.0).astype(BF16)


def bits_of(n):
    return int(math.log2(n))


def pair_order(ids, local, devices):
    core = lax.rem(lax.axis_index("trade"), 2)
    owner = jnp.right_shift(ids, bits_of(local))
    side = jnp.bitwise_xor(jnp.bitwise_and(owner, 1), core)
    place = side * (devices // 2) + jnp.right_shift(owner, 1)
    return place * local + jnp.bitwise_and(ids, local - 1)


def steps_of(devices):
    bits = [1 << k for k in range(1, bits_of(devices))]
    return bits[2:][::-1], bits[:2]


def cube_place(owner, devices):
    distance = jnp.bitwise_xor(owner, lax.axis_index("trade"))
    single, group = steps_of(devices)
    place = jnp.zeros_like(distance)
    for k, mask in enumerate(single + group + [1]):
        bit = jnp.bitwise_and(jnp.right_shift(distance, bits_of(mask)), 1)
        place = jnp.bitwise_or(place, jnp.left_shift(bit, k))
    return place


def cube_order(ids, local, devices):
    place = cube_place(jnp.right_shift(ids, bits_of(local)), devices)
    return place * local + jnp.bitwise_and(ids, local - 1)


def fetch(pairs, sems):
    copies = [pltpu.make_async_copy(src, dst, sems.at[k]) for k, (src, dst) in enumerate(pairs)]
    for copy in copies:
        copy.start()
    for copy in copies:
        copy.wait()


def curves_of(basis, factors):
    dims = (((0,), (1,)), ((), ()))
    return lax.dot_general(basis, factors, dims, preferred_element_type=F32).astype(BF16)


def curve_kernel(
    factors_hbm, basis_hbm, weight_hbm, out, basis_out, weight_ref, extra, factors_ref,
    basis_ref, sems,
):
    fetch(
        [(factors_hbm, factors_ref), (basis_hbm, basis_ref), (weight_hbm, weight_ref)], sems
    )
    factors = factors_ref.shape[1]
    tenors, size = basis_ref.shape
    basis = block_basis(basis_ref[...], factors, factors // size * tenors)
    basis_out[...] = basis
    out[...] = curves_of(basis, factors_ref[...])
    dates, sets = weight_ref.shape
    rows, lanes = extra.shape
    first = lax.axis_index("trade") // 2 * sets
    spot = (iota((sets, lanes), 1) == iota((sets, lanes), 0) + lax.rem(first, lanes)).astype(BF16)
    total = jnp.zeros((rows, lanes), F32)
    for k, part in enumerate(split_bf16(weight_ref[...])):
        top = (first // lanes * 2 + k) * dates
        lift = (iota((rows, dates), 0) == iota((rows, dates), 1) + top).astype(BF16)
        lifted = jnp.dot(lift, part, preferred_element_type=F32).astype(BF16)
        total += jnp.dot(lifted, spot, preferred_element_type=F32)
    extra[...] = total.astype(BF16)


def next_curve_kernel(own, arrived, basis, out):
    height = own.shape[0]
    out[:height, :] = own[...]
    out[height:, :] = curves_of(basis[...], arrived[...])


def join_kernel(*refs):
    *parts, _, out = refs
    height = parts[0].shape[0]
    for k, part in enumerate(parts):
        out[k * height : (k + 1) * height, :] = part[...]


def prep_kernel(devices, *refs):
    sources, rest = refs[:8], refs[9:]
    w_fwd, w_low, w_disc, onehot = rest[:4]
    params, (blocks_ref, set_ref, weights_ref, sems) = rest[4:9], rest[9:]
    fetch(list(zip(sources, (blocks_ref, set_ref, weights_ref) + tuple(params))), sems)
    tenors, trades = weights_ref.shape
    height = w_fwd.shape[0]
    blocks = height // tenors
    sets = onehot.shape[0]
    zero = jnp.zeros((tenors, LANES), F32)
    row = iota((16, LANES), 0)
    set_rows = pair_order(set_ref[...], sets // devices, devices)
    block_rows = cube_order(blocks_ref[...], blocks // devices, devices)
    for t in range(0, trades, LANES):
        lanes = slice(t, t + LANES)
        weights = weights_ref[:, lanes]
        low = weights - weights.astype(BF16).astype(F32)
        for k, out in enumerate((w_fwd, w_disc)):
            ids = jnp.broadcast_to(block_rows[k : k + 1, lanes], (tenors, LANES))
            for b in range(blocks):
                here = ids == b
                band = slice(b * tenors, (b + 1) * tenors)
                out[band, lanes] = jnp.where(here, weights, zero).astype(BF16)
                if k == 0:
                    w_low[band, lanes] = jnp.where(here, low, zero).astype(BF16)
        ids = jnp.broadcast_to(set_rows[t // LANES : t // LANES + 1, :], (16, LANES))
        for n in range(0, sets, 16):
            onehot[n : n + 16, lanes] = jnp.where(ids == row + n, 1.0, 0.0).astype(BF16)


def param_row(ref, start, tile):
    return jnp.concatenate(
        [ref[j : j + 1, :] for j in range(start // LANES, (start + tile) // LANES)], axis=1
    )


def half_price_kernel(curves, w_fwd, w_low, w_disc, forward, annuity):
    half, trades = curves.shape[0], w_fwd.shape[1]
    tile = TILE if trades % TILE == 0 else trades
    curve = curves[...]
    discount = jnp.exp(-0.5 * curve.astype(F32)).astype(BF16)
    for t in range(0, trades, tile):
        lanes = slice(t, t + tile)
        forward[:, lanes] = lax.dot_general(
            curve, w_fwd[:half, lanes], TN, preferred_element_type=F32
        ) + lax.dot_general(curve, w_low[:half, lanes], TN, preferred_element_type=F32)
        annuity[:, lanes] = lax.dot_general(
            discount, w_disc[:half, lanes], TN, preferred_element_type=F32
        )


def option_terms(forward, strike, vol):
    moneyness = forward - strike
    return moneyness, jnp.exp(jnp.abs(moneyness) * (-1.0 / vol))


def swaption_payoff(moneyness, e, vol):
    return jnp.maximum(moneyness, 0.0) + vol * log1p_unit(e)


def price_kernel(
    curves, forward_ref, annuity_ref, w_fwd, w_low, w_disc, onehot, kind_ref, notional_ref, strike_ref,
    vol_ref, send, values, forward_out, annuity_out,
):
    near, rows = curves.shape
    trades = w_fwd.shape[1]
    half = send.shape[0]
    tile = TILE if trades % TILE == 0 else trades
    curve = curves[...]
    discount = jnp.exp(-0.5 * curve.astype(F32)).astype(BF16)
    total = jnp.zeros((half, rows), F32)
    for t in range(0, trades, tile):
        lanes = slice(t, t + tile)
        forward = forward_ref[:, lanes] + lax.dot_general(
            curve, w_fwd[near:, lanes], TN, preferred_element_type=F32
        ) + lax.dot_general(curve, w_low[near:, lanes], TN, preferred_element_type=F32)
        annuity = annuity_ref[:, lanes] + lax.dot_general(
            discount, w_disc[near:, lanes], TN, preferred_element_type=F32
        )
        forward_out[:, lanes] = forward
        annuity_out[:, lanes] = annuity
        vol = param_row(vol_ref, t, tile)
        option = jnp.broadcast_to(param_row(kind_ref, t, tile) == 1, (rows, tile))
        moneyness, e = option_terms(forward, param_row(strike_ref, t, tile), vol)
        payoff = jnp.where(option, swaption_payoff(moneyness, e, vol), moneyness)
        value = (param_row(notional_ref, t, tile) * annuity * payoff).astype(BF16)
        values[:, lanes] = value
        total += lax.dot_general(onehot[half:, lanes], value, NT, preferred_element_type=F32)
    send[...] = total.astype(BF16)


def own_sets_kernel(values, onehot, threshold_ref, keep):
    half = keep.shape[0]
    keep[...] = lax.dot_general(onehot[:half, :], values[...], NT, preferred_element_type=F32)
    sets = threshold_ref.shape[1]
    chip = lax.axis_index("trade") // 2
    own = pl.ds(pl.multiple_of(chip * sets, sets), sets)
    square = iota((sets, sets), 0) == iota((sets, sets), 1)
    column = jnp.sum(jnp.where(square, threshold_ref[...], 0.0), axis=1, keepdims=True)
    keep[own, :] = keep[own, :] - column


def scale_kernel(
    forward_ref, annuity_ref, kind_ref, notional_ref, strike_ref, vol_ref, fwd_scale, ann_scale
):
    rows, trades = forward_ref.shape
    tile = TILE if trades % TILE == 0 else trades
    for t in range(0, trades, tile):
        lanes = slice(t, t + tile)
        vol = param_row(vol_ref, t, tile)
        notional = param_row(notional_ref, t, tile)
        option = jnp.broadcast_to(param_row(kind_ref, t, tile) == 1, (rows, tile))
        moneyness, e = option_terms(forward_ref[:, lanes], param_row(strike_ref, t, tile), vol)
        payoff = jnp.where(option, swaption_payoff(moneyness, e, vol), moneyness)
        sigmoid = jnp.where(moneyness >= 0.0, 1.0, e) / (1.0 + e)
        fwd_scale[:, lanes] = notional * annuity_ref[:, lanes] * jnp.where(option, sigmoid, 1.0)
        ann_scale[:, lanes] = notional * payoff


def pair_kernel(keep, arrived, extra, out):
    half = keep.shape[0]
    out[:half, :] = (keep[...] + arrived[...].astype(F32)).astype(BF16)
    out[half:, :] = extra[...]


def sets_kernel(weight_ref, *refs):
    parts, (cots, cva, excess_ref) = refs[:-3], refs[-3:]
    dates, sets = weight_ref.shape
    half, rows = excess_ref.shape
    me = lax.axis_index("trade")
    total = parts[0][...].astype(F32)
    for part in parts[1:]:
        total += part[...].astype(F32)
    excess = total[:half]
    excess_ref[...] = excess
    span = rows // dates
    pieces = total[half:].astype(BF16)
    line = iota((pieces.shape[0], rows), 0)
    weights = []
    for k in range(max(1, half // rows)):
        spread = (line % dates == iota(line.shape, 1) // span) & (line // (2 * dates) == k)
        weights.append(
            lax.dot_general(pieces, spread.astype(BF16), TN, preferred_element_type=F32)
        )
    weights = jnp.concatenate(weights, axis=0)[:half]
    e = jnp.exp(-jnp.abs(excess))
    sigmoid = jnp.where(excess >= 0.0, 1.0, e) / (1.0 + e)
    cots[...] = (weights * sigmoid).astype(BF16)
    chip = me // 2
    own = excess_ref[pl.ds(pl.multiple_of(chip * sets, sets), sets), :]
    exposure = jnp.maximum(own, 0.0) + log1p_unit(jnp.exp(-jnp.abs(own)))
    square = iota((sets, sets), 0) == iota((sets, sets), 1)
    date = iota((sets, rows), 1) // span
    column = jnp.zeros((sets, 1), F32)
    for d in range(dates):
        weight = jnp.where(square, weight_ref[d : d + 1, :], 0.0)
        weight = jnp.sum(weight, axis=1, keepdims=True)
        column += weight * jnp.sum(jnp.where(date == d, exposure, 0.0), axis=1, keepdims=True)
    cva[...] = jnp.sum(jnp.where(square, column, 0.0), axis=0, keepdims=True)


def half_cot(side, curves, fwd_cots, ann_cots, w_fwd, w_disc):
    half, trades = curves.shape[0], w_fwd.shape[1]
    tile = TILE if trades % TILE == 0 else trades
    band = slice(side * half, (side + 1) * half)
    from_fwd = from_disc = 0.0
    for t in range(0, trades, tile):
        lanes = slice(t, t + tile)
        from_fwd += lax.dot_general(
            w_fwd[band, lanes], fwd_cots[:, lanes], NT, preferred_element_type=F32
        )
        from_disc += lax.dot_general(
            w_disc[band, lanes], ann_cots[:, lanes], NT, preferred_element_type=F32
        )
    return from_fwd - 0.5 * jnp.exp(-0.5 * curves[...].astype(F32)) * from_disc


def adjoint_kernel(
    partner, cots_mine, cots_partner, fwd_scale, ann_scale, w_fwd, w_disc, onehot, send,
    fwd_cots, ann_cots,
):
    trades = fwd_scale.shape[1]
    tile = TILE if trades % TILE == 0 else trades
    cots = jnp.concatenate([cots_mine[...], cots_partner[...]], axis=0)
    for t in range(0, trades, tile):
        lanes = slice(t, t + tile)
        trade_cot = lax.dot_general(cots, onehot[:, lanes], TN, preferred_element_type=F32)
        fwd_cots[:, lanes] = (trade_cot * fwd_scale[:, lanes]).astype(BF16)
        ann_cots[:, lanes] = (trade_cot * ann_scale[:, lanes]).astype(BF16)
    send[...] = half_cot(1, partner, fwd_cots, ann_cots, w_fwd, w_disc).astype(BF16)


def keep_kernel(mine, fwd_cots, ann_cots, w_fwd, w_disc, keep):
    keep[...] = half_cot(0, mine, fwd_cots, ann_cots, w_fwd, w_disc)


def fold_kernel(count, kept, *refs):
    arrived, (keep, *sends) = refs[:count], refs[count:]
    total = kept[...]
    for part in arrived:
        total += part[...].astype(F32)
    size = keep.shape[0]
    keep[...] = total[:size]
    for k, send in enumerate(sends):
        send[...] = total[(k + 1) * size : (k + 2) * size].astype(BF16)


def factor_kernel(kept, arrived, basis, out):
    total = kept[...] + arrived[...].astype(F32)
    dims = (((0,), (1,)), ((), ()))
    high, low = split_bf16(total)
    out[...] = lax.dot_general(high, basis[...], dims, preferred_element_type=F32)
    out[...] += lax.dot_general(low, basis[...], dims, preferred_element_type=F32)


def call(
    kernel, name, out_shape, scratch=(), flops=1_000_000, moved=1_000_000, space=VMEM, last=None
):
    def run(*args):
        spaces = [space] * len(args)
        if last is not None:
            spaces[-1] = last
        args = [
            pltpu.with_memory_space_constraint(x, pltpu.HBM) if where is HBM else x
            for x, where in zip(args, spaces)
        ]
        return pl.pallas_call(
            kernel,
            in_specs=spaces,
            out_specs=jax.tree.map(lambda _: VMEM, out_shape),
            out_shape=out_shape,
            scratch_shapes=scratch,
            cost_estimate=pl.CostEstimate(flops=flops, bytes_accessed=moved, transcendentals=0),
            compiler_params=pltpu.CompilerParams(vmem_limit_bytes=VMEM_LIMIT),
            name=name,
        )(*args)

    return run


def swap(x, mask):
    n = lax.axis_size("trade")
    return lax.ppermute(x, "trade", [(i, i ^ mask) for i in range(n)])


def swaps(x, step):
    masks = [sum(b for k, b in enumerate(step) if j >> k & 1) for j in range(1, 2 ** len(step))]
    parts = {}
    for j in sorted(range(len(masks)), key=lambda j: -bin(masks[j]).count("1")):
        parts[j] = swap(x[j] if isinstance(x, (list, tuple)) else x, masks[j])
    return [parts[j] for j in range(len(masks))]


def ordered(parts, order):
    return [parts[k] for k in order] if len(parts) == len(order) else parts


def sum_over(x, axis):
    n = lax.axis_size(axis)
    total = x
    for shift in range(1, n):
        total = total + lax.ppermute(x, axis, [(i, (i + shift) % n) for i in range(n)])
    return total


def shards(
    factor_paths, tenor_basis, trade_blocks, trade_set, trade_type, notional, strike,
    vol_level, cash_weights, set_threshold, date_weight,
):
    factor_rows, dates, paths = factor_paths.shape
    block_size, tenors = tenor_basis.shape
    rows = dates * paths
    devices = lax.axis_size("trade")
    local_blocks = factor_rows // block_size
    height = local_blocks * tenors
    local_sets = set_threshold.shape[0]
    half_sets = local_sets * devices // 2
    all_rows = height * devices
    trades = trade_set.shape[0]
    shape = jax.ShapeDtypeStruct
    extra_rows = -(-max(1, half_sets // rows) * 2 * dates // 8) * 8
    lane_rows = (trades // LANES, LANES)
    dma = pltpu.SemaphoreType.DMA

    factors = jnp.transpose(factor_paths, (1, 2, 0)).reshape(rows, factor_rows)
    single, group = steps_of(devices)
    arrived = swap(factors, single[0])
    curves, basis, weights, extra = call(
        curve_kernel, "curves",
        [shape((height, rows), BF16), shape((factor_rows, height), BF16),
         shape((dates, local_sets), F32), shape((extra_rows, rows), BF16)],
        [pltpu.VMEM((rows, factor_rows), BF16), pltpu.VMEM((tenors, block_size), BF16), dma((3,))],
        space=HBM,
    )(factors, jnp.transpose(tenor_basis), jnp.transpose(date_weight))
    curves = call(next_curve_kernel, "curves2", shape((2 * height, rows), BF16))(
        curves, arrived, basis
    )
    for mask in single[1:]:
        curves = jnp.concatenate([curves, swap(curves, mask)], axis=0)
    near = [curves] + swaps(curves, group)
    w_fwd, w_low, w_disc, onehot, *params = call(
        functools.partial(prep_kernel, devices), "prep",
        [shape((all_rows, trades), BF16)] * 3 + [shape((2 * half_sets, trades), BF16)]
        + [shape(lane_rows, jnp.int32)] + [shape(lane_rows, F32)] * 3 + [shape((1, local_sets), F32)],
        [pltpu.VMEM((2, trades), jnp.int32), pltpu.VMEM(lane_rows, jnp.int32),
         pltpu.VMEM((tenors, trades), F32), dma((8,))],
        flops=400_000_000, moved=8_000_000, space=HBM,
        last=VMEM,
    )(
        trade_blocks, trade_set.reshape(lane_rows), cash_weights, trade_type.reshape(lane_rows),
        notional.reshape(lane_rows), strike.reshape(lane_rows), vol_level.reshape(lane_rows),
        set_threshold[None], curves,
    )
    mine = call(join_kernel, "join", shape((all_rows // 2, rows), BF16))(*near, params[-1])
    partner = swap(mine, 1)
    forward, annuity = call(
        half_price_kernel, "price1", [shape((rows, trades), F32)] * 2,
        flops=400_000_000, moved=4_000_000,
    )(mine, w_fwd, w_low, w_disc)
    send, values, forward, annuity = call(
        price_kernel, "price2",
        [shape((half_sets, rows), BF16), shape((rows, trades), BF16),
         shape((rows, trades), F32), shape((rows, trades), F32)],
    )(partner, forward, annuity, w_fwd, w_low, w_disc, onehot, *params[:-1])
    keep = call(own_sets_kernel, "ownsets", shape((half_sets, rows), F32))(
        values, onehot, params[-1]
    )
    fwd_scale, ann_scale = call(
        scale_kernel, "scales", [shape((rows, trades), F32)] * 2,
        flops=400_000_000, moved=4_000_000,
    )(forward, annuity, *params[:-1])

    total = call(pair_kernel, "pair", shape((half_sets + extra_rows, rows), BF16))(
        keep, swap(send, 1), extra
    )
    bits = [1 << k for k in range(1, bits_of(devices))]
    steps = [bits[:1]] if len(bits) % 2 else []
    steps += [bits[k : k + 2] for k in range(len(bits) % 2, len(bits), 2)]
    for step in steps:
        parts = [total] + swaps(total, step)
        if step is not steps[-1]:
            total = functools.reduce(jnp.add, [p.astype(F32) for p in parts]).astype(BF16)
    cots_mine, cva = call(
        sets_kernel, "sets",
        [shape((half_sets, rows), BF16), shape((1, local_sets), F32)],
        [pltpu.VMEM((half_sets, rows), F32)],
    )(weights, *ordered(parts, (0, 1, 3, 2)))
    cots_partner = swap(cots_mine, 1)

    send, fwd_cots, ann_cots = call(
        adjoint_kernel, "adjoint",
        [shape((all_rows // 2, rows), BF16)] + [shape((rows, trades), BF16)] * 2,
    )(partner, cots_mine, cots_partner, fwd_scale, ann_scale, w_fwd, w_disc, onehot)
    keep = call(
        keep_kernel, "keep", shape((all_rows // 2, rows), F32),
        flops=200_000_000, moved=4_000_000,
    )(mine, fwd_cots, ann_cots, w_fwd, w_disc)
    arrived = [swap(send, 1)]
    size = all_rows // 2
    for step in [group] + [[mask] for mask in single[::-1]]:
        size >>= len(step)
        shapes = [shape((size, rows), F32)]
        shapes += [shape((size, rows), BF16)] * (2 ** len(step) - 1)
        keep, *sends = call(
            functools.partial(fold_kernel, len(arrived)), f"fold{step[0]}", shapes
        )(keep, *ordered(arrived, (2, 0, 1)))
        arrived = swaps(sends, step)
    factor_cot = call(factor_kernel, "factors", shape((rows, factor_rows), F32))(
        keep, *arrived, basis
    )
    factor_cot = jnp.transpose(factor_cot.reshape(dates, paths, factor_rows), (2, 0, 1))
    netting_cva = sum_over(cva[0], "path") / (paths * lax.axis_size("path"))
    return netting_cva, factor_cot


def solution(mesh):
    return jax.shard_map(
        shards,
        mesh=mesh,
        in_specs=(
            P("trade", None, "path"), P(), P(None, "trade"), P("trade"), P("trade"),
            P("trade"), P("trade"), P("trade"), P(None, "trade"), P("trade"),
            P("trade", None),
        ),
        out_specs=(P("trade"), P("trade", None, "path")),
        check_vma=False,
    )
```

```python
import functools
import math

import jax
import jax.numpy as jnp
from jax import lax
from jax.experimental import pallas as pl
from jax.experimental.pallas import tpu as pltpu
from jax.sharding import PartitionSpec as P

F32 = jnp.float32
BF16 = jnp.bfloat16
NT = (((1,), (1,)), ((), ()))
TN = (((0,), (0,)), ((), ()))
LANES = 128
TILE = 1536
VMEM = pl.BlockSpec(memory_space=pltpu.VMEM)
HBM = pl.BlockSpec(memory_space=pltpu.HBM)
VMEM_LIMIT = 8 * 2**20


def log1p_unit(e):
    return jnp.where(e < 1e-4, (1.0 - 0.5 * e) * e, jnp.log(1.0 + e))


def split_bf16(x):
    high = x.astype(BF16)
    return high, (x - high.astype(F32)).astype(BF16)


def iota(shape, dim):
    return lax.broadcasted_iota(jnp.int32, shape, dim)


def block_basis(basis_t, factors, height):
    tenors, size = basis_t.shape
    down = (iota((factors, size), 0) % size == iota((factors, size), 1)).astype(BF16)
    across = (iota((tenors, height), 1) % tenors == iota((tenors, height), 0)).astype(BF16)
    spread = lax.dot_general(down, basis_t, NT, preferred_element_type=F32).astype(BF16)
    tiled = jnp.dot(spread, across, preferred_element_type=F32)
    same = iota((factors, height), 0) // size == iota((factors, height), 1) // tenors
    return jnp.where(same, tiled, 0.0).astype(BF16)


def bits_of(n):
    return int(math.log2(n))


def pair_order(ids, local, devices):
    core = lax.rem(lax.axis_index("trade"), 2)
    owner = jnp.right_shift(ids, bits_of(local))
    side = jnp.bitwise_xor(jnp.bitwise_and(owner, 1), core)
    place = side * (devices // 2) + jnp.right_shift(owner, 1)
    return place * local + jnp.bitwise_and(ids, local - 1)


def steps_of(devices):
    bits = [1 << k for k in range(1, bits_of(devices))]
    return bits[2:][::-1], bits[:2]


def cube_place(owner, devices):
    distance = jnp.bitwise_xor(owner, lax.axis_index("trade"))
    single, group = steps_of(devices)
    place = jnp.zeros_like(distance)
    for k, mask in enumerate(single + group + [1]):
        bit = jnp.bitwise_and(jnp.right_shift(distance, bits_of(mask)), 1)
        place = jnp.bitwise_or(place, jnp.left_shift(bit, k))
    return place


def cube_order(ids, local, devices):
    place = cube_place(jnp.right_shift(ids, bits_of(local)), devices)
    return place * local + jnp.bitwise_and(ids, local - 1)


def fetch(pairs, sems):
    copies = [pltpu.make_async_copy(src, dst, sems.at[k]) for k, (src, dst) in enumerate(pairs)]
    for copy in copies:
        copy.start()
    for copy in copies:
        copy.wait()


def curves_of(basis, factors):
    dims = (((0,), (1,)), ((), ()))
    return lax.dot_general(basis, factors, dims, preferred_element_type=F32).astype(BF16)


def curve_kernel(
    factors_hbm, basis_hbm, weight_hbm, out, basis_out, weight_ref, extra, factors_ref,
    basis_ref, sems,
):
    fetch(
        [(factors_hbm, factors_ref), (basis_hbm, basis_ref), (weight_hbm, weight_ref)], sems
    )
    factors = factors_ref.shape[1]
    tenors, size = basis_ref.shape
    basis = block_basis(basis_ref[...], factors, factors // size * tenors)
    basis_out[...] = basis
    out[...] = curves_of(basis, factors_ref[...])
    dates, sets = weight_ref.shape
    rows, lanes = extra.shape
    first = lax.axis_index("trade") // 2 * sets
    spot = (iota((sets, lanes), 1) == iota((sets, lanes), 0) + lax.rem(first, lanes)).astype(BF16)
    total = jnp.zeros((rows, lanes), F32)
    for k, part in enumerate(split_bf16(weight_ref[...])):
        top = (first // lanes * 2 + k) * dates
        lift = (iota((rows, dates), 0) == iota((rows, dates), 1) + top).astype(BF16)
        lifted = jnp.dot(lift, part, preferred_element_type=F32).astype(BF16)
        total += jnp.dot(lifted, spot, preferred_element_type=F32)
    extra[...] = total.astype(BF16)


def next_curve_kernel(own, arrived, basis, out):
    height = own.shape[0]
    out[:height, :] = own[...]
    out[height:, :] = curves_of(basis[...], arrived[...])


def join_kernel(*refs):
    *parts, _, out = refs
    height = parts[0].shape[0]
    for k, part in enumerate(parts):
        out[k * height : (k + 1) * height, :] = part[...]


def prep_kernel(devices, *refs):
    sources, rest = refs[:8], refs[9:]
    w_fwd, w_low, w_disc, onehot = rest[:4]
    params, (blocks_ref, set_ref, weights_ref, sems) = rest[4:9], rest[9:]
    fetch(list(zip(sources, (blocks_ref, set_ref, weights_ref) + tuple(params))), sems)
    tenors, trades = weights_ref.shape
    height = w_fwd.shape[0]
    blocks = height // tenors
    sets = onehot.shape[0]
    zero = jnp.zeros((tenors, LANES), F32)
    row = iota((16, LANES), 0)
    set_rows = pair_order(set_ref[...], sets // devices, devices)
    block_rows = cube_order(blocks_ref[...], blocks // devices, devices)
    for t in range(0, trades, LANES):
        lanes = slice(t, t + LANES)
        weights = weights_ref[:, lanes]
        low = weights - weights.astype(BF16).astype(F32)
        for k, out in enumerate((w_fwd, w_disc)):
            ids = jnp.broadcast_to(block_rows[k : k + 1, lanes], (tenors, LANES))
            for b in range(blocks):
                here = ids == b
                band = slice(b * tenors, (b + 1) * tenors)
                out[band, lanes] = jnp.where(here, weights, zero).astype(BF16)
                if k == 0:
                    w_low[band, lanes] = jnp.where(here, low, zero).astype(BF16)
        ids = jnp.broadcast_to(set_rows[t // LANES : t // LANES + 1, :], (16, LANES))
        for n in range(0, sets, 16):
            onehot[n : n + 16, lanes] = jnp.where(ids == row + n, 1.0, 0.0).astype(BF16)


def param_row(ref, start, tile):
    return jnp.concatenate(
        [ref[j : j + 1, :] for j in range(start // LANES, (start + tile) // LANES)], axis=1
    )


def half_price_kernel(curves, w_fwd, w_low, w_disc, forward, annuity):
    half, trades = curves.shape[0], w_fwd.shape[1]
    tile = TILE if trades % TILE == 0 else trades
    curve = curves[...]
    discount = jnp.exp(-0.5 * curve.astype(F32)).astype(BF16)
    for t in range(0, trades, tile):
        lanes = slice(t, t + tile)
        forward[:, lanes] = lax.dot_general(
            curve, w_fwd[:half, lanes], TN, preferred_element_type=F32
        ) + lax.dot_general(curve, w_low[:half, lanes], TN, preferred_element_type=F32)
        annuity[:, lanes] = lax.dot_general(
            discount, w_disc[:half, lanes], TN, preferred_element_type=F32
        )


def option_terms(forward, strike, vol):
    moneyness = forward - strike
    return moneyness, jnp.exp(jnp.abs(moneyness) * (-1.0 / vol))


def swaption_payoff(moneyness, e, vol):
    return jnp.maximum(moneyness, 0.0) + vol * log1p_unit(e)


def price_kernel(
    curves, forward_ref, annuity_ref, w_fwd, w_low, w_disc, onehot, kind_ref, notional_ref, strike_ref,
    vol_ref, send, values, forward_out, annuity_out,
):
    near, rows = curves.shape
    trades = w_fwd.shape[1]
    half = send.shape[0]
    tile = TILE if trades % TILE == 0 else trades
    curve = curves[...]
    discount = jnp.exp(-0.5 * curve.astype(F32)).astype(BF16)
    total = jnp.zeros((half, rows), F32)
    for t in range(0, trades, tile):
        lanes = slice(t, t + tile)
        forward = forward_ref[:, lanes] + lax.dot_general(
            curve, w_fwd[near:, lanes], TN, preferred_element_type=F32
        ) + lax.dot_general(curve, w_low[near:, lanes], TN, preferred_element_type=F32)
        annuity = annuity_ref[:, lanes] + lax.dot_general(
            discount, w_disc[near:, lanes], TN, preferred_element_type=F32
        )
        forward_out[:, lanes] = forward
        annuity_out[:, lanes] = annuity
        vol = param_row(vol_ref, t, tile)
        option = jnp.broadcast_to(param_row(kind_ref, t, tile) == 1, (rows, tile))
        moneyness, e = option_terms(forward, param_row(strike_ref, t, tile), vol)
        payoff = jnp.where(option, swaption_payoff(moneyness, e, vol), moneyness)
        value = (param_row(notional_ref, t, tile) * annuity * payoff).astype(BF16)
        values[:, lanes] = value
        total += lax.dot_general(onehot[half:, lanes], value, NT, preferred_element_type=F32)
    send[...] = total.astype(BF16)


def own_sets_kernel(values, onehot, threshold_ref, keep):
    half = keep.shape[0]
    keep[...] = lax.dot_general(onehot[:half, :], values[...], NT, preferred_element_type=F32)
    sets = threshold_ref.shape[1]
    chip = lax.axis_index("trade") // 2
    own = pl.ds(pl.multiple_of(chip * sets, sets), sets)
    square = iota((sets, sets), 0) == iota((sets, sets), 1)
    column = jnp.sum(jnp.where(square, threshold_ref[...], 0.0), axis=1, keepdims=True)
    keep[own, :] = keep[own, :] - column


def scale_kernel(
    forward_ref, annuity_ref, kind_ref, notional_ref, strike_ref, vol_ref, fwd_scale, ann_scale
):
    rows, trades = forward_ref.shape
    tile = TILE if trades % TILE == 0 else trades
    for t in range(0, trades, tile):
        lanes = slice(t, t + tile)
        vol = param_row(vol_ref, t, tile)
        notional = param_row(notional_ref, t, tile)
        option = jnp.broadcast_to(param_row(kind_ref, t, tile) == 1, (rows, tile))
        moneyness, e = option_terms(forward_ref[:, lanes], param_row(strike_ref, t, tile), vol)
        payoff = jnp.where(option, swaption_payoff(moneyness, e, vol), moneyness)
        sigmoid = jnp.where(moneyness >= 0.0, 1.0, e) / (1.0 + e)
        fwd_scale[:, lanes] = notional * annuity_ref[:, lanes] * jnp.where(option, sigmoid, 1.0)
        ann_scale[:, lanes] = notional * payoff


def pair_kernel(keep, arrived, extra, out):
    half = keep.shape[0]
    out[:half, :] = (keep[...] + arrived[...].astype(F32)).astype(BF16)
    out[half:, :] = extra[...]


def sets_kernel(weight_ref, *refs):
    parts, (cots, cva, excess_ref) = refs[:-3], refs[-3:]
    dates, sets = weight_ref.shape
    half, rows = excess_ref.shape
    me = lax.axis_index("trade")
    total = parts[0][...].astype(F32)
    for part in parts[1:]:
        total += part[...].astype(F32)
    excess = total[:half]
    excess_ref[...] = excess
    span = rows // dates
    pieces = total[half:].astype(BF16)
    line = iota((pieces.shape[0], rows), 0)
    weights = []
    for k in range(max(1, half // rows)):
        spread = (line % dates == iota(line.shape, 1) // span) & (line // (2 * dates) == k)
        weights.append(
            lax.dot_general(pieces, spread.astype(BF16), TN, preferred_element_type=F32)
        )
    weights = jnp.concatenate(weights, axis=0)[:half]
    e = jnp.exp(-jnp.abs(excess))
    sigmoid = jnp.where(excess >= 0.0, 1.0, e) / (1.0 + e)
    cots[...] = (weights * sigmoid).astype(BF16)
    chip = me // 2
    own = excess_ref[pl.ds(pl.multiple_of(chip * sets, sets), sets), :]
    exposure = jnp.maximum(own, 0.0) + log1p_unit(jnp.exp(-jnp.abs(own)))
    square = iota((sets, sets), 0) == iota((sets, sets), 1)
    date = iota((sets, rows), 1) // span
    column = jnp.zeros((sets, 1), F32)
    for d in range(dates):
        weight = jnp.where(square, weight_ref[d : d + 1, :], 0.0)
        weight = jnp.sum(weight, axis=1, keepdims=True)
        column += weight * jnp.sum(jnp.where(date == d, exposure, 0.0), axis=1, keepdims=True)
    cva[...] = jnp.sum(jnp.where(square, column, 0.0), axis=0, keepdims=True)


def half_cot(side, curves, fwd_cots, ann_cots, w_fwd, w_disc):
    half, trades = curves.shape[0], w_fwd.shape[1]
    tile = TILE if trades % TILE == 0 else trades
    band = slice(side * half, (side + 1) * half)
    from_fwd = from_disc = 0.0
    for t in range(0, trades, tile):
        lanes = slice(t, t + tile)
        from_fwd += lax.dot_general(
            w_fwd[band, lanes], fwd_cots[:, lanes], NT, preferred_element_type=F32
        )
        from_disc += lax.dot_general(
            w_disc[band, lanes], ann_cots[:, lanes], NT, preferred_element_type=F32
        )
    return from_fwd - 0.5 * jnp.exp(-0.5 * curves[...].astype(F32)) * from_disc


def adjoint_kernel(
    partner, cots_mine, cots_partner, fwd_scale, ann_scale, w_fwd, w_disc, onehot, send,
    fwd_cots, ann_cots,
):
    trades = fwd_scale.shape[1]
    tile = TILE if trades % TILE == 0 else trades
    cots = jnp.concatenate([cots_mine[...], cots_partner[...]], axis=0)
    for t in range(0, trades, tile):
        lanes = slice(t, t + tile)
        trade_cot = lax.dot_general(cots, onehot[:, lanes], TN, preferred_element_type=F32)
        fwd_cots[:, lanes] = (trade_cot * fwd_scale[:, lanes]).astype(BF16)
        ann_cots[:, lanes] = (trade_cot * ann_scale[:, lanes]).astype(BF16)
    send[...] = half_cot(1, partner, fwd_cots, ann_cots, w_fwd, w_disc).astype(BF16)


def keep_kernel(mine, fwd_cots, ann_cots, w_fwd, w_disc, keep):
    keep[...] = half_cot(0, mine, fwd_cots, ann_cots, w_fwd, w_disc)


def fold_kernel(count, kept, *refs):
    arrived, (keep, *sends) = refs[:count], refs[count:]
    total = kept[...]
    for part in arrived:
        total += part[...].astype(F32)
    size = keep.shape[0]
    keep[...] = total[:size]
    for k, send in enumerate(sends):
        send[...] = total[(k + 1) * size : (k + 2) * size].astype(BF16)


def factor_kernel(kept, arrived, basis, out):
    total = kept[...] + arrived[...].astype(F32)
    dims = (((0,), (1,)), ((), ()))
    high, low = split_bf16(total)
    out[...] = lax.dot_general(high, basis[...], dims, preferred_element_type=F32)
    out[...] += lax.dot_general(low, basis[...], dims, preferred_element_type=F32)


def call(
    kernel, name, out_shape, scratch=(), flops=1_000_000, moved=1_000_000, space=VMEM, last=None
):
    def run(*args):
        spaces = [space] * len(args)
        if last is not None:
            spaces[-1] = last
        args = [
            pltpu.with_memory_space_constraint(x, pltpu.HBM) if where is HBM else x
            for x, where in zip(args, spaces)
        ]
        return pl.pallas_call(
            kernel,
            in_specs=spaces,
            out_specs=jax.tree.map(lambda _: VMEM, out_shape),
            out_shape=out_shape,
            scratch_shapes=scratch,
            cost_estimate=pl.CostEstimate(flops=flops, bytes_accessed=moved, transcendentals=0),
            compiler_params=pltpu.CompilerParams(vmem_limit_bytes=VMEM_LIMIT),
            name=name,
        )(*args)

    return run


def swap(x, mask):
    n = lax.axis_size("trade")
    return lax.ppermute(x, "trade", [(i, i ^ mask) for i in range(n)])


def swaps(x, step):
    masks = [sum(b for k, b in enumerate(step) if j >> k & 1) for j in range(1, 2 ** len(step))]
    parts = {}
    for j in sorted(range(len(masks)), key=lambda j: -bin(masks[j]).count("1")):
        parts[j] = swap(x[j] if isinstance(x, (list, tuple)) else x, masks[j])
    return [parts[j] for j in range(len(masks))]


def ordered(parts, order):
    return [parts[k] for k in order] if len(parts) == len(order) else parts


def sum_over(x, axis):
    n = lax.axis_size(axis)
    total = x
    for shift in range(1, n):
        total = total + lax.ppermute(x, axis, [(i, (i + shift) % n) for i in range(n)])
    return total


def shards(
    factor_paths, tenor_basis, trade_blocks, trade_set, trade_type, notional, strike,
    vol_level, cash_weights, set_threshold, date_weight,
):
    factor_rows, dates, paths = factor_paths.shape
    block_size, tenors = tenor_basis.shape
    rows = dates * paths
    devices = lax.axis_size("trade")
    local_blocks = factor_rows // block_size
    height = local_blocks * tenors
    local_sets = set_threshold.shape[0]
    half_sets = local_sets * devices // 2
    all_rows = height * devices
    trades = trade_set.shape[0]
    shape = jax.ShapeDtypeStruct
    extra_rows = -(-max(1, half_sets // rows) * 2 * dates // 8) * 8
    lane_rows = (trades // LANES, LANES)
    dma = pltpu.SemaphoreType.DMA

    factors = jnp.transpose(factor_paths, (1, 2, 0)).reshape(rows, factor_rows)
    single, group = steps_of(devices)
    arrived = swap(factors, single[0])
    curves, basis, weights, extra = call(
        curve_kernel, "curves",
        [shape((height, rows), BF16), shape((factor_rows, height), BF16),
         shape((dates, local_sets), F32), shape((extra_rows, rows), BF16)],
        [pltpu.VMEM((rows, factor_rows), BF16), pltpu.VMEM((tenors, block_size), BF16), dma((3,))],
        space=HBM,
    )(factors, jnp.transpose(tenor_basis), jnp.transpose(date_weight))
    curves = call(next_curve_kernel, "curves2", shape((2 * height, rows), BF16))(
        curves, arrived, basis
    )
    for mask in single[1:]:
        curves = jnp.concatenate([curves, swap(curves, mask)], axis=0)
    near = [curves] + swaps(curves, group)
    w_fwd, w_low, w_disc, onehot, *params = call(
        functools.partial(prep_kernel, devices), "prep",
        [shape((all_rows, trades), BF16)] * 3 + [shape((2 * half_sets, trades), BF16)]
        + [shape(lane_rows, jnp.int32)] + [shape(lane_rows, F32)] * 3 + [shape((1, local_sets), F32)],
        [pltpu.VMEM((2, trades), jnp.int32), pltpu.VMEM(lane_rows, jnp.int32),
         pltpu.VMEM((tenors, trades), F32), dma((8,))],
        flops=400_000_000, moved=8_000_000, space=HBM,
        last=VMEM,
    )(
        trade_blocks, trade_set.reshape(lane_rows), cash_weights, trade_type.reshape(lane_rows),
        notional.reshape(lane_rows), strike.reshape(lane_rows), vol_level.reshape(lane_rows),
        set_threshold[None], curves,
    )
    mine = call(join_kernel, "join", shape((all_rows // 2, rows), BF16))(*near, params[-1])
    partner = swap(mine, 1)
    forward, annuity = call(
        half_price_kernel, "price1", [shape((rows, trades), F32)] * 2,
        flops=400_000_000, moved=4_000_000,
    )(mine, w_fwd, w_low, w_disc)
    send, values, forward, annuity = call(
        price_kernel, "price2",
        [shape((half_sets, rows), BF16), shape((rows, trades), BF16),
         shape((rows, trades), F32), shape((rows, trades), F32)],
    )(partner, forward, annuity, w_fwd, w_low, w_disc, onehot, *params[:-1])
    keep = call(own_sets_kernel, "ownsets", shape((half_sets, rows), F32))(
        values, onehot, params[-1]
    )
    fwd_scale, ann_scale = call(
        scale_kernel, "scales", [shape((rows, trades), F32)] * 2,
        flops=400_000_000, moved=4_000_000,
    )(forward, annuity, *params[:-1])

    total = call(pair_kernel, "pair", shape((half_sets + extra_rows, rows), BF16))(
        keep, swap(send, 1), extra
    )
    bits = [1 << k for k in range(1, bits_of(devices))]
    steps = [bits[:1]] if len(bits) % 2 else []
    steps += [bits[k : k + 2] for k in range(len(bits) % 2, len(bits), 2)]
    for step in steps:
        parts = [total] + swaps(total, step)
        if step is not steps[-1]:
            total = functools.reduce(jnp.add, [p.astype(F32) for p in parts]).astype(BF16)
    cots_mine, cva = call(
        sets_kernel, "sets",
        [shape((half_sets, rows), BF16), shape((1, local_sets), F32)],
        [pltpu.VMEM((half_sets, rows), F32)],
    )(weights, *ordered(parts, (0, 1, 3, 2)))
    cots_partner = swap(cots_mine, 1)

    send, fwd_cots, ann_cots = call(
        adjoint_kernel, "adjoint",
        [shape((all_rows // 2, rows), BF16)] + [shape((rows, trades), BF16)] * 2,
    )(partner, cots_mine, cots_partner, fwd_scale, ann_scale, w_fwd, w_disc, onehot)
    keep = call(
        keep_kernel, "keep", shape((all_rows // 2, rows), F32),
        flops=200_000_000, moved=4_000_000,
    )(mine, fwd_cots, ann_cots, w_fwd, w_disc)
    arrived = [swap(send, 1)]
    size = all_rows // 2
    for step in [group] + [[mask] for mask in single[::-1]]:
        size >>= len(step)
        shapes = [shape((size, rows), F32)]
        shapes += [shape((size, rows), BF16)] * (2 ** len(step) - 1)
        keep, *sends = call(
            functools.partial(fold_kernel, len(arrived)), f"fold{step[0]}", shapes
        )(keep, *ordered(arrived, (2, 0, 1)))
        arrived = swaps(sends, step)
    factor_cot = call(factor_kernel, "factors", shape((rows, factor_rows), F32))(
        keep, *arrived, basis
    )
    factor_cot = jnp.transpose(factor_cot.reshape(dates, paths, factor_rows), (2, 0, 1))
    netting_cva = sum_over(cva[0], "path") / (paths * lax.axis_size("path"))
    return netting_cva, factor_cot


def solution(mesh):
    return jax.shard_map(
        shards,
        mesh=mesh,
        in_specs=(
            P("trade", None, "path"), P(), P(None, "trade"), P("trade"), P("trade"),
            P("trade"), P("trade"), P("trade"), P(None, "trade"), P("trade"),
            P("trade", None),
        ),
        out_specs=(P("trade"), P("trade", None, "path")),
        check_vma=False,
    )
```
